32 devices in a mesh: tm: 8 (over z, y), mp: 4 (over x, core).
Axes of the slice: x: 2, y: 2, z: 4, core: 2. Of those that a mesh axis runs over, the one named last changes fastest.
Arguments:
- queries: bfloat16 [1536, 1024], P('tm', 'mp'), may hold values from -8 to 8
- d_queries: bfloat16 [1536, 1024], P('tm', 'mp'), may hold values from -6 to 6
- key_rows: bfloat16 [1536, 1024], P('tm', 'mp'), may hold values from -8 to 8
- value_rows: bfloat16 [1536, 1024], P('tm', 'mp'), may hold values from -6 to 6
- d_key_rows: bfloat16 [1536, 1024], P('tm', 'mp'), may hold values from -6 to 6
- d_value_rows: bfloat16 [1536, 1024], P('tm', 'mp'), may hold values from -6 to 6
- live_flags: int32 [1536], P('tm'), may hold values from 0 to 1, as said below
- out_weight: bfloat16 [1024, 5120], P('mp'), may hold values from -1 to 1
- gate_scale: float32 [5120], P('mp'), may hold values from 0.25 to 1.75
- tokens: bfloat16 [1536, 5120], P('tm', 'mp'), may hold values from -6 to 6
- d_tokens: bfloat16 [1536, 5120], P('tm', 'mp'), may hold values from -6 to 6
Outputs:
- result: bfloat16 [1536, 5120], P('tm', 'mp')
- d_result: bfloat16 [1536, 5120], P('tm', 'mp')
The draws below stay inside these ranges and needn't reach their ends.
Inputs may be any that keep to these rules, and one draw needn't show every extreme that they name: live_flags are equal within each aligned run of 32 tokens.
All inputs are finite; a program needn't handle non-finite values.
Results may differ from the reference program's by a relative error of at most 0.019.
Values may be sent and summed in bfloat16 or wider, within the bound.
A program may use at most 128 MiB of HBM per device.

```python
import math
import jax
import jax.numpy as jnp
from jax import lax

D = 5120
HD = 128
H_DEV = 2
FRAME = 32
HEADS = 8
TOKENS = 1536
N_MP = 4


def drawn_field(key):
    values = 1.2 * jax.random.normal(key, (TOKENS, HEADS * HD), jnp.float32)
    return values


def draw_queries(key, part):
    values = drawn_field(jax.random.fold_in(key, 11))
    return jnp.clip(values, -8.0, 8.0).astype(jnp.bfloat16)


def draw_key_rows(key, part):
    values = drawn_field(jax.random.fold_in(key, 13))
    return jnp.clip(values, -8.0, 8.0).astype(jnp.bfloat16)


def draw_live_flags(key, part):
    frames = jax.random.randint(jax.random.fold_in(key, 17), (TOKENS // FRAME,), 0, 4)
    flags = (frames > 0).astype(jnp.int32)
    return jnp.repeat(flags, FRAME)


def levels(rng, dims, cuts, least, top_value):
    def one(axis_at, shards_of):
        draws = jax.random.uniform(jax.random.fold_in(jax.random.fold_in(rng, 6), axis_at), (shards_of,), jnp.float32, least / len(cuts), top_value / len(cuts))
        return jnp.repeat(jnp.exp(draws), dims[axis_at] // shards_of).reshape((-1,) + (1,) * (len(dims) - axis_at - 1))

    loudness = one(*cuts[0])
    for cut in cuts[1:]:
        loudness = loudness * one(*cut)
    return loudness


def noise(own_key, extent, spread, most, cuts=(), dtype=jnp.bfloat16):
    drawn = jax.random.normal(own_key, extent, jnp.float32) * spread
    if len(cuts) > 0:
        drawn = levels(own_key, extent, cuts, -0.22, 0.18) * drawn
    return jnp.clip(drawn, min=-most, max=most).astype(dtype)


def setup_inputs(seed: int = 0) -> dict:
    seeds = jax.random.split(jax.random.key(seed), 12)
    return {
        "queries": draw_queries(jax.random.fold_in(seeds[11], 71), 0),
        "d_queries": noise(seeds[1], (TOKENS, HEADS * HD), 1.0, 6.0, ((0, 8), (1, 4))),
        "key_rows": draw_key_rows(jax.random.fold_in(seeds[11], 71), 0),
        "value_rows": noise(seeds[3], (TOKENS, HEADS * HD), 1.0, 6.0, ((0, 8), (1, 4))),
        "d_key_rows": noise(seeds[4], (TOKENS, HEADS * HD), 1.0, 6.0, ((0, 8), (1, 4))),
        "d_value_rows": noise(seeds[5], (TOKENS, HEADS * HD), 1.0, 6.0, ((0, 8), (1, 4))),
        "live_flags": draw_live_flags(jax.random.fold_in(seeds[11], 71), 0),
        "out_weight": noise(seeds[7], (HEADS * HD, D), (H_DEV * HD // 8) ** -0.5, 1.0, ((0, 4),)),
        "gate_scale": jnp.clip(1.0 + 0.15 * jax.random.normal(seeds[8], (D,), jnp.float32), 0.25, 1.75),
        "tokens": noise(seeds[9], (TOKENS, D), 1.0, 6.0, ((0, 8), (1, 4))),
        "d_tokens": noise(seeds[10], (TOKENS, D), 1.0, 6.0, ((0, 8), (1, 4))),
    }


def one_head(pieces):
    query_h, tangent_q, key_h, value_h, tangent_k, tangent_v = pieces
    factor = 1.0 / math.sqrt(HD)
    scores = jnp.dot(query_h, key_h.T, preferred_element_type=jnp.float32) * factor
    d_scores = (jnp.dot(tangent_q, key_h.T, preferred_element_type=jnp.float32) + jnp.dot(query_h, tangent_k.T, preferred_element_type=jnp.float32)) * factor
    peak = lax.optimization_barrier(jnp.max(scores, axis=1, keepdims=True))
    weights = jnp.exp(scores - peak)
    totals = lax.optimization_barrier(jnp.sum(weights, axis=1, keepdims=True))
    product = weights * d_scores
    slopes = lax.optimization_barrier(jnp.sum(product, axis=1, keepdims=True))
    weights_b = weights.astype(jnp.bfloat16)
    product_b = product.astype(jnp.bfloat16)
    primal = jnp.dot(weights_b, value_h, preferred_element_type=jnp.float32)
    tangent = jnp.dot(product_b, value_h, preferred_element_type=jnp.float32) + jnp.dot(weights_b, tangent_v, preferred_element_type=jnp.float32)
    outputs = primal / totals
    d_outputs = tangent / totals - slopes / totals * outputs
    return (outputs.astype(jnp.bfloat16), d_outputs.astype(jnp.bfloat16))

def reference(queries, d_queries, key_rows, value_rows, d_key_rows, d_value_rows, live_flags, out_weight, gate_scale, tokens, d_tokens):
    live_rows = live_flags[:, None] > 0

    def masked(matrix):
        return jnp.where(live_rows, matrix, jnp.zeros_like(matrix))

    def by_heads(matrix):
        return matrix.reshape(TOKENS, HEADS, HD).transpose(1, 0, 2)
    stacked = tuple((by_heads(matrix) for matrix in (queries, masked(d_queries), key_rows, value_rows, masked(d_key_rows), masked(d_value_rows))))
    outputs, d_outputs = lax.map(one_head, stacked)

    def regroup(heads_out):
        return heads_out.transpose(1, 0, 2).reshape(TOKENS, N_MP, H_DEV * HD).transpose(1, 0, 2)
    weight_groups = out_weight.reshape(N_MP, H_DEV * HD, D)

    def add_group(running, pieces):
        group_o, group_do, group_w = pieces
        part_y = jnp.dot(group_o, group_w, preferred_element_type=jnp.float32)
        part_dy = jnp.dot(group_do, group_w, preferred_element_type=jnp.float32)
        rounded = lax.optimization_barrier((part_y.astype(jnp.bfloat16), part_dy.astype(jnp.bfloat16)))
        return ((running[0] + rounded[0].astype(jnp.float32), running[1] + rounded[1].astype(jnp.float32)), None)
    blank_sum = jnp.zeros((TOKENS, D), jnp.float32)
    sums, unused = lax.scan(add_group, (blank_sum, blank_sum), (regroup(outputs), regroup(d_outputs), weight_groups))
    result = (tokens.astype(jnp.float32) + gate_scale * sums[0]).astype(jnp.bfloat16)
    d_result = (masked(d_tokens).astype(jnp.float32) + gate_scale * sums[1]).astype(jnp.bfloat16)
    return (result, d_result)
```

```python
import functools
import math

import jax
import jax.numpy as jnp
from jax import lax
from jax.experimental import pallas as pl
from jax.experimental.pallas import tpu as pltpu
from jax.sharding import PartitionSpec as P

HD = 128
FRAME = 32
MESH = pl.DeviceIdType.MESH
F32 = jnp.float32
BF16 = jnp.bfloat16


def ring_place(t, n):
    return jnp.where(t % 2 == 0, t // 2, n - 1 - t // 2)


def ring_member(r, n):
    return jnp.where(r < n // 2, 2 * r, 2 * (n - 1 - r) + 1)


def flipped(me, j):
    other = me
    bit = 1
    while bit <= j:
        if j & bit:
            other = other + bit * (1 - 2 * ((me // bit) % 2))
        bit *= 2
    return other


def dot_nt(a, b):
    return lax.dot_general(a, b, (((1,), (1,)), ((), ())), preferred_element_type=F32)


def dot_nn(a, b):
    return lax.dot_general(a, b, (((1,), (0,)), ((), ())), preferred_element_type=F32)


def fused(
    n,
    n_mp,
    move_w,
    q_hbm,
    dq_hbm,
    k_hbm,
    v_hbm,
    dk_hbm,
    dv_hbm,
    flags_hbm,
    w_hbm,
    gate_hbm,
    x_hbm,
    dx_hbm,
    out,
    d_out,
    own,
    qcat,
    tkv,
    kv,
    opp,
    m_s,
    l_s,
    c_s,
    a_s,
    g_s,
    ao,
    wbuf,
    acc,
    xbuf,
    flags,
    gate,
    own_sem,
    x_sem,
    small_sem,
    w_local,
    ks,
    kr,
    ws,
    wr,
    as_,
    ar,
):
    rows, width = q_hbm.shape
    heads = width // HD
    cols = out.shape[1]
    half = n // 2
    t = lax.axis_index("tm")
    m = lax.axis_index("mp")
    place = ring_place(t, n)
    right = ring_member((place + 1) % n, n)
    left = ring_member((place + n - 1) % n, n)
    peers = [flipped(m, j) for j in range(n_mp)]
    factor = 1.0 / math.sqrt(HD)

    def lanes(h):
        return slice(h * HD, (h + 1) * HD)

    loads = [
        pltpu.make_async_copy(src, own.at[i], own_sem.at[i])
        for i, src in enumerate((k_hbm, v_hbm, dk_hbm, dv_hbm, q_hbm, dq_hbm))
    ]
    loads.append(pltpu.make_async_copy(flags_hbm, flags, small_sem.at[0]))
    for load in loads:
        load.start()

    barrier = pltpu.get_barrier_semaphore()
    for dev in [(right, m), (left, m)] + [(t, peers[j]) for j in range(1, n_mp)]:
        pl.semaphore_signal(barrier, inc=1, device_id=dev, device_id_type=MESH)
    pl.semaphore_wait(barrier, 1 + n_mp)

    def exists(d, s, p):
        return s < half or (s == half and (p < 2) == (d == 0))

    def kv_copy(h, d, s, p):
        side = slice(d * rows, (d + 1) * rows)
        if s > 1:
            src = kv.at[h, s - 2, p, side]
        elif p < 2:
            src = (k_hbm, v_hbm)[p].at[:, lanes(h)]
        else:
            src = tkv.at[h, p - 2]
        dst = kv.at[h, s - 1, p, side] if s < half else opp.at[h, p]
        return pltpu.make_async_remote_copy(
            src_ref=src,
            dst_ref=dst,
            send_sem=ks.at[h, d, s - 1, p],
            recv_sem=kr.at[h, d, s - 1, p],
            device_id=((right, left)[d], m),
            device_id_type=MESH,
        )

    def send_own(h, pieces):
        for p in pieces:
            for d in (0, 1):
                kv_copy(h, d, 1, p).start()

    def w_copy(h, j):
        span = pl.ds(pl.multiple_of(peers[j] * cols, HD), cols)
        part = slice(h * HD, (h + 1) * HD)
        if j == 0:
            return pltpu.make_async_copy(
                w_hbm.at[part, span], wbuf.at[0, part], w_local.at[h]
            )
        return pltpu.make_async_remote_copy(
            src_ref=w_hbm.at[part, span],
            dst_ref=wbuf.at[j, part],
            send_sem=ws.at[h, j],
            recv_sem=wr.at[h, j],
            device_id=(t, peers[j]),
            device_id_type=MESH,
        )

    def ao_copy(h, j):
        relay = j % 2 == 1 and j > 1
        return pltpu.make_async_remote_copy(
            src_ref=ao.at[h, j - 1 if relay else 0],
            dst_ref=ao.at[h, j],
            send_sem=as_.at[h, j],
            recv_sem=ar.at[h, j],
            device_id=(t, peers[1] if relay else peers[j]),
            device_id_type=MESH,
        )

    send_own(0, (0, 1))
    if move_w:
        for h in range(heads):
            for j in list(range(2, n_mp)) + [1, 0]:
                w_copy(h, j).start()
    x_loads = [
        pltpu.make_async_copy(src, xbuf.at[i], x_sem.at[i])
        for i, src in enumerate((x_hbm, dx_hbm))
    ]
    x_loads.append(pltpu.make_async_copy(gate_hbm, gate, small_sem.at[1]))
    for load in x_loads:
        load.start()
    for load in loads:
        load.wait()

    live = [
        jnp.where(flags[i * FRAME] > 0, 1.0, 0.0).astype(F32)
        for i in range(rows // FRAME)
    ]

    def masked(value, i):
        scale = jnp.full(value.shape, live[i], F32)
        return (value.astype(F32) * scale).astype(BF16)

    for h in range(heads):
        for i in range(rows // FRAME):
            part = slice(i * FRAME, (i + 1) * FRAME)
            tkv[h, 0, part] = masked(own[2, part, lanes(h)], i)
            tkv[h, 1, part] = masked(own[3, part, lanes(h)], i)
        if h == 0:
            send_own(0, (2, 3))
            for g in range(1, heads):
                send_own(g, (0, 1))
        else:
            send_own(h, (2, 3))
    for h in range(heads):
        for i in range(rows // FRAME):
            part = slice(i * FRAME, (i + 1) * FRAME)
            qcat[h, part, 0:HD] = masked(own[5, part, lanes(h)], i)
        qcat[h, :, HD : 2 * HD] = own[4, :, lanes(h)]

    def attend(h, k, tk, values, first):
        queries = qcat[h, :, HD : 2 * HD]
        scores = dot_nt(queries, k)
        d_scores = dot_nt(qcat[h], jnp.concatenate([k, tk], axis=1)) * factor
        peak = jnp.max(scores, axis=1, keepdims=True)
        if not first:
            peak_old = m_s[h]
            peak = jnp.maximum(peak_old, peak)
            rescale = jnp.exp((peak_old - peak) * factor)
        weights = jnp.exp((scores - peak) * factor)
        product = weights * d_scores
        total = jnp.sum(weights, axis=1, keepdims=True)
        slope = jnp.sum(product, axis=1, keepdims=True)
        weights_b = weights.astype(BF16)
        product_b = product.astype(BF16)
        v, tv = values()
        primal = dot_nn(weights_b, v)
        tangent = dot_nn(product_b, v) + dot_nn(weights_b, tv)
        m_s[h] = peak
        if first:
            l_s[h] = total
            c_s[h] = slope
            a_s[h] = primal
            g_s[h] = tangent
        else:
            l_s[h] = l_s[h] * rescale + total
            c_s[h] = c_s[h] * rescale + slope
            a_s[h] = a_s[h] * rescale + primal
            g_s[h] = g_s[h] * rescale + tangent

    def finish(h):
        inverse = 1.0 / l_s[h]
        outputs = a_s[h] * inverse
        d_outputs = g_s[h] * inverse - (c_s[h] * inverse) * outputs
        ao[h, 0, 0:rows] = outputs.astype(BF16)
        ao[h, 0, rows : 2 * rows] = d_outputs.astype(BF16)
        for j in list(range(2, n_mp, 2)) + [1]:
            ao_copy(h, j).start()

    def relay(h):
        for j in range(2, n_mp, 2):
            ao_copy(h, j).wait_recv()
            ao_copy(h, j + 1).start()

    for h in range(heads):
        attend(
            h, own[0, :, lanes(h)], tkv[h, 0], lambda: (own[1, :, lanes(h)], tkv[h, 1]), True
        )
    for s in range(1, half):
        for h in range(heads):
            for p in range(4):
                for d in (0, 1):
                    kv_copy(h, d, s, p).wait_recv()
                    if exists(d, s + 1, p):
                        kv_copy(h, d, s + 1, p).start()
            attend(
                h,
                kv[h, s - 1, 0],
                kv[h, s - 1, 2],
                lambda: (kv[h, s - 1, 1], kv[h, s - 1, 3]),
                False,
            )
    for h in range(heads):
        def opposite(first_p, second_p):
            kv_copy(h, 0, half, first_p).wait_recv()
            kv_copy(h, 1, half, second_p).wait_recv()
            return opp[h, first_p], opp[h, second_p]

        keys, d_keys = opposite(0, 2)
        attend(h, keys, d_keys, lambda: opposite(1, 3), False)
        finish(h)

    step = 2 * HD if cols % (2 * HD) == 0 else cols
    chunks = [slice(c, c + step) for c in range(0, cols, step)]

    def w_part(h, j, chunk):
        part = slice(h * HD, (h + 1) * HD)
        if move_w:
            return wbuf[j, part, chunk]
        return w_hbm[peers[j], part, chunk]

    def project(slots, chunk):
        attn = jnp.concatenate([ao[h, j] for h, j in slots], axis=1)
        weight = jnp.concatenate([w_part(h, j, chunk) for h, j in slots], axis=0)
        return dot_nn(attn, weight)

    if move_w:
        for h in range(heads):
            w_copy(h, 0).wait()
            for j in range(1, n_mp):
                w_copy(h, j).wait_recv()
    for load in x_loads:
        load.wait()
    last = heads - 1
    for h in range(heads):
        ao_copy(h, 1).wait_recv()
    near = [(h, j) for h in range(heads) for j in (0, 1)]
    for chunk in chunks:
        acc[:, chunk] = project(near, chunk)
    for h in range(last):
        relay(h)
    for h in range(last):
        for j in range(3, n_mp, 2):
            ao_copy(h, j).wait_recv()
    far = [(h, j) for h in range(last) for j in range(2, n_mp)]
    for chunk in chunks:
        acc[:, chunk] += project(far, chunk)
    for h in range(heads):
        for s in range(1, half + 1):
            for p in range(4):
                for d in (0, 1):
                    if exists(d, s, p):
                        kv_copy(h, d, s, p).wait_send()
        if move_w:
            for j in range(1, n_mp):
                w_copy(h, j).wait_send()
    relay(last)
    even = [(last, j) for j in range(2, n_mp, 2)]
    for chunk in chunks:
        acc[:, chunk] += project(even, chunk)
    for j in range(3, n_mp, 2):
        ao_copy(last, j).wait_recv()
    odd = [(last, j) for j in range(3, n_mp, 2)]
    for chunk in chunks:
        part = acc[:, chunk] + project(odd, chunk)
        scale = gate[chunk].reshape(1, step)
        out[:, chunk] = (xbuf[0, :, chunk].astype(F32) + scale * part[0:rows]).astype(BF16)
        for i in range(rows // FRAME):
            piece = slice(i * FRAME, (i + 1) * FRAME)
            base = xbuf[1, piece, chunk].astype(F32)
            base = base * jnp.full(base.shape, live[i], F32)
            delta = part[rows + i * FRAME : rows + (i + 1) * FRAME]
            d_out[piece, chunk] = (base + scale * delta).astype(BF16)

    for h in range(heads):
        for j in range(1, n_mp):
            ao_copy(h, j).wait_send()


def per_device(n, n_mp, q, dq, k, v, dk, dv, flags, w, gate, x, dx):
    rows, width = q.shape
    cols = x.shape[1]
    heads = width // HD
    half = n // 2
    move_w = cols % HD == 0
    if not move_w:
        w = lax.all_to_all(w, "mp", split_axis=1, concat_axis=0, tiled=True)
        w = w.reshape(n_mp, width, cols)
    anywhere = pl.BlockSpec(memory_space=pl.ANY)
    vmem = pl.BlockSpec(memory_space=pltpu.VMEM)
    dma = pltpu.SemaphoreType.DMA
    return pl.pallas_call(
        functools.partial(fused, n, n_mp, move_w),
        out_shape=(pltpu.VMEM(x.shape, BF16), pltpu.VMEM(x.shape, BF16)),
        in_specs=[anywhere] * 6
        + [anywhere, anywhere if move_w else vmem, anywhere]
        + [anywhere] * 2,
        out_specs=(vmem, vmem),
        scratch_shapes=[
            pltpu.VMEM((6, rows, width), BF16),
            pltpu.VMEM((heads, rows, 2 * HD), BF16),
            pltpu.VMEM((heads, 2, rows, HD), BF16),
            pltpu.VMEM((heads, half - 1, 4, 2 * rows, HD), BF16),
            pltpu.VMEM((heads, 4, rows, HD), BF16),
            pltpu.VMEM((heads, rows, 1), F32),
            pltpu.VMEM((heads, rows, 1), F32),
            pltpu.VMEM((heads, rows, 1), F32),
            pltpu.VMEM((heads, rows, HD), F32),
            pltpu.VMEM((heads, rows, HD), F32),
            pltpu.VMEM((heads, n_mp, 2 * rows, HD), BF16),
            pltpu.VMEM((n_mp, width, cols) if move_w else (1, 16, HD), BF16),
            pltpu.VMEM((2 * rows, cols), F32),
            pltpu.VMEM((2, rows, cols), BF16),
            pltpu.SMEM((rows,), jnp.int32),
            pltpu.VMEM((cols,), F32),
            dma((6,)),
            dma((2,)),
            dma((2,)),
            dma((heads,)),
            dma((heads, 2, half, 4)),
            dma((heads, 2, half, 4)),
            dma((heads, n_mp)),
            dma((heads, n_mp)),
            dma((heads, n_mp)),
            dma((heads, n_mp)),
        ],
        compiler_params=pltpu.CompilerParams(
            collective_id=0, has_side_effects=True, vmem_limit_bytes=65000000
        ),
    )(q, dq, k, v, dk, dv, flags, w, gate, x, dx)


def spread(
    n,
    n_mp,
    q_hbm,
    dq_hbm,
    k_hbm,
    v_hbm,
    dk_hbm,
    dv_hbm,
    flags_hbm,
    w_hbm,
    gate_hbm,
    x_hbm,
    dx_hbm,
    out,
    d_out,
    own,
    tang,
    qcat,
    kv,
    m_s,
    l_s,
    c_s,
    a_s,
    g_s,
    res,
    ao,
    wbuf,
    acc,
    xbuf,
    flags,
    gate,
    own_sem,
    x_sem,
    small_sem,
    w_local,
    zs,
    qr,
    kr,
    fs,
    ys,
    wts,
    wtr,
    wxs,
    wxr,
    wys,
    wyr,
    wzs,
    wzr,
    rs,
    rr,
    as_,
    ar,
):
    rows, width = q_hbm.shape
    heads = width // HD
    cols = out.shape[1]
    t = lax.axis_index("tm")
    m = lax.axis_index("mp")
    z, y = t // 2, t % 2
    plane, core = m // 2, m % 2
    side = z // 2
    role = jnp.where(side == 0, 1 - z % 2, z % 2)
    far = (side + core) % 2

    def device(side_, role_, core_):
        z_ = 2 * side_ + jnp.where(side_ == 0, 1 - role_, role_)
        return (2 * z_ + y, 2 * plane + core_)

    partners = [device(core, j, side) for j in range(heads)]
    mine = [jnp.logical_and(far == 0, role == j) for j in range(heads)]
    twin = (t, 2 * plane + 1 - core)
    across = (t, 2 * (1 - plane) + core)
    diagonal = (t, 2 * (1 - plane) + 1 - core)
    row_peer = (2 * z + 1 - y, m)
    z_peer = device(side, 1 - role, core)
    factor = 1.0 / math.sqrt(HD)

    def lanes(h):
        return slice(h * HD, (h + 1) * HD)

    def both(flag, yes, no):
        pl.when(flag)(yes)
        pl.when(jnp.logical_not(flag))(no)

    loads = [
        pltpu.make_async_copy(src, own.at[i], own_sem.at[i])
        for i, src in enumerate((dq_hbm, dk_hbm, dv_hbm))
    ]
    loads.append(pltpu.make_async_copy(flags_hbm, flags, small_sem.at[0]))
    for load in loads:
        load.start()

    barrier = pltpu.get_barrier_semaphore()
    for dev in (twin, across, diagonal, row_peer, z_peer):
        pl.semaphore_signal(barrier, inc=1, device_id=dev, device_id_type=MESH)

    @pl.when(far == 1)
    def _():
        for dev in partners:
            pl.semaphore_signal(barrier, inc=1, device_id=dev, device_id_type=MESH)

    pl.semaphore_wait(barrier, 5 + heads * far)

    def z_ends(j, p):
        src = (
            q_hbm.at[:, lanes(j)],
            tang.at[0, j],
            k_hbm.at[:, lanes(j)],
            tang.at[1, j],
            v_hbm.at[:, lanes(j)],
            tang.at[2, j],
        )[p]
        if p == 0:
            return src, qcat.at[role, :, HD : 2 * HD], qr.at[role, 0]
        if p == 1:
            return src, qcat.at[role, :, 0:HD], qr.at[role, 1]
        return src, kv.at[0, far, p - 2, role], kr.at[0, far, p - 2, role]

    def z_remote(j, p):
        src, dst, sem = z_ends(j, p)
        return pltpu.make_async_remote_copy(
            src_ref=src,
            dst_ref=dst,
            send_sem=zs.at[j, p],
            recv_sem=sem,
            device_id=partners[j],
            device_id_type=MESH,
        )

    def z_start(j, pieces):
        def local():
            for p in pieces:
                src, dst, sem = z_ends(j, p)
                pltpu.make_async_copy(src, dst, sem).start()

        def remote():
            for p in pieces:
                z_remote(j, p).start()

        both(mine[j], local, remote)

    def z_sent():
        for j in range(heads):

            @pl.when(jnp.logical_not(mine[j]))
            def _():
                for p in range(6):
                    z_remote(j, p).wait_send()

    tile = 16
    tiles = width // tile
    y_rows = (tiles * 5 // 16) * tile
    z_rows = (tiles // 2) * tile - y_rows
    halves = 2 if cols % (2 * HD) == 0 else 1
    span = cols // halves

    def y_part(index):
        return pl.ds(pl.multiple_of(index * y_rows, tile), y_rows)

    def z_part(index):
        return pl.ds(pl.multiple_of(2 * y_rows + index * z_rows, tile), z_rows)

    def w_cols(owner, first, size):
        return pl.ds(pl.multiple_of(owner * cols + first, HD), size)

    def w_cross(slot, piece):
        dev = across if slot == 0 else diagonal
        if piece < halves:
            part = y_part(y)
            first, size = piece * span, span
        else:
            part = z_part(role)
            first, size = 0, cols
        return pltpu.make_async_remote_copy(
            src_ref=w_hbm.at[part, w_cols(dev[1], first, size)],
            dst_ref=wbuf.at[2 + slot, part, pl.ds(first, size)],
            send_sem=wxs.at[slot, piece],
            recv_sem=wxr.at[slot, piece],
            device_id=dev,
            device_id_type=MESH,
        )

    def w_row(slot, piece):
        ref = wbuf.at[2 + slot, y_part(y), pl.ds(piece * span, span)]
        return pltpu.make_async_remote_copy(
            src_ref=ref,
            dst_ref=ref,
            send_sem=wys.at[slot, piece],
            recv_sem=wyr.at[slot, piece],
            device_id=row_peer,
            device_id_type=MESH,
        )

    def w_z(slot):
        ref = wbuf.at[2 + slot, z_part(role)]
        return pltpu.make_async_remote_copy(
            src_ref=ref,
            dst_ref=ref,
            send_sem=wzs.at[slot],
            recv_sem=wzr.at[slot],
            device_id=z_peer,
            device_id_type=MESH,
        )

    def w_row_relay(piece):
        for slot in range(2):
            w_cross(slot, piece).wait_recv()
            w_row(slot, piece).start()

    def w_z_relay():
        for slot in range(2):
            w_cross(slot, halves).wait_recv()
            w_z(slot).start()

    w_twin = pltpu.make_async_remote_copy(
        src_ref=w_hbm.at[:, w_cols(twin[1], 0, cols)],
        dst_ref=wbuf.at[1],
        send_sem=wts,
        recv_sem=wtr,
        device_id=twin,
        device_id_type=MESH,
    )
    w_own = pltpu.make_async_copy(w_hbm.at[:, w_cols(m, 0, cols)], wbuf.at[0], w_local)

    z_start(0, (0, 2))
    for piece in range(halves + 1):
        for slot in range(2):
            w_cross(slot, piece).start()
    z_start(0, (4,))
    for load in loads:
        load.wait()

    live = [
        jnp.where(flags[i * FRAME] > 0, 1.0, 0.0).astype(F32)
        for i in range(rows // FRAME)
    ]

    def masked(value, i):
        scale = jnp.full(value.shape, live[i], F32)
        return (value.astype(F32) * scale).astype(BF16)

    for h in range(heads):
        for a in range(3):
            for i in range(rows // FRAME):
                part = slice(i * FRAME, (i + 1) * FRAME)
                tang[a, h, part] = masked(own[a, part, lanes(h)], i)
        if h == 0:
            z_start(0, (1, 3, 5))
            z_start(1, (0, 2))
        else:
            z_start(1, (1, 3, 4, 5))
    w_twin.start()
    w_own.start()
    x_loads = [
        pltpu.make_async_copy(src, xbuf.at[i], x_sem.at[i])
        for i, src in enumerate((x_hbm, dx_hbm))
    ]
    x_loads.append(pltpu.make_async_copy(gate_hbm, gate, small_sem.at[1]))
    for load in x_loads:
        load.start()

    def kv_wait(yr, rel, p, i):
        ref = kv.at[yr, rel, p, i]
        pltpu.make_async_copy(ref, ref, kr.at[yr, rel, p, i]).wait()

    def to_twin(yr, p, i):
        ref = kv.at[yr, far, p, i]
        return pltpu.make_async_remote_copy(
            src_ref=ref,
            dst_ref=ref,
            send_sem=fs.at[yr, p, i],
            recv_sem=kr.at[yr, far, p, i],
            device_id=twin,
            device_id_type=MESH,
        )

    def to_row(p, i):
        return pltpu.make_async_remote_copy(
            src_ref=kv.at[0, far, p, i],
            dst_ref=kv.at[1, far, p, i],
            send_sem=ys.at[p, i],
            recv_sem=kr.at[1, far, p, i],
            device_id=row_peer,
            device_id_type=MESH,
        )

    def arrivals(yr, rel):
        def passing():
            for p in range(4):
                for i in range(heads):
                    kv_wait(yr, rel, p, i)
                    if yr == 0:
                        to_row(p, i).start()
                    to_twin(yr, p, i).start()

        def staying():
            for p in range(4):
                for i in range(heads):
                    kv_wait(yr, rel, p, i)

        both(far == rel, passing, staying)

    def attend(yr, rel, i):
        first = yr == 0 and rel == 0
        k = kv[yr, rel, 0].reshape(heads * rows, HD)
        tk = kv[yr, rel, 1].reshape(heads * rows, HD)
        v = kv[yr, rel, 2].reshape(heads * rows, HD)
        tv = kv[yr, rel, 3].reshape(heads * rows, HD)
        scores = dot_nt(qcat[i, :, HD : 2 * HD], k)
        d_scores = dot_nt(qcat[i], jnp.concatenate([k, tk], axis=1)) * factor
        peak = jnp.max(scores, axis=1, keepdims=True)
        if not first:
            peak_old = m_s[i]
            peak = jnp.maximum(peak_old, peak)
            rescale = jnp.exp((peak_old - peak) * factor)
        weights = jnp.exp((scores - peak) * factor)
        product = weights * d_scores
        total = jnp.sum(weights, axis=1, keepdims=True)
        slope = jnp.sum(product, axis=1, keepdims=True)
        weights_b = weights.astype(BF16)
        product_b = product.astype(BF16)
        wide = dot_nn(weights_b, jnp.concatenate([v, tv], axis=1))
        primal = wide[:, 0:HD]
        tangent = dot_nn(product_b, v) + wide[:, HD : 2 * HD]
        if not first:
            total = l_s[i] * rescale + total
            slope = c_s[i] * rescale + slope
            primal = a_s[i] * rescale + primal
            tangent = g_s[i] * rescale + tangent
        if yr == 1 and rel == 1:
            inverse = 1.0 / total
            outputs = primal * inverse
            d_outputs = tangent * inverse - (slope * inverse) * outputs
            res[i, 0:rows] = outputs.astype(BF16)
            res[i, rows : 2 * rows] = d_outputs.astype(BF16)
        else:
            m_s[i] = peak
            l_s[i] = total
            c_s[i] = slope
            a_s[i] = primal
            g_s[i] = tangent

    def res_ends(i):
        return res.at[i], ao.at[role, 0], rr.at[role]

    def res_remote(i):
        src, dst, sem = res_ends(i)
        return pltpu.make_async_remote_copy(
            src_ref=src,
            dst_ref=dst,
            send_sem=rs.at[i],
            recv_sem=sem,
            device_id=partners[i],
            device_id_type=MESH,
        )

    def res_start(i):
        both(
            mine[i],
            lambda: pltpu.make_async_copy(*res_ends(i)).start(),
            lambda: res_remote(i).start(),
        )

    for i in range(heads):
        for a in range(2):
            ref = qcat.at[i, :, (1 - a) * HD : (2 - a) * HD]
            pltpu.make_async_copy(ref, ref, qr.at[i, a]).wait()
    arrivals(0, 0)
    for i in range(heads):
        attend(0, 0, i)
    w_row_relay(0)
    arrivals(1, 0)
    for i in range(heads):
        attend(1, 0, i)

    def w_rest():
        for piece in range(1, halves):
            w_row_relay(piece)
        w_z_relay()

    pl.when(role == 1)(w_rest)
    arrivals(0, 1)
    for i in range(heads):
        attend(0, 1, i)
    arrivals(1, 1)
    z_sent()
    for i in range(heads):
        attend(1, 1, i)
        res_start(i)
    pl.when(role == 0)(w_rest)

    def ao_copy(h, j):
        relay = j == 3
        return pltpu.make_async_remote_copy(
            src_ref=ao.at[h, 2 if relay else 0],
            dst_ref=ao.at[h, j],
            send_sem=as_.at[h, j],
            recv_sem=ar.at[h, j],
            device_id=across if j == 2 else twin,
            device_id_type=MESH,
        )

    def own_heads(h):
        pltpu.make_async_copy(ao.at[h, 0], ao.at[h, 0], rr.at[h]).wait()
        ao_copy(h, 2).start()
        ao_copy(h, 1).start()

    def cross_heads(h):
        ao_copy(h, 2).wait_recv()
        ao_copy(h, 3).start()

    step = 2 * HD if cols % (2 * HD) == 0 else cols
    chunks = [slice(c, c + step) for c in range(0, cols, step)]

    def project(slots, chunk):
        attn = jnp.concatenate([ao[h, j] for h, j in slots], axis=1)
        weight = jnp.concatenate(
            [wbuf[j, h * HD : (h + 1) * HD, chunk] for h, j in slots], axis=0
        )
        return dot_nn(attn, weight)

    own_heads(0)
    cross_heads(0)
    w_own.wait()
    w_twin.wait_recv()
    for slot in range(2):
        for piece in range(halves):
            w_row(slot, piece).wait_recv()
        w_z(slot).wait_recv()
    ao_copy(0, 1).wait_recv()
    for load in x_loads:
        load.wait()
    ao_copy(0, 3).wait_recv()
    for chunk in chunks:
        acc[:, chunk] = project([(0, j) for j in range(n_mp)], chunk)
    own_heads(1)
    ao_copy(1, 1).wait_recv()
    for chunk in chunks:
        acc[:, chunk] += project([(1, 0), (1, 1)], chunk)
    cross_heads(1)
    ao_copy(1, 3).wait_recv()
    for chunk in chunks:
        part = acc[:, chunk] + project([(1, 2), (1, 3)], chunk)
        scale = gate[chunk].reshape(1, step)
        out[:, chunk] = (xbuf[0, :, chunk].astype(F32) + scale * part[0:rows]).astype(BF16)
        for i in range(rows // FRAME):
            piece = slice(i * FRAME, (i + 1) * FRAME)
            base = xbuf[1, piece, chunk].astype(F32)
            base = base * jnp.full(base.shape, live[i], F32)
            delta = part[rows + i * FRAME : rows + (i + 1) * FRAME]
            d_out[piece, chunk] = (base + scale * delta).astype(BF16)

    for slot in range(2):
        for piece in range(halves + 1):
            w_cross(slot, piece).wait_send()
        for piece in range(halves):
            w_row(slot, piece).wait_send()
        w_z(slot).wait_send()
    w_twin.wait_send()
    for p in range(4):
        for i in range(heads):
            to_row(p, i).wait_send()
            for yr in range(2):
                to_twin(yr, p, i).wait_send()
    for i in range(heads):

        @pl.when(jnp.logical_not(mine[i]))
        def _():
            res_remote(i).wait_send()

        for j in range(1, n_mp):
            ao_copy(i, j).wait_send()


def spread_call(n, n_mp, q, dq, k, v, dk, dv, flags, w, gate, x, dx):
    rows, width = q.shape
    cols = x.shape[1]
    heads = width // HD
    halves = 2 if cols % (2 * HD) == 0 else 1
    anywhere = pl.BlockSpec(memory_space=pl.ANY)
    vmem = pl.BlockSpec(memory_space=pltpu.VMEM)
    dma = pltpu.SemaphoreType.DMA
    return pl.pallas_call(
        functools.partial(spread, n, n_mp),
        out_shape=(pltpu.VMEM(x.shape, BF16), pltpu.VMEM(x.shape, BF16)),
        in_specs=[anywhere] * 11,
        out_specs=(vmem, vmem),
        scratch_shapes=[
            pltpu.VMEM((3, rows, width), BF16),
            pltpu.VMEM((3, heads, rows, HD), BF16),
            pltpu.VMEM((heads, rows, 2 * HD), BF16),
            pltpu.VMEM((2, 2, 4, heads, rows, HD), BF16),
            pltpu.VMEM((heads, rows, 1), F32),
            pltpu.VMEM((heads, rows, 1), F32),
            pltpu.VMEM((heads, rows, 1), F32),
            pltpu.VMEM((heads, rows, HD), F32),
            pltpu.VMEM((heads, rows, HD), F32),
            pltpu.VMEM((heads, 2 * rows, HD), BF16),
            pltpu.VMEM((heads, n_mp, 2 * rows, HD), BF16),
            pltpu.VMEM((n_mp, width, cols), BF16),
            pltpu.VMEM((2 * rows, cols), F32),
            pltpu.VMEM((2, rows, cols), BF16),
            pltpu.SMEM((rows,), jnp.int32),
            pltpu.VMEM((cols,), F32),
            dma((3,)),
            dma((2,)),
            dma((2,)),
            dma,
            dma((heads, 6)),
            dma((heads, 2)),
            dma((2, 2, 4, heads)),
            dma((2, 4, heads)),
            dma((4, heads)),
            dma,
            dma,
            dma((2, halves + 1)),
            dma((2, halves + 1)),
            dma((2, halves)),
            dma((2, halves)),
            dma((2,)),
            dma((2,)),
            dma((heads,)),
            dma((heads,)),
            dma((heads, n_mp)),
            dma((heads, n_mp)),
        ],
        compiler_params=pltpu.CompilerParams(
            collective_id=0, has_side_effects=True, vmem_limit_bytes=65000000
        ),
    )(q, dq, k, v, dk, dv, flags, w, gate, x, dx)


def spreads(n, n_mp, q, x):
    cores = planes = sides = 2
    heads = q.shape[1] // HD
    return (
        n_mp == planes * cores
        and heads == 2
        and n == 2 * sides * heads
        and x.shape[1] % HD == 0
        and q.shape[0] % FRAME == 0
    )


def program(n, n_mp, q, dq, k, v, dk, dv, flags, w, gate, x, dx):
    call = spread_call if spreads(n, n_mp, q, x) else per_device
    return call(n, n_mp, q, dq, k, v, dk, dv, flags, w, gate, x, dx)


def solution(mesh):
    both = P("tm", "mp")
    placed = (both,) * 6 + (P("tm"), P("mp", None), P("mp"), both, both)
    return jax.shard_map(
        functools.partial(program, mesh.shape["tm"], mesh.shape["mp"]),
        mesh=mesh,
        in_specs=placed,
        out_specs=(both, both),
        check_vma=False,
    )
```

```python
import functools
import math

import jax
import jax.numpy as jnp
from jax import lax
from jax.experimental import pallas as pl
from jax.experimental.pallas import tpu as pltpu
from jax.sharding import PartitionSpec as P

HD = 128
FRAME = 32
MESH = pl.DeviceIdType.MESH
F32 = jnp.float32
BF16 = jnp.bfloat16


def ring_place(t, n):
    return jnp.where(t % 2 == 0, t // 2, n - 1 - t // 2)


def ring_member(r, n):
    return jnp.where(r < n // 2, 2 * r, 2 * (n - 1 - r) + 1)


def flipped(me, j):
    other = me
    bit = 1
    while bit <= j:
        if j & bit:
            other = other + bit * (1 - 2 * ((me // bit) % 2))
        bit *= 2
    return other


def dot_nt(a, b):
    return lax.dot_general(a, b, (((1,), (1,)), ((), ())), preferred_element_type=F32)


def dot_nn(a, b):
    return lax.dot_general(a, b, (((1,), (0,)), ((), ())), preferred_element_type=F32)


def fused(
    n,
    n_mp,
    move_w,
    q_hbm,
    dq_hbm,
    k_hbm,
    v_hbm,
    dk_hbm,
    dv_hbm,
    flags_hbm,
    w_hbm,
    gate_hbm,
    x_hbm,
    dx_hbm,
    out,
    d_out,
    own,
    qcat,
    tkv,
    kv,
    opp,
    m_s,
    l_s,
    c_s,
    a_s,
    g_s,
    ao,
    wbuf,
    acc,
    xbuf,
    flags,
    gate,
    own_sem,
    x_sem,
    small_sem,
    w_local,
    ks,
    kr,
    ws,
    wr,
    as_,
    ar,
):
    rows, width = q_hbm.shape
    heads = width // HD
    cols = out.shape[1]
    half = n // 2
    t = lax.axis_index("tm")
    m = lax.axis_index("mp")
    place = ring_place(t, n)
    right = ring_member((place + 1) % n, n)
    left = ring_member((place + n - 1) % n, n)
    peers = [flipped(m, j) for j in range(n_mp)]
    factor = 1.0 / math.sqrt(HD)

    def lanes(h):
        return slice(h * HD, (h + 1) * HD)

    loads = [
        pltpu.make_async_copy(src, own.at[i], own_sem.at[i])
        for i, src in enumerate((k_hbm, v_hbm, dk_hbm, dv_hbm, q_hbm, dq_hbm))
    ]
    loads.append(pltpu.make_async_copy(flags_hbm, flags, small_sem.at[0]))
    for load in loads:
        load.start()

    barrier = pltpu.get_barrier_semaphore()
    for dev in [(right, m), (left, m)] + [(t, peers[j]) for j in range(1, n_mp)]:
        pl.semaphore_signal(barrier, inc=1, device_id=dev, device_id_type=MESH)
    pl.semaphore_wait(barrier, 1 + n_mp)

    def exists(d, s, p):
        return s < half or (s == half and (p < 2) == (d == 0))

    def kv_copy(h, d, s, p):
        side = slice(d * rows, (d + 1) * rows)
        if s > 1:
            src = kv.at[h, s - 2, p, side]
        elif p < 2:
            src = (k_hbm, v_hbm)[p].at[:, lanes(h)]
        else:
            src = tkv.at[h, p - 2]
        dst = kv.at[h, s - 1, p, side] if s < half else opp.at[h, p]
        return pltpu.make_async_remote_copy(
            src_ref=src,
            dst_ref=dst,
            send_sem=ks.at[h, d, s - 1, p],
            recv_sem=kr.at[h, d, s - 1, p],
            device_id=((right, left)[d], m),
            device_id_type=MESH,
        )

    def send_own(h, pieces):
        for p in pieces:
            for d in (0, 1):
                kv_copy(h, d, 1, p).start()

    def w_copy(h, j):
        span = pl.ds(pl.multiple_of(peers[j] * cols, HD), cols)
        part = slice(h * HD, (h + 1) * HD)
        if j == 0:
            return pltpu.make_async_copy(
                w_hbm.at[part, span], wbuf.at[0, part], w_local.at[h]
            )
        return pltpu.make_async_remote_copy(
            src_ref=w_hbm.at[part, span],
            dst_ref=wbuf.at[j, part],
            send_sem=ws.at[h, j],
            recv_sem=wr.at[h, j],
            device_id=(t, peers[j]),
            device_id_type=MESH,
        )

    def ao_copy(h, j):
        relay = j % 2 == 1 and j > 1
        return pltpu.make_async_remote_copy(
            src_ref=ao.at[h, j - 1 if relay else 0],
            dst_ref=ao.at[h, j],
            send_sem=as_.at[h, j],
            recv_sem=ar.at[h, j],
            device_id=(t, peers[1] if relay else peers[j]),
            device_id_type=MESH,
        )

    send_own(0, (0, 1))
    if move_w:
        for h in range(heads):
            for j in list(range(2, n_mp)) + [1, 0]:
                w_copy(h, j).start()
    x_loads = [
        pltpu.make_async_copy(src, xbuf.at[i], x_sem.at[i])
        for i, src in enumerate((x_hbm, dx_hbm))
    ]
    x_loads.append(pltpu.make_async_copy(gate_hbm, gate, small_sem.at[1]))
    for load in x_loads:
        load.start()
    for load in loads:
        load.wait()

    live = [
        jnp.where(flags[i * FRAME] > 0, 1.0, 0.0).astype(F32)
        for i in range(rows // FRAME)
    ]

    def masked(value, i):
        scale = jnp.full(value.shape, live[i], F32)
        return (value.astype(F32) * scale).astype(BF16)

    for h in range(heads):
        for i in range(rows // FRAME):
            part = slice(i * FRAME, (i + 1) * FRAME)
            tkv[h, 0, part] = masked(own[2, part, lanes(h)], i)
            tkv[h, 1, part] = masked(own[3, part, lanes(h)], i)
        if h == 0:
            send_own(0, (2, 3))
            for g in range(1, heads):
                send_own(g, (0, 1))
        else:
            send_own(h, (2, 3))
    for h in range(heads):
        for i in range(rows // FRAME):
            part = slice(i * FRAME, (i + 1) * FRAME)
            qcat[h, part, 0:HD] = masked(own[5, part, lanes(h)], i)
        qcat[h, :, HD : 2 * HD] = own[4, :, lanes(h)]

    def attend(h, k, tk, values, first):
        queries = qcat[h, :, HD : 2 * HD]
        scores = dot_nt(queries, k)
        d_scores = dot_nt(qcat[h], jnp.concatenate([k, tk], axis=1)) * factor
        peak = jnp.max(scores, axis=1, keepdims=True)
        if not first:
            peak_old = m_s[h]
            peak = jnp.maximum(peak_old, peak)
            rescale = jnp.exp((peak_old - peak) * factor)
        weights = jnp.exp((scores - peak) * factor)
        product = weights * d_scores
        total = jnp.sum(weights, axis=1, keepdims=True)
        slope = jnp.sum(product, axis=1, keepdims=True)
        weights_b = weights.astype(BF16)
        product_b = product.astype(BF16)
        v, tv = values()
        primal = dot_nn(weights_b, v)
        tangent = dot_nn(product_b, v) + dot_nn(weights_b, tv)
        m_s[h] = peak
        if first:
            l_s[h] = total
            c_s[h] = slope
            a_s[h] = primal
            g_s[h] = tangent
        else:
            l_s[h] = l_s[h] * rescale + total
            c_s[h] = c_s[h] * rescale + slope
            a_s[h] = a_s[h] * rescale + primal
            g_s[h] = g_s[h] * rescale + tangent

    def finish(h):
        inverse = 1.0 / l_s[h]
        outputs = a_s[h] * inverse
        d_outputs = g_s[h] * inverse - (c_s[h] * inverse) * outputs
        ao[h, 0, 0:rows] = outputs.astype(BF16)
        ao[h, 0, rows : 2 * rows] = d_outputs.astype(BF16)
        for j in list(range(2, n_mp, 2)) + [1]:
            ao_copy(h, j).start()

    def relay(h):
        for j in range(2, n_mp, 2):
            ao_copy(h, j).wait_recv()
            ao_copy(h, j + 1).start()

    for h in range(heads):
        attend(
            h, own[0, :, lanes(h)], tkv[h, 0], lambda: (own[1, :, lanes(h)], tkv[h, 1]), True
        )
    for s in range(1, half):
        for h in range(heads):
            for p in range(4):
                for d in (0, 1):
                    kv_copy(h, d, s, p).wait_recv()
                    if exists(d, s + 1, p):
                        kv_copy(h, d, s + 1, p).start()
            attend(
                h,
                kv[h, s - 1, 0],
                kv[h, s - 1, 2],
                lambda: (kv[h, s - 1, 1], kv[h, s - 1, 3]),
                False,
            )
    for h in range(heads):
        def opposite(first_p, second_p):
            kv_copy(h, 0, half, first_p).wait_recv()
            kv_copy(h, 1, half, second_p).wait_recv()
            return opp[h, first_p], opp[h, second_p]

        keys, d_keys = opposite(0, 2)
        attend(h, keys, d_keys, lambda: opposite(1, 3), False)
        finish(h)

    step = 2 * HD if cols % (2 * HD) == 0 else cols
    chunks = [slice(c, c + step) for c in range(0, cols, step)]

    def w_part(h, j, chunk):
        part = slice(h * HD, (h + 1) * HD)
        if move_w:
            return wbuf[j, part, chunk]
        return w_hbm[peers[j], part, chunk]

    def project(slots, chunk):
        attn = jnp.concatenate([ao[h, j] for h, j in slots], axis=1)
        weight = jnp.concatenate([w_part(h, j, chunk) for h, j in slots], axis=0)
        return dot_nn(attn, weight)

    if move_w:
        for h in range(heads):
            w_copy(h, 0).wait()
            for j in range(1, n_mp):
                w_copy(h, j).wait_recv()
    for load in x_loads:
        load.wait()
    last = heads - 1
    for h in range(heads):
        ao_copy(h, 1).wait_recv()
    near = [(h, j) for h in range(heads) for j in (0, 1)]
    for chunk in chunks:
        acc[:, chunk] = project(near, chunk)
    for h in range(last):
        relay(h)
    for h in range(last):
        for j in range(3, n_mp, 2):
            ao_copy(h, j).wait_recv()
    far = [(h, j) for h in range(last) for j in range(2, n_mp)]
    for chunk in chunks:
        acc[:, chunk] += project(far, chunk)
    for h in range(heads):
        for s in range(1, half + 1):
            for p in range(4):
                for d in (0, 1):
                    if exists(d, s, p):
                        kv_copy(h, d, s, p).wait_send()
        if move_w:
            for j in range(1, n_mp):
                w_copy(h, j).wait_send()
    relay(last)
    even = [(last, j) for j in range(2, n_mp, 2)]
    for chunk in chunks:
        acc[:, chunk] += project(even, chunk)
    for j in range(3, n_mp, 2):
        ao_copy(last, j).wait_recv()
    odd = [(last, j) for j in range(3, n_mp, 2)]
    for chunk in chunks:
        part = acc[:, chunk] + project(odd, chunk)
        scale = gate[chunk].reshape(1, step)
        out[:, chunk] = (xbuf[0, :, chunk].astype(F32) + scale * part[0:rows]).astype(BF16)
        for i in range(rows // FRAME):
            piece = slice(i * FRAME, (i + 1) * FRAME)
            base = xbuf[1, piece, chunk].astype(F32)
            base = base * jnp.full(base.shape, live[i], F32)
            delta = part[rows + i * FRAME : rows + (i + 1) * FRAME]
            d_out[piece, chunk] = (base + scale * delta).astype(BF16)

    for h in range(heads):
        for j in range(1, n_mp):
            ao_copy(h, j).wait_send()


def per_device(n, n_mp, q, dq, k, v, dk, dv, flags, w, gate, x, dx):
    rows, width = q.shape
    cols = x.shape[1]
    heads = width // HD
    half = n // 2
    move_w = cols % HD == 0
    if not move_w:
        w = lax.all_to_all(w, "mp", split_axis=1, concat_axis=0, tiled=True)
        w = w.reshape(n_mp, width, cols)
    anywhere = pl.BlockSpec(memory_space=pl.ANY)
    vmem = pl.BlockSpec(memory_space=pltpu.VMEM)
    dma = pltpu.SemaphoreType.DMA
    return pl.pallas_call(
        functools.partial(fused, n, n_mp, move_w),
        out_shape=(pltpu.VMEM(x.shape, BF16), pltpu.VMEM(x.shape, BF16)),
        in_specs=[anywhere] * 6
        + [anywhere, anywhere if move_w else vmem, anywhere]
        + [anywhere] * 2,
        out_specs=(vmem, vmem),
        scratch_shapes=[
            pltpu.VMEM((6, rows, width), BF16),
            pltpu.VMEM((heads, rows, 2 * HD), BF16),
            pltpu.VMEM((heads, 2, rows, HD), BF16),
            pltpu.VMEM((heads, half - 1, 4, 2 * rows, HD), BF16),
            pltpu.VMEM((heads, 4, rows, HD), BF16),
            pltpu.VMEM((heads, rows, 1), F32),
            pltpu.VMEM((heads, rows, 1), F32),
            pltpu.VMEM((heads, rows, 1), F32),
            pltpu.VMEM((heads, rows, HD), F32),
            pltpu.VMEM((heads, rows, HD), F32),
            pltpu.VMEM((heads, n_mp, 2 * rows, HD), BF16),
            pltpu.VMEM((n_mp, width, cols) if move_w else (1, 16, HD), BF16),
            pltpu.VMEM((2 * rows, cols), F32),
            pltpu.VMEM((2, rows, cols), BF16),
            pltpu.SMEM((rows,), jnp.int32),
            pltpu.VMEM((cols,), F32),
            dma((6,)),
            dma((2,)),
            dma((2,)),
            dma((heads,)),
            dma((heads, 2, half, 4)),
            dma((heads, 2, half, 4)),
            dma((heads, n_mp)),
            dma((heads, n_mp)),
            dma((heads, n_mp)),
            dma((heads, n_mp)),
        ],
        compiler_params=pltpu.CompilerParams(
            collective_id=0, has_side_effects=True, vmem_limit_bytes=65000000
        ),
    )(q, dq, k, v, dk, dv, flags, w, gate, x, dx)


def gathered(
    n,
    n_mp,
    subs,
    q_hbm,
    dq_hbm,
    k_hbm,
    v_hbm,
    dk_hbm,
    dv_hbm,
    flags_hbm,
    w_hbm,
    gate_hbm,
    x_hbm,
    dx_hbm,
    out,
    d_out,
    own,
    qpack,
    pack,
    qcat,
    kv,
    m_s,
    l_s,
    c_s,
    a_s,
    g_s,
    res,
    ao,
    wbuf,
    acc,
    xbuf,
    flags,
    gate,
    own_sem,
    raw_sem,
    x_sem,
    small_sem,
    w_local,
    qs_,
    qr,
    ks,
    kr,
    fs,
    wts,
    wtr,
    wxs,
    wxr,
    wys,
    wyr,
    rs,
    rr,
    as_,
    ar,
):
    rows, width = q_hbm.shape
    heads = width // HD
    cols = out.shape[1]
    part = rows // subs
    t = lax.axis_index("tm")
    m = lax.axis_index("mp")
    z, y = t // 2, t % 2
    plane, core = m // 2, m % 2
    side = z // 2
    role = jnp.where(side == 0, 1 - z % 2, z % 2)
    far = (side + core) % 2
    home = role == 0
    itself = jnp.logical_and(home, jnp.logical_and(side == core, y == core))

    def chip(side_, role_):
        return 2 * side_ + jnp.where(side_ == 0, 1 - role_, role_)

    homes = [(2 * chip(core, 0) + j, 2 * plane + y) for j in range(heads)]
    at_home = [jnp.logical_and(itself, y == j) for j in range(heads)]
    sources = [
        (2 * chip((side + i // 2) % 2, i % 2) + core, 2 * plane + side)
        for i in range(4)
    ]
    twin = (t, 2 * plane + 1 - core)
    across = (t, 2 * (1 - plane) + core)
    diagonal = (t, 2 * (1 - plane) + 1 - core)
    row_peer = (2 * z + 1 - y, m)
    factor = 1.0 / math.sqrt(HD)

    def lanes(h):
        return slice(h * HD, (h + 1) * HD)

    def both(flag, yes, no):
        pl.when(flag)(yes)
        pl.when(jnp.logical_not(flag))(no)

    def unless(flag, no):
        pl.when(jnp.logical_not(flag))(no)

    barrier = pltpu.get_barrier_semaphore()

    def greet(dev):
        pl.semaphore_signal(barrier, inc=1, device_id=dev, device_id_type=MESH)

    for j in range(heads):
        unless(at_home[j], lambda: greet(homes[j]))

    @pl.when(home)
    def _():
        for i in (3, 2, 1):
            greet(sources[i])
        unless(itself, lambda: greet(sources[0]))

    for dev in (across, diagonal, row_peer, twin):
        greet(dev)

    loads = [
        pltpu.make_async_copy(src, own.at[i], own_sem.at[i])
        for i, src in enumerate((dq_hbm, dk_hbm, dv_hbm))
    ]
    loads.append(pltpu.make_async_copy(flags_hbm, flags, small_sem.at[0]))
    raw = []
    for j in range(heads):
        for i, (src, dst) in enumerate(
            (
                (q_hbm, qpack.at[j, :, HD : 2 * HD]),
                (k_hbm, pack.at[j, 0]),
                (v_hbm, pack.at[j, 2]),
            )
        ):
            raw.append(
                pltpu.make_async_copy(src.at[:, lanes(j)], dst, raw_sem.at[j, i])
            )
    for load in loads + raw:
        load.start()
    for load in loads:
        load.wait()

    live = [
        jnp.where(flags[i * FRAME] > 0, 1.0, 0.0).astype(F32)
        for i in range(rows // FRAME)
    ]

    def masked(value, i):
        scale = jnp.full(value.shape, live[i], F32)
        return (value.astype(F32) * scale).astype(BF16)

    for h in range(heads):
        for i in range(rows // FRAME):
            piece = slice(i * FRAME, (i + 1) * FRAME)
            qpack[h, piece, 0:HD] = masked(own[0, piece, lanes(h)], i)
            pack[h, 1, piece] = masked(own[1, piece, lanes(h)], i)
            pack[h, 3, piece] = masked(own[2, piece, lanes(h)], i)
    for load in raw:
        load.wait()

    pl.semaphore_wait(
        barrier,
        4 + heads + 4 * home.astype(jnp.int32) - 2 * itself.astype(jnp.int32),
    )

    def q_ends(j):
        slot = 2 * far + role
        return qpack.at[j], qcat.at[slot], qr.at[slot]

    def kv_ends(j, sub):
        blk = 2 * y + role
        src = pack.at[j, :, sub * part : (sub + 1) * part]
        return src, kv.at[far, sub, :, blk], kr.at[far, sub, blk]

    def remote(ends, send_sem, dev):
        src, dst, sem = ends
        return pltpu.make_async_remote_copy(
            src_ref=src,
            dst_ref=dst,
            send_sem=send_sem,
            recv_sem=sem,
            device_id=dev,
            device_id_type=MESH,
        )

    def q_remote(j):
        return remote(q_ends(j), qs_.at[j], homes[j])

    def kv_remote(j, sub):
        return remote(kv_ends(j, sub), ks.at[j, sub], homes[j])

    for j in range(heads):
        both(
            at_home[j],
            lambda: pltpu.make_async_copy(*q_ends(j)).start(),
            lambda: q_remote(j).start(),
        )
    for sub in range(subs):
        for j in range(heads):
            both(
                at_home[j],
                lambda: pltpu.make_async_copy(*kv_ends(j, sub)).start(),
                lambda: kv_remote(j, sub).start(),
            )

    tile = 16
    y_rows = (width // tile * 5 // 16) * tile
    rest = slice(2 * y_rows, width)
    halves = 2 if cols % (2 * HD) == 0 else 1
    span = cols // halves

    def y_part(index):
        return pl.ds(pl.multiple_of(index * y_rows, tile), y_rows)

    def w_cols(owner, first, size):
        return pl.ds(pl.multiple_of(owner * cols + first, HD), size)

    def w_cross(slot, piece):
        dev = across if slot == 0 else diagonal
        if piece < halves:
            rows_ = y_part(y)
            first, size = piece * span, span
        else:
            rows_ = rest
            first, size = (piece - halves) * span, span
        return remote(
            (
                w_hbm.at[rows_, w_cols(dev[1], first, size)],
                wbuf.at[2 + slot, rows_, pl.ds(first, size)],
                wxr.at[slot, piece],
            ),
            wxs.at[slot, piece],
            dev,
        )

    def w_row(slot, piece):
        ref = wbuf.at[2 + slot, y_part(y), pl.ds(piece * span, span)]
        return remote((ref, ref, wyr.at[slot, piece]), wys.at[slot, piece], row_peer)

    def w_row_relay(piece):
        for slot in range(2):
            w_cross(slot, piece).wait_recv()
            w_row(slot, piece).start()

    w_twin = remote(
        (w_hbm.at[:, w_cols(twin[1], 0, cols)], wbuf.at[1], wtr), wts, twin
    )
    w_own = pltpu.make_async_copy(w_hbm.at[:, w_cols(m, 0, cols)], wbuf.at[0], w_local)

    for piece in range(2 * halves):
        for slot in range(2):
            w_cross(slot, piece).start()
    w_twin.start()
    w_own.start()
    x_loads = [
        pltpu.make_async_copy(src, xbuf.at[i], x_sem.at[i])
        for i, src in enumerate((x_hbm, dx_hbm))
    ]
    x_loads.append(pltpu.make_async_copy(gate_hbm, gate, small_sem.at[1]))
    for load in x_loads:
        load.start()

    def to_twin(rel, sub, i):
        blk = 2 * core + i
        ref = kv.at[rel, sub, :, blk]
        return remote((ref, ref, kr.at[rel, sub, blk]), fs.at[rel, sub, i], twin)

    def kv_wait(rel, sub, blk):
        ref = kv.at[rel, sub, :, blk]
        pltpu.make_async_copy(ref, ref, kr.at[rel, sub, blk]).wait()

    def arrivals(rel, sub):
        for i in range(2):
            kv_wait(rel, sub, 2 * core + i)
            to_twin(rel, sub, i).start()
        for i in range(2):
            kv_wait(rel, sub, 2 * (1 - core) + i)

    def q_wait(i):
        pltpu.make_async_copy(qcat.at[i], qcat.at[i], qr.at[i]).wait()

    def attend(rel, sub, i):
        first = rel == 0 and sub == 0
        keys = 4 * part
        k, tk, v, tv = (kv[rel, sub, p].reshape(keys, HD) for p in range(4))
        scores = dot_nt(qcat[i, :, HD : 2 * HD], k)
        d_scores = dot_nt(qcat[i], jnp.concatenate([k, tk], axis=1)) * factor
        peak = jnp.max(scores, axis=1, keepdims=True)
        if not first:
            peak_old = m_s[i]
            peak = jnp.maximum(peak_old, peak)
            rescale = jnp.exp((peak_old - peak) * factor)
        weights = jnp.exp((scores - peak) * factor)
        product = weights * d_scores
        total = jnp.sum(weights, axis=1, keepdims=True)
        slope = jnp.sum(product, axis=1, keepdims=True)
        weights_b = weights.astype(BF16)
        product_b = product.astype(BF16)
        wide = dot_nn(weights_b, jnp.concatenate([v, tv], axis=1))
        primal = wide[:, 0:HD]
        tangent = dot_nn(product_b, v) + wide[:, HD : 2 * HD]
        if not first:
            total = l_s[i] * rescale + total
            slope = c_s[i] * rescale + slope
            primal = a_s[i] * rescale + primal
            tangent = g_s[i] * rescale + tangent
        if rel == 1 and sub == subs - 1:
            inverse = 1.0 / total
            outputs = primal * inverse
            d_outputs = tangent * inverse - (slope * inverse) * outputs
            res[i, 0] = outputs.astype(BF16)
            res[i, 1] = d_outputs.astype(BF16)
        else:
            m_s[i] = peak
            l_s[i] = total
            c_s[i] = slope
            a_s[i] = primal
            g_s[i] = tangent

    def res_ends(i, a):
        return res.at[i, a], ao.at[y, 0, a], rr.at[y, a]

    def res_remote(i, a):
        return remote(res_ends(i, a), rs.at[i, a], sources[i])

    def res_start(i):
        def local():
            for a in range(2):
                pltpu.make_async_copy(*res_ends(i, a)).start()

        def away():
            for a in range(2):
                res_remote(i, a).start()

        if i == 0:
            both(itself, local, away)
        else:
            away()

    @pl.when(home)
    def _():
        q_wait(0)
        q_wait(1)
        for sub in range(subs):
            arrivals(0, sub)
            for i in (0, 1):
                attend(0, sub, i)
        w_row_relay(0)
        q_wait(2)
        q_wait(3)
        for sub in range(subs):
            for i in (2, 3):
                attend(0, sub, i)
        for piece in range(1, halves):
            w_row_relay(piece)
        for sub in range(subs):
            arrivals(1, sub)
            for i in (2, 3, 0, 1):
                attend(1, sub, i)
                if sub == subs - 1:
                    res_start(i)

    @pl.when(jnp.logical_not(home))
    def _():
        for piece in range(halves):
            w_row_relay(piece)

    def ao_copy(h, j, a):
        src = ao.at[h, 2 if j == 3 else 0, a]
        dst = ao.at[h, j, a]
        dev = across if j == 2 else twin
        return remote((src, dst, ar.at[h, j, a]), as_.at[h, j, a], dev)

    def own_heads(h, a):
        ref = ao.at[h, 0, a]
        pltpu.make_async_copy(ref, ref, rr.at[h, a]).wait()
        ao_copy(h, 2, a).start()
        ao_copy(h, 1, a).start()

    def cross_heads(h, a):
        ao_copy(h, 2, a).wait_recv()
        ao_copy(h, 3, a).start()

    step = 2 * HD if cols % (2 * HD) == 0 else cols
    chunks = [slice(c, c + step) for c in range(0, cols, step)]

    def project(slots, a, chunk):
        attn = jnp.concatenate([ao[h, j, a] for h, j in slots], axis=1)
        weight = jnp.concatenate(
            [wbuf[j, h * HD : (h + 1) * HD, chunk] for h, j in slots], axis=0
        )
        return dot_nn(attn, weight)

    own_plane = [(h, j) for j in (0, 1) for h in range(heads)]
    other_plane = [(h, j) for j in (2, 3) for h in range(heads)]
    for a in range(2):
        for h in range(heads):
            own_heads(h, a)
    w_own.wait()
    w_twin.wait_recv()
    for load in x_loads:
        load.wait()
    for a in range(2):
        for h in range(heads):
            ao_copy(h, 1, a).wait_recv()
        for chunk in chunks:
            acc[a, :, chunk] = project(own_plane, a, chunk)
    for slot in range(2):
        for piece in range(halves, 2 * halves):
            w_cross(slot, piece).wait_recv()
        for piece in range(halves):
            w_row(slot, piece).wait_recv()
    for a in range(2):
        for h in range(heads):
            cross_heads(h, a)
    for h in range(heads):
        ao_copy(h, 3, 0).wait_recv()
    for chunk in chunks:
        total = acc[0, :, chunk] + project(other_plane, 0, chunk)
        scale = gate[chunk].reshape(1, step)
        out[:, chunk] = (xbuf[0, :, chunk].astype(F32) + scale * total).astype(BF16)
    for h in range(heads):
        ao_copy(h, 3, 1).wait_recv()
    for chunk in chunks:
        total = acc[1, :, chunk] + project(other_plane, 1, chunk)
        scale = gate[chunk].reshape(1, step)
        for i in range(rows // FRAME):
            piece = slice(i * FRAME, (i + 1) * FRAME)
            base = xbuf[1, piece, chunk].astype(F32)
            base = base * jnp.full(base.shape, live[i], F32)
            d_out[piece, chunk] = (base + scale * total[piece]).astype(BF16)

    for j in range(heads):

        def sent():
            q_remote(j).wait_send()
            for sub in range(subs):
                kv_remote(j, sub).wait_send()

        unless(at_home[j], sent)
    for slot in range(2):
        for piece in range(2 * halves):
            w_cross(slot, piece).wait_send()
        for piece in range(halves):
            w_row(slot, piece).wait_send()
    w_twin.wait_send()

    @pl.when(home)
    def _():
        for rel in range(2):
            for sub in range(subs):
                for i in range(2):
                    to_twin(rel, sub, i).wait_send()
        for i in range(1, 4):
            for a in range(2):
                res_remote(i, a).wait_send()

        @pl.when(jnp.logical_not(itself))
        def _():
            for a in range(2):
                res_remote(0, a).wait_send()

    for h in range(heads):
        for j in range(1, n_mp):
            for a in range(2):
                ao_copy(h, j, a).wait_send()


def gathered_call(n, n_mp, q, dq, k, v, dk, dv, flags, w, gate, x, dx):
    rows, width = q.shape
    cols = x.shape[1]
    heads = width // HD
    halves = 2 if cols % (2 * HD) == 0 else 1
    subs = 3 if rows % (3 * FRAME) == 0 else 1
    part = rows // subs
    anywhere = pl.BlockSpec(memory_space=pl.ANY)
    vmem = pl.BlockSpec(memory_space=pltpu.VMEM)
    dma = pltpu.SemaphoreType.DMA
    return pl.pallas_call(
        functools.partial(gathered, n, n_mp, subs),
        out_shape=(pltpu.VMEM(x.shape, BF16), pltpu.VMEM(x.shape, BF16)),
        in_specs=[anywhere] * 11,
        out_specs=(vmem, vmem),
        scratch_shapes=[
            pltpu.VMEM((3, rows, width), BF16),
            pltpu.VMEM((heads, rows, 2 * HD), BF16),
            pltpu.VMEM((heads, 4, rows, HD), BF16),
            pltpu.VMEM((4, rows, 2 * HD), BF16),
            pltpu.VMEM((2, subs, 4, 4, part, HD), BF16),
            pltpu.VMEM((4, rows, 1), F32),
            pltpu.VMEM((4, rows, 1), F32),
            pltpu.VMEM((4, rows, 1), F32),
            pltpu.VMEM((4, rows, HD), F32),
            pltpu.VMEM((4, rows, HD), F32),
            pltpu.VMEM((4, 2, rows, HD), BF16),
            pltpu.VMEM((heads, n_mp, 2, rows, HD), BF16),
            pltpu.VMEM((n_mp, width, cols), BF16),
            pltpu.VMEM((2, rows, cols), F32),
            pltpu.VMEM((2, rows, cols), BF16),
            pltpu.SMEM((rows,), jnp.int32),
            pltpu.VMEM((cols,), F32),
            dma((3,)),
            dma((heads, 3)),
            dma((2,)),
            dma((2,)),
            dma,
            dma((heads,)),
            dma((4,)),
            dma((heads, subs)),
            dma((2, subs, 4)),
            dma((2, subs, 2)),
            dma,
            dma,
            dma((2, 2 * halves)),
            dma((2, 2 * halves)),
            dma((2, halves)),
            dma((2, halves)),
            dma((4, 2)),
            dma((heads, 2)),
            dma((heads, n_mp, 2)),
            dma((heads, n_mp, 2)),
        ],
        compiler_params=pltpu.CompilerParams(
            collective_id=0, has_side_effects=True, vmem_limit_bytes=65000000
        ),
    )(q, dq, k, v, dk, dv, flags, w, gate, x, dx)


def gathers(n, n_mp, q, x):
    heads = q.shape[1] // HD
    return (
        n_mp == 4
        and n == 8
        and heads == 2
        and x.shape[1] % HD == 0
        and q.shape[0] % FRAME == 0
    )


def program(n, n_mp, q, dq, k, v, dk, dv, flags, w, gate, x, dx):
    call = gathered_call if gathers(n, n_mp, q, x) else per_device
    return call(n, n_mp, q, dq, k, v, dk, dv, flags, w, gate, x, dx)


def solution(mesh):
    both = P("tm", "mp")
    placed = (both,) * 6 + (P("tm"), P("mp", None), P("mp"), both, both)
    return jax.shard_map(
        functools.partial(program, mesh.shape["tm"], mesh.shape["mp"]),
        mesh=mesh,
        in_specs=placed,
        out_specs=(both, both),
        check_vma=False,
    )
```

```python
import functools
import math

import jax
import jax.numpy as jnp
from jax import lax
from jax.experimental import pallas as pl
from jax.experimental.pallas import tpu as pltpu
from jax.sharding import PartitionSpec as P

HD = 128
FRAME = 32
MESH = pl.DeviceIdType.MESH
F32 = jnp.float32
BF16 = jnp.bfloat16


def ring_place(t, n):
    return jnp.where(t % 2 == 0, t // 2, n - 1 - t // 2)


def ring_member(r, n):
    return jnp.where(r < n // 2, 2 * r, 2 * (n - 1 - r) + 1)


def flipped(me, j):
    other = me
    bit = 1
    while bit <= j:
        if j & bit:
            other = other + bit * (1 - 2 * ((me // bit) % 2))
        bit *= 2
    return other


def dot_nt(a, b):
    return lax.dot_general(a, b, (((1,), (1,)), ((), ())), preferred_element_type=F32)


def dot_nn(a, b):
    return lax.dot_general(a, b, (((1,), (0,)), ((), ())), preferred_element_type=F32)


def fused(
    n,
    n_mp,
    move_w,
    q_hbm,
    dq_hbm,
    k_hbm,
    v_hbm,
    dk_hbm,
    dv_hbm,
    flags_hbm,
    w_hbm,
    gate_hbm,
    x_hbm,
    dx_hbm,
    out,
    d_out,
    own,
    qcat,
    tkv,
    kv,
    opp,
    m_s,
    l_s,
    c_s,
    a_s,
    g_s,
    ao,
    wbuf,
    acc,
    xbuf,
    flags,
    gate,
    own_sem,
    x_sem,
    small_sem,
    w_local,
    ks,
    kr,
    ws,
    wr,
    as_,
    ar,
):
    rows, width = q_hbm.shape
    heads = width // HD
    cols = out.shape[1]
    half = n // 2
    t = lax.axis_index("tm")
    m = lax.axis_index("mp")
    place = ring_place(t, n)
    right = ring_member((place + 1) % n, n)
    left = ring_member((place + n - 1) % n, n)
    peers = [flipped(m, j) for j in range(n_mp)]
    factor = 1.0 / math.sqrt(HD)

    def lanes(h):
        return slice(h * HD, (h + 1) * HD)

    loads = [
        pltpu.make_async_copy(src, own.at[i], own_sem.at[i])
        for i, src in enumerate((k_hbm, v_hbm, dk_hbm, dv_hbm, q_hbm, dq_hbm))
    ]
    loads.append(pltpu.make_async_copy(flags_hbm, flags, small_sem.at[0]))
    for load in loads:
        load.start()

    barrier = pltpu.get_barrier_semaphore()
    for dev in [(right, m), (left, m)] + [(t, peers[j]) for j in range(1, n_mp)]:
        pl.semaphore_signal(barrier, inc=1, device_id=dev, device_id_type=MESH)
    pl.semaphore_wait(barrier, 1 + n_mp)

    def exists(d, s, p):
        return s < half or (s == half and (p < 2) == (d == 0))

    def kv_copy(h, d, s, p):
        side = slice(d * rows, (d + 1) * rows)
        if s > 1:
            src = kv.at[h, s - 2, p, side]
        elif p < 2:
            src = (k_hbm, v_hbm)[p].at[:, lanes(h)]
        else:
            src = tkv.at[h, p - 2]
        dst = kv.at[h, s - 1, p, side] if s < half else opp.at[h, p]
        return pltpu.make_async_remote_copy(
            src_ref=src,
            dst_ref=dst,
            send_sem=ks.at[h, d, s - 1, p],
            recv_sem=kr.at[h, d, s - 1, p],
            device_id=((right, left)[d], m),
            device_id_type=MESH,
        )

    def send_own(h, pieces):
        for p in pieces:
            for d in (0, 1):
                kv_copy(h, d, 1, p).start()

    def w_copy(h, j):
        span = pl.ds(pl.multiple_of(peers[j] * cols, HD), cols)
        part = slice(h * HD, (h + 1) * HD)
        if j == 0:
            return pltpu.make_async_copy(
                w_hbm.at[part, span], wbuf.at[0, part], w_local.at[h]
            )
        return pltpu.make_async_remote_copy(
            src_ref=w_hbm.at[part, span],
            dst_ref=wbuf.at[j, part],
            send_sem=ws.at[h, j],
            recv_sem=wr.at[h, j],
            device_id=(t, peers[j]),
            device_id_type=MESH,
        )

    def ao_copy(h, j):
        relay = j % 2 == 1 and j > 1
        return pltpu.make_async_remote_copy(
            src_ref=ao.at[h, j - 1 if relay else 0],
            dst_ref=ao.at[h, j],
            send_sem=as_.at[h, j],
            recv_sem=ar.at[h, j],
            device_id=(t, peers[1] if relay else peers[j]),
            device_id_type=MESH,
        )

    send_own(0, (0, 1))
    if move_w:
        for h in range(heads):
            for j in list(range(2, n_mp)) + [1, 0]:
                w_copy(h, j).start()
    x_loads = [
        pltpu.make_async_copy(src, xbuf.at[i], x_sem.at[i])
        for i, src in enumerate((x_hbm, dx_hbm))
    ]
    x_loads.append(pltpu.make_async_copy(gate_hbm, gate, small_sem.at[1]))
    for load in x_loads:
        load.start()
    for load in loads:
        load.wait()

    live = [
        jnp.where(flags[i * FRAME] > 0, 1.0, 0.0).astype(F32)
        for i in range(rows // FRAME)
    ]

    def masked(value, i):
        scale = jnp.full(value.shape, live[i], F32)
        return (value.astype(F32) * scale).astype(BF16)

    for h in range(heads):
        for i in range(rows // FRAME):
            part = slice(i * FRAME, (i + 1) * FRAME)
            tkv[h, 0, part] = masked(own[2, part, lanes(h)], i)
            tkv[h, 1, part] = masked(own[3, part, lanes(h)], i)
        if h == 0:
            send_own(0, (2, 3))
            for g in range(1, heads):
                send_own(g, (0, 1))
        else:
            send_own(h, (2, 3))
    for h in range(heads):
        for i in range(rows // FRAME):
            part = slice(i * FRAME, (i + 1) * FRAME)
            qcat[h, part, 0:HD] = masked(own[5, part, lanes(h)], i)
        qcat[h, :, HD : 2 * HD] = own[4, :, lanes(h)]

    def attend(h, k, tk, values, first):
        queries = qcat[h, :, HD : 2 * HD]
        scores = dot_nt(queries, k)
        d_scores = dot_nt(qcat[h], jnp.concatenate([k, tk], axis=1)) * factor
        peak = jnp.max(scores, axis=1, keepdims=True)
        if not first:
            peak_old = m_s[h]
            peak = jnp.maximum(peak_old, peak)
            rescale = jnp.exp((peak_old - peak) * factor)
        weights = jnp.exp((scores - peak) * factor)
        product = weights * d_scores
        total = jnp.sum(weights, axis=1, keepdims=True)
        slope = jnp.sum(product, axis=1, keepdims=True)
        weights_b = weights.astype(BF16)
        product_b = product.astype(BF16)
        v, tv = values()
        primal = dot_nn(weights_b, v)
        tangent = dot_nn(product_b, v) + dot_nn(weights_b, tv)
        m_s[h] = peak
        if first:
            l_s[h] = total
            c_s[h] = slope
            a_s[h] = primal
            g_s[h] = tangent
        else:
            l_s[h] = l_s[h] * rescale + total
            c_s[h] = c_s[h] * rescale + slope
            a_s[h] = a_s[h] * rescale + primal
            g_s[h] = g_s[h] * rescale + tangent

    def finish(h):
        inverse = 1.0 / l_s[h]
        outputs = a_s[h] * inverse
        d_outputs = g_s[h] * inverse - (c_s[h] * inverse) * outputs
        ao[h, 0, 0:rows] = outputs.astype(BF16)
        ao[h, 0, rows : 2 * rows] = d_outputs.astype(BF16)
        for j in list(range(2, n_mp, 2)) + [1]:
            ao_copy(h, j).start()

    def relay(h):
        for j in range(2, n_mp, 2):
            ao_copy(h, j).wait_recv()
            ao_copy(h, j + 1).start()

    for h in range(heads):
        attend(
            h, own[0, :, lanes(h)], tkv[h, 0], lambda: (own[1, :, lanes(h)], tkv[h, 1]), True
        )
    for s in range(1, half):
        for h in range(heads):
            for p in range(4):
                for d in (0, 1):
                    kv_copy(h, d, s, p).wait_recv()
                    if exists(d, s + 1, p):
                        kv_copy(h, d, s + 1, p).start()
            attend(
                h,
                kv[h, s - 1, 0],
                kv[h, s - 1, 2],
                lambda: (kv[h, s - 1, 1], kv[h, s - 1, 3]),
                False,
            )
    for h in range(heads):
        def opposite(first_p, second_p):
            kv_copy(h, 0, half, first_p).wait_recv()
            kv_copy(h, 1, half, second_p).wait_recv()
            return opp[h, first_p], opp[h, second_p]

        keys, d_keys = opposite(0, 2)
        attend(h, keys, d_keys, lambda: opposite(1, 3), False)
        finish(h)

    step = 2 * HD if cols % (2 * HD) == 0 else cols
    chunks = [slice(c, c + step) for c in range(0, cols, step)]

    def w_part(h, j, chunk):
        part = slice(h * HD, (h + 1) * HD)
        if move_w:
            return wbuf[j, part, chunk]
        return w_hbm[peers[j], part, chunk]

    def project(slots, chunk):
        attn = jnp.concatenate([ao[h, j] for h, j in slots], axis=1)
        weight = jnp.concatenate([w_part(h, j, chunk) for h, j in slots], axis=0)
        return dot_nn(attn, weight)

    if move_w:
        for h in range(heads):
            w_copy(h, 0).wait()
            for j in range(1, n_mp):
                w_copy(h, j).wait_recv()
    for load in x_loads:
        load.wait()
    last = heads - 1
    for h in range(heads):
        ao_copy(h, 1).wait_recv()
    near = [(h, j) for h in range(heads) for j in (0, 1)]
    for chunk in chunks:
        acc[:, chunk] = project(near, chunk)
    for h in range(last):
        relay(h)
    for h in range(last):
        for j in range(3, n_mp, 2):
            ao_copy(h, j).wait_recv()
    far = [(h, j) for h in range(last) for j in range(2, n_mp)]
    for chunk in chunks:
        acc[:, chunk] += project(far, chunk)
    for h in range(heads):
        for s in range(1, half + 1):
            for p in range(4):
                for d in (0, 1):
                    if exists(d, s, p):
                        kv_copy(h, d, s, p).wait_send()
        if move_w:
            for j in range(1, n_mp):
                w_copy(h, j).wait_send()
    relay(last)
    even = [(last, j) for j in range(2, n_mp, 2)]
    for chunk in chunks:
        acc[:, chunk] += project(even, chunk)
    for j in range(3, n_mp, 2):
        ao_copy(last, j).wait_recv()
    odd = [(last, j) for j in range(3, n_mp, 2)]
    for chunk in chunks:
        part = acc[:, chunk] + project(odd, chunk)
        scale = gate[chunk].reshape(1, step)
        out[:, chunk] = (xbuf[0, :, chunk].astype(F32) + scale * part[0:rows]).astype(BF16)
        for i in range(rows // FRAME):
            piece = slice(i * FRAME, (i + 1) * FRAME)
            base = xbuf[1, piece, chunk].astype(F32)
            base = base * jnp.full(base.shape, live[i], F32)
            delta = part[rows + i * FRAME : rows + (i + 1) * FRAME]
            d_out[piece, chunk] = (base + scale * delta).astype(BF16)

    for h in range(heads):
        for j in range(1, n_mp):
            ao_copy(h, j).wait_send()


def per_device(n, n_mp, q, dq, k, v, dk, dv, flags, w, gate, x, dx):
    rows, width = q.shape
    cols = x.shape[1]
    heads = width // HD
    half = n // 2
    move_w = cols % HD == 0
    if not move_w:
        w = lax.all_to_all(w, "mp", split_axis=1, concat_axis=0, tiled=True)
        w = w.reshape(n_mp, width, cols)
    anywhere = pl.BlockSpec(memory_space=pl.ANY)
    vmem = pl.BlockSpec(memory_space=pltpu.VMEM)
    dma = pltpu.SemaphoreType.DMA
    return pl.pallas_call(
        functools.partial(fused, n, n_mp, move_w),
        out_shape=(pltpu.VMEM(x.shape, BF16), pltpu.VMEM(x.shape, BF16)),
        in_specs=[anywhere] * 6
        + [anywhere, anywhere if move_w else vmem, anywhere]
        + [anywhere] * 2,
        out_specs=(vmem, vmem),
        scratch_shapes=[
            pltpu.VMEM((6, rows, width), BF16),
            pltpu.VMEM((heads, rows, 2 * HD), BF16),
            pltpu.VMEM((heads, 2, rows, HD), BF16),
            pltpu.VMEM((heads, half - 1, 4, 2 * rows, HD), BF16),
            pltpu.VMEM((heads, 4, rows, HD), BF16),
            pltpu.VMEM((heads, rows, 1), F32),
            pltpu.VMEM((heads, rows, 1), F32),
            pltpu.VMEM((heads, rows, 1), F32),
            pltpu.VMEM((heads, rows, HD), F32),
            pltpu.VMEM((heads, rows, HD), F32),
            pltpu.VMEM((heads, n_mp, 2 * rows, HD), BF16),
            pltpu.VMEM((n_mp, width, cols) if move_w else (1, 16, HD), BF16),
            pltpu.VMEM((2 * rows, cols), F32),
            pltpu.VMEM((2, rows, cols), BF16),
            pltpu.SMEM((rows,), jnp.int32),
            pltpu.VMEM((cols,), F32),
            dma((6,)),
            dma((2,)),
            dma((2,)),
            dma((heads,)),
            dma((heads, 2, half, 4)),
            dma((heads, 2, half, 4)),
            dma((heads, n_mp)),
            dma((heads, n_mp)),
            dma((heads, n_mp)),
            dma((heads, n_mp)),
        ],
        compiler_params=pltpu.CompilerParams(
            collective_id=0, has_side_effects=True, vmem_limit_bytes=65000000
        ),
    )(q, dq, k, v, dk, dv, flags, w, gate, x, dx)


def gathered(
    n,
    n_mp,
    q_hbm,
    dq_hbm,
    k_hbm,
    v_hbm,
    dk_hbm,
    dv_hbm,
    flags_hbm,
    w_hbm,
    gate_hbm,
    x_hbm,
    dx_hbm,
    out,
    d_out,
    own,
    qpack,
    pack,
    qcat,
    kv,
    m_s,
    l_s,
    c_s,
    a_s,
    g_s,
    res,
    ao,
    wbuf,
    acc,
    xbuf,
    flags,
    gate,
    own_sem,
    raw_sem,
    x_sem,
    small_sem,
    w_local,
    qr,
    ks,
    kr,
    fs,
    wts,
    wtr,
    wxs,
    wxr,
    wys,
    wyr,
    rs,
    rr,
    as_,
    ar,
):
    rows, width = q_hbm.shape
    heads = width // HD
    cols = out.shape[1]
    t = lax.axis_index("tm")
    m = lax.axis_index("mp")
    z, y = t // 2, t % 2
    plane, core = m // 2, m % 2
    side = z // 2
    role = jnp.where(side == 0, 1 - z % 2, z % 2)
    home = role == 0
    itself = jnp.logical_and(home, y == core)

    def chip(side_, role_):
        return 2 * side_ + jnp.where(side_ == 0, 1 - role_, role_)

    order = (jnp.where(home, 1 - side, side), jnp.where(home, side, 1 - side))
    rels = (1 - role, role)
    homes = [(2 * chip(h, 0) + core, 2 * plane + y) for h in order]
    sources = [
        (2 * chip((side + g // 2) % 2, g % 2) + core, 2 * plane + y) for g in range(4)
    ]
    twin = (t, 2 * plane + 1 - core)
    across = (t, 2 * (1 - plane) + core)
    diagonal = (t, 2 * (1 - plane) + 1 - core)
    row_peer = (2 * z + 1 - y, m)
    factor = 1.0 / math.sqrt(HD)

    def lanes(h):
        return slice(h * HD, (h + 1) * HD)

    def both(flag, yes, no):
        pl.when(flag)(yes)
        pl.when(jnp.logical_not(flag))(no)

    def unless(flag, no):
        pl.when(jnp.logical_not(flag))(no)

    barrier = pltpu.get_barrier_semaphore()

    def greet(dev):
        pl.semaphore_signal(barrier, inc=1, device_id=dev, device_id_type=MESH)

    greet(homes[0])
    unless(itself, lambda: greet(homes[1]))

    @pl.when(home)
    def _():
        for i in (3, 2, 1):
            greet(sources[i])
        unless(itself, lambda: greet(sources[0]))

    for dev in (across, diagonal, row_peer, twin):
        greet(dev)

    loads = [
        pltpu.make_async_copy(src, own.at[i], own_sem.at[i])
        for i, src in enumerate((dq_hbm, dk_hbm, dv_hbm))
    ]
    loads.append(pltpu.make_async_copy(flags_hbm, flags, small_sem.at[0]))
    raw = []
    for j in range(heads):
        for i, (src, dst) in enumerate(
            (
                (q_hbm, qpack.at[j, :, HD : 2 * HD]),
                (k_hbm, pack.at[j, 0]),
                (v_hbm, pack.at[j, 2]),
            )
        ):
            raw.append(
                pltpu.make_async_copy(src.at[:, lanes(j)], dst, raw_sem.at[j, i])
            )
    for load in loads + raw:
        load.start()
    for load in loads:
        load.wait()

    live = [
        jnp.where(flags[i * FRAME] > 0, 1.0, 0.0).astype(F32)
        for i in range(rows // FRAME)
    ]

    def masked(value, i):
        scale = jnp.full(value.shape, live[i], F32)
        return (value.astype(F32) * scale).astype(BF16)

    for h in range(heads):
        for i in range(rows // FRAME):
            piece = slice(i * FRAME, (i + 1) * FRAME)
            qpack[h, piece, 0:HD] = masked(own[0, piece, lanes(h)], i)
            pack[h, 1, piece] = masked(own[1, piece, lanes(h)], i)
            pack[h, 3, piece] = masked(own[2, piece, lanes(h)], i)
    for load in raw:
        load.wait()

    pl.semaphore_wait(
        barrier,
        4 + heads + 4 * home.astype(jnp.int32) - 2 * itself.astype(jnp.int32),
    )

    def remote(ends, send_sem, dev):
        src, dst, sem = ends
        return pltpu.make_async_remote_copy(
            src_ref=src,
            dst_ref=dst,
            send_sem=send_sem,
            recv_sem=sem,
            device_id=dev,
            device_id_type=MESH,
        )

    def home_ends(o, piece):
        h = order[o]
        g = 2 * rels[o] + role
        if piece == 0:
            return qpack.at[h], qcat.at[g], qr.at[g]
        pair = slice(2 * piece - 2, 2 * piece)
        blk = 2 * g + y
        return pack.at[h, pair], kv.at[pair, blk], kr.at[piece - 1, blk]

    def home_copy(o, piece):
        return remote(home_ends(o, piece), ks.at[o, piece], homes[o])

    def home_all(o):
        for piece in range(3):
            home_copy(o, piece).start()

    def home_local():
        for piece in range(3):
            pltpu.make_async_copy(*home_ends(1, piece)).start()

    home_all(0)
    both(itself, home_local, lambda: home_all(1))

    tile = 16
    y_rows = (width // tile * 5 // 16) * tile
    rest = slice(2 * y_rows, width)
    halves = 2 if cols % (2 * HD) == 0 else 1
    span = cols // halves

    def y_part(index):
        return pl.ds(pl.multiple_of(index * y_rows, tile), y_rows)

    def w_cols(owner, first, size):
        return pl.ds(pl.multiple_of(owner * cols + first, HD), size)

    def w_cross(slot, piece):
        dev = across if slot == 0 else diagonal
        if piece < halves:
            rows_ = y_part(y)
            first, size = piece * span, span
        else:
            rows_ = rest
            first, size = (piece - halves) * span, span
        return remote(
            (
                w_hbm.at[rows_, w_cols(dev[1], first, size)],
                wbuf.at[2 + slot, rows_, pl.ds(first, size)],
                wxr.at[slot, piece],
            ),
            wxs.at[slot, piece],
            dev,
        )

    def w_row(slot, piece):
        ref = wbuf.at[2 + slot, y_part(y), pl.ds(piece * span, span)]
        return remote((ref, ref, wyr.at[slot, piece]), wys.at[slot, piece], row_peer)

    def w_row_relay(piece):
        for slot in range(2):
            w_cross(slot, piece).wait_recv()
            w_row(slot, piece).start()

    w_twin = remote(
        (w_hbm.at[:, w_cols(twin[1], 0, cols)], wbuf.at[1], wtr), wts, twin
    )
    w_own = pltpu.make_async_copy(w_hbm.at[:, w_cols(m, 0, cols)], wbuf.at[0], w_local)

    for piece in range(2 * halves):
        for slot in range(2):
            w_cross(slot, piece).start()
    w_twin.start()
    w_own.start()
    x_loads = [
        pltpu.make_async_copy(src, xbuf.at[i], x_sem.at[i])
        for i, src in enumerate((x_hbm, dx_hbm))
    ]
    x_loads.append(pltpu.make_async_copy(gate_hbm, gate, small_sem.at[1]))
    for load in x_loads:
        load.start()

    def to_twin(pair, g):
        ref = kv.at[2 * pair : 2 * pair + 2, 2 * g + core]
        return remote((ref, ref, kr.at[pair, 2 * g + core]), fs.at[pair, g], twin)

    def kv_wait(pair, blk):
        ref = kv.at[2 * pair : 2 * pair + 2, blk]
        pltpu.make_async_copy(ref, ref, kr.at[pair, blk]).wait()

    def arrive(g):
        for pair in range(2):
            kv_wait(pair, 2 * g + core)
            to_twin(pair, g).start()

    def from_twin(g):
        for pair in range(2):
            kv_wait(pair, 2 * g + 1 - core)

    def q_wait(i):
        pltpu.make_async_copy(qcat.at[i], qcat.at[i], qr.at[i]).wait()

    def attend(blocks, i):
        first = blocks[0] == 0
        last = blocks[1] == 8
        keys = (blocks[1] - blocks[0]) * rows
        k, tk, v, tv = (
            kv[p, blocks[0] : blocks[1]].reshape(keys, HD) for p in range(4)
        )
        scores = dot_nt(qcat[i, :, HD : 2 * HD], k)
        d_scores = dot_nt(qcat[i], jnp.concatenate([k, tk], axis=1)) * factor
        peak = jnp.max(scores, axis=1, keepdims=True)
        if not first:
            peak_old = m_s[i]
            peak = jnp.maximum(peak_old, peak)
            rescale = jnp.exp((peak_old - peak) * factor)
        weights = jnp.exp((scores - peak) * factor)
        product = weights * d_scores
        total = jnp.sum(weights, axis=1, keepdims=True)
        slope = jnp.sum(product, axis=1, keepdims=True)
        weights_b = weights.astype(BF16)
        product_b = product.astype(BF16)
        wide = dot_nn(weights_b, jnp.concatenate([v, tv], axis=1))
        primal = wide[:, 0:HD]
        tangent = dot_nn(product_b, v) + wide[:, HD : 2 * HD]
        if not first:
            total = l_s[i] * rescale + total
            slope = c_s[i] * rescale + slope
            primal = a_s[i] * rescale + primal
            tangent = g_s[i] * rescale + tangent
        if last:
            inverse = 1.0 / total
            outputs = primal * inverse
            d_outputs = tangent * inverse - (slope * inverse) * outputs
            res[i, 0] = outputs.astype(BF16)
            res[i, 1] = d_outputs.astype(BF16)
        else:
            m_s[i] = peak
            l_s[i] = total
            c_s[i] = slope
            a_s[i] = primal
            g_s[i] = tangent

    def res_ends(i, a):
        return res.at[i, a], ao.at[side, 0, a], rr.at[side, a]

    def res_remote(i, a):
        return remote(res_ends(i, a), rs.at[i, a], sources[i])

    def res_start(i):
        def local():
            for a in range(2):
                pltpu.make_async_copy(*res_ends(i, a)).start()

        def away():
            for a in range(2):
                res_remote(i, a).start()

        if i == 0:
            both(itself, local, away)
        else:
            away()

    @pl.when(home)
    def _():
        arrive(0)
        w_row_relay(0)
        arrive(2)
        arrive(1)
        for g in range(3):
            q_wait(g)
            from_twin(g)
        for i in range(3):
            attend((0, 6), i)
        for piece in range(1, halves):
            w_row_relay(piece)
        q_wait(3)
        attend((0, 6), 3)
        arrive(3)
        from_twin(3)
        for i in (3, 2, 1, 0):
            attend((6, 8), i)
            res_start(i)

    @pl.when(jnp.logical_not(home))
    def _():
        for piece in range(halves):
            w_row_relay(piece)

    def ao_copy(h, j, a):
        src = ao.at[h, 2 if j == 3 else 0, a]
        dst = ao.at[h, j, a]
        dev = across if j == 2 else twin
        return remote((src, dst, ar.at[h, j, a]), as_.at[h, j, a], dev)

    def own_heads(h, a):
        ref = ao.at[h, 0, a]
        pltpu.make_async_copy(ref, ref, rr.at[h, a]).wait()
        ao_copy(h, 2, a).start()
        ao_copy(h, 1, a).start()

    def cross_heads(h, a):
        ao_copy(h, 2, a).wait_recv()
        ao_copy(h, 3, a).start()

    step = 2 * HD if cols % (2 * HD) == 0 else cols
    chunks = [slice(c, c + step) for c in range(0, cols, step)]

    def project(slots, a, chunk):
        attn = jnp.concatenate([ao[heads_[h], j, a] for h, j in slots], axis=1)
        weight = jnp.concatenate([wbuf[j, w_rows[h], chunk] for h, j in slots], axis=0)
        return dot_nn(attn, weight)

    heads_ = (side, 1 - side)
    w_rows = [pl.ds(pl.multiple_of(h * HD, HD), HD) for h in heads_]
    near, far = heads_
    for a in range(2):
        own_heads(near, a)
    w_own.wait()
    w_twin.wait_recv()
    for load in x_loads:
        load.wait()
    for a in range(2):
        ao_copy(near, 1, a).wait_recv()
    for a in range(2):
        own_heads(far, a)
    for slot in range(2):
        for piece in range(halves, 2 * halves):
            w_cross(slot, piece).wait_recv()
        for piece in range(halves):
            w_row(slot, piece).wait_recv()
    for a in range(2):
        cross_heads(near, a)
    for a in range(2):
        ao_copy(far, 1, a).wait_recv()
    for a in range(2):
        for chunk in chunks:
            acc[a, :, chunk] = project([(0, 0), (0, 1), (1, 0), (1, 1)], a, chunk)
    for a in range(2):
        cross_heads(far, a)
    for a in range(2):
        ao_copy(near, 3, a).wait_recv()
    ao_copy(far, 3, 0).wait_recv()
    other_plane = [(0, 2), (0, 3), (1, 2), (1, 3)]
    for chunk in chunks:
        total = acc[0, :, chunk] + project(other_plane, 0, chunk)
        scale = gate[chunk].reshape(1, step)
        out[:, chunk] = (xbuf[0, :, chunk].astype(F32) + scale * total).astype(BF16)
    ao_copy(far, 3, 1).wait_recv()
    for chunk in chunks:
        total = acc[1, :, chunk] + project(other_plane, 1, chunk)
        scale = gate[chunk].reshape(1, step)
        for i in range(rows // FRAME):
            piece = slice(i * FRAME, (i + 1) * FRAME)
            base = xbuf[1, piece, chunk].astype(F32)
            base = base * jnp.full(base.shape, live[i], F32)
            d_out[piece, chunk] = (base + scale * total[piece]).astype(BF16)

    def sent(o):
        for piece in range(3):
            home_copy(o, piece).wait_send()

    sent(0)
    unless(itself, lambda: sent(1))
    for slot in range(2):
        for piece in range(2 * halves):
            w_cross(slot, piece).wait_send()
        for piece in range(halves):
            w_row(slot, piece).wait_send()
    w_twin.wait_send()

    @pl.when(home)
    def _():
        for g in range(4):
            for pair in range(2):
                to_twin(pair, g).wait_send()
        for i in range(1, 4):
            for a in range(2):
                res_remote(i, a).wait_send()

        @pl.when(jnp.logical_not(itself))
        def _():
            for a in range(2):
                res_remote(0, a).wait_send()

    for h in range(heads):
        for j in range(1, n_mp):
            for a in range(2):
                ao_copy(h, j, a).wait_send()


def gathered_call(n, n_mp, q, dq, k, v, dk, dv, flags, w, gate, x, dx):
    rows, width = q.shape
    cols = x.shape[1]
    heads = width // HD
    halves = 2 if cols % (2 * HD) == 0 else 1
    anywhere = pl.BlockSpec(memory_space=pl.ANY)
    vmem = pl.BlockSpec(memory_space=pltpu.VMEM)
    dma = pltpu.SemaphoreType.DMA
    return pl.pallas_call(
        functools.partial(gathered, n, n_mp),
        out_shape=(pltpu.VMEM(x.shape, BF16), pltpu.VMEM(x.shape, BF16)),
        in_specs=[anywhere] * 11,
        out_specs=(vmem, vmem),
        scratch_shapes=[
            pltpu.VMEM((3, rows, width), BF16),
            pltpu.VMEM((heads, rows, 2 * HD), BF16),
            pltpu.VMEM((heads, 4, rows, HD), BF16),
            pltpu.VMEM((4, rows, 2 * HD), BF16),
            pltpu.VMEM((4, 8, rows, HD), BF16),
            pltpu.VMEM((4, rows, 1), F32),
            pltpu.VMEM((4, rows, 1), F32),
            pltpu.VMEM((4, rows, 1), F32),
            pltpu.VMEM((4, rows, HD), F32),
            pltpu.VMEM((4, rows, HD), F32),
            pltpu.VMEM((4, 2, rows, HD), BF16),
            pltpu.VMEM((heads, n_mp, 2, rows, HD), BF16),
            pltpu.VMEM((n_mp, width, cols), BF16),
            pltpu.VMEM((2, rows, cols), F32),
            pltpu.VMEM((2, rows, cols), BF16),
            pltpu.SMEM((rows,), jnp.int32),
            pltpu.VMEM((cols,), F32),
            dma((3,)),
            dma((heads, 3)),
            dma((2,)),
            dma((2,)),
            dma,
            dma((4,)),
            dma((heads, 3)),
            dma((2, 8)),
            dma((2, 4)),
            dma,
            dma,
            dma((2, 2 * halves)),
            dma((2, 2 * halves)),
            dma((2, halves)),
            dma((2, halves)),
            dma((4, 2)),
            dma((heads, 2)),
            dma((heads, n_mp, 2)),
            dma((heads, n_mp, 2)),
        ],
        compiler_params=pltpu.CompilerParams(
            collective_id=0, has_side_effects=True, vmem_limit_bytes=65000000
        ),
    )(q, dq, k, v, dk, dv, flags, w, gate, x, dx)


def gathers(n, n_mp, q, x):
    heads = q.shape[1] // HD
    return (
        n_mp == 4
        and n == 8
        and heads == 2
        and x.shape[1] % HD == 0
        and q.shape[0] % FRAME == 0
    )


def program(n, n_mp, q, dq, k, v, dk, dv, flags, w, gate, x, dx):
    call = gathered_call if gathers(n, n_mp, q, x) else per_device
    return call(n, n_mp, q, dq, k, v, dk, dv, flags, w, gate, x, dx)


def solution(mesh):
    both = P("tm", "mp")
    placed = (both,) * 6 + (P("tm"), P("mp", None), P("mp"), both, both)
    return jax.shard_map(
        functools.partial(program, mesh.shape["tm"], mesh.shape["mp"]),
        mesh=mesh,
        in_specs=placed,
        out_specs=(both, both),
        check_vma=False,
    )
```

```python
import functools
import math

import jax
import jax.numpy as jnp
from jax import lax
from jax.experimental import pallas as pl
from jax.experimental.pallas import tpu as pltpu
from jax.sharding import PartitionSpec as P

HD = 128
FRAME = 32
MESH = pl.DeviceIdType.MESH
F32 = jnp.float32
BF16 = jnp.bfloat16


def ring_place(t, n):
    return jnp.where(t % 2 == 0, t // 2, n - 1 - t // 2)


def ring_member(r, n):
    return jnp.where(r < n // 2, 2 * r, 2 * (n - 1 - r) + 1)


def flipped(me, j):
    other = me
    bit = 1
    while bit <= j:
        if j & bit:
            other = other + bit * (1 - 2 * ((me // bit) % 2))
        bit *= 2
    return other


def dot_nt(a, b):
    return lax.dot_general(a, b, (((1,), (1,)), ((), ())), preferred_element_type=F32)


def dot_nn(a, b):
    return lax.dot_general(a, b, (((1,), (0,)), ((), ())), preferred_element_type=F32)


def fused(
    n,
    n_mp,
    move_w,
    q_hbm,
    dq_hbm,
    k_hbm,
    v_hbm,
    dk_hbm,
    dv_hbm,
    flags_hbm,
    w_hbm,
    gate_hbm,
    x_hbm,
    dx_hbm,
    out,
    d_out,
    own,
    qcat,
    tkv,
    kv,
    opp,
    m_s,
    l_s,
    c_s,
    a_s,
    g_s,
    ao,
    wbuf,
    acc,
    xbuf,
    flags,
    gate,
    own_sem,
    x_sem,
    small_sem,
    w_local,
    ks,
    kr,
    ws,
    wr,
    as_,
    ar,
):
    rows, width = q_hbm.shape
    heads = width // HD
    cols = out.shape[1]
    half = n // 2
    t = lax.axis_index("tm")
    m = lax.axis_index("mp")
    place = ring_place(t, n)
    right = ring_member((place + 1) % n, n)
    left = ring_member((place + n - 1) % n, n)
    peers = [flipped(m, j) for j in range(n_mp)]
    factor = 1.0 / math.sqrt(HD)

    def lanes(h):
        return slice(h * HD, (h + 1) * HD)

    loads = [
        pltpu.make_async_copy(src, own.at[i], own_sem.at[i])
        for i, src in enumerate((k_hbm, v_hbm, dk_hbm, dv_hbm, q_hbm, dq_hbm))
    ]
    loads.append(pltpu.make_async_copy(flags_hbm, flags, small_sem.at[0]))
    for load in loads:
        load.start()

    barrier = pltpu.get_barrier_semaphore()
    for dev in [(right, m), (left, m)] + [(t, peers[j]) for j in range(1, n_mp)]:
        pl.semaphore_signal(barrier, inc=1, device_id=dev, device_id_type=MESH)
    pl.semaphore_wait(barrier, 1 + n_mp)

    def exists(d, s, p):
        return s < half or (s == half and (p < 2) == (d == 0))

    def kv_copy(h, d, s, p):
        side = slice(d * rows, (d + 1) * rows)
        if s > 1:
            src = kv.at[h, s - 2, p, side]
        elif p < 2:
            src = (k_hbm, v_hbm)[p].at[:, lanes(h)]
        else:
            src = tkv.at[h, p - 2]
        dst = kv.at[h, s - 1, p, side] if s < half else opp.at[h, p]
        return pltpu.make_async_remote_copy(
            src_ref=src,
            dst_ref=dst,
            send_sem=ks.at[h, d, s - 1, p],
            recv_sem=kr.at[h, d, s - 1, p],
            device_id=((right, left)[d], m),
            device_id_type=MESH,
        )

    def send_own(h, pieces):
        for p in pieces:
            for d in (0, 1):
                kv_copy(h, d, 1, p).start()

    def w_copy(h, j):
        span = pl.ds(pl.multiple_of(peers[j] * cols, HD), cols)
        part = slice(h * HD, (h + 1) * HD)
        if j == 0:
            return pltpu.make_async_copy(
                w_hbm.at[part, span], wbuf.at[0, part], w_local.at[h]
            )
        return pltpu.make_async_remote_copy(
            src_ref=w_hbm.at[part, span],
            dst_ref=wbuf.at[j, part],
            send_sem=ws.at[h, j],
            recv_sem=wr.at[h, j],
            device_id=(t, peers[j]),
            device_id_type=MESH,
        )

    def ao_copy(h, j):
        relay = j % 2 == 1 and j > 1
        return pltpu.make_async_remote_copy(
            src_ref=ao.at[h, j - 1 if relay else 0],
            dst_ref=ao.at[h, j],
            send_sem=as_.at[h, j],
            recv_sem=ar.at[h, j],
            device_id=(t, peers[1] if relay else peers[j]),
            device_id_type=MESH,
        )

    send_own(0, (0, 1))
    if move_w:
        for h in range(heads):
            for j in list(range(2, n_mp)) + [1, 0]:
                w_copy(h, j).start()
    x_loads = [
        pltpu.make_async_copy(src, xbuf.at[i], x_sem.at[i])
        for i, src in enumerate((x_hbm, dx_hbm))
    ]
    x_loads.append(pltpu.make_async_copy(gate_hbm, gate, small_sem.at[1]))
    for load in x_loads:
        load.start()
    for load in loads:
        load.wait()

    live = [
        jnp.where(flags[i * FRAME] > 0, 1.0, 0.0).astype(F32)
        for i in range(rows // FRAME)
    ]

    def masked(value, i):
        scale = jnp.full(value.shape, live[i], F32)
        return (value.astype(F32) * scale).astype(BF16)

    for h in range(heads):
        for i in range(rows // FRAME):
            part = slice(i * FRAME, (i + 1) * FRAME)
            tkv[h, 0, part] = masked(own[2, part, lanes(h)], i)
            tkv[h, 1, part] = masked(own[3, part, lanes(h)], i)
        if h == 0:
            send_own(0, (2, 3))
            for g in range(1, heads):
                send_own(g, (0, 1))
        else:
            send_own(h, (2, 3))
    for h in range(heads):
        for i in range(rows // FRAME):
            part = slice(i * FRAME, (i + 1) * FRAME)
            qcat[h, part, 0:HD] = masked(own[5, part, lanes(h)], i)
        qcat[h, :, HD : 2 * HD] = own[4, :, lanes(h)]

    def attend(h, k, tk, values, first):
        queries = qcat[h, :, HD : 2 * HD]
        scores = dot_nt(queries, k)
        d_scores = dot_nt(qcat[h], jnp.concatenate([k, tk], axis=1)) * factor
        peak = jnp.max(scores, axis=1, keepdims=True)
        if not first:
            peak_old = m_s[h]
            peak = jnp.maximum(peak_old, peak)
            rescale = jnp.exp((peak_old - peak) * factor)
        weights = jnp.exp((scores - peak) * factor)
        product = weights * d_scores
        total = jnp.sum(weights, axis=1, keepdims=True)
        slope = jnp.sum(product, axis=1, keepdims=True)
        weights_b = weights.astype(BF16)
        product_b = product.astype(BF16)
        v, tv = values()
        primal = dot_nn(weights_b, v)
        tangent = dot_nn(product_b, v) + dot_nn(weights_b, tv)
        m_s[h] = peak
        if first:
            l_s[h] = total
            c_s[h] = slope
            a_s[h] = primal
            g_s[h] = tangent
        else:
            l_s[h] = l_s[h] * rescale + total
            c_s[h] = c_s[h] * rescale + slope
            a_s[h] = a_s[h] * rescale + primal
            g_s[h] = g_s[h] * rescale + tangent

    def finish(h):
        inverse = 1.0 / l_s[h]
        outputs = a_s[h] * inverse
        d_outputs = g_s[h] * inverse - (c_s[h] * inverse) * outputs
        ao[h, 0, 0:rows] = outputs.astype(BF16)
        ao[h, 0, rows : 2 * rows] = d_outputs.astype(BF16)
        for j in list(range(2, n_mp, 2)) + [1]:
            ao_copy(h, j).start()

    def relay(h):
        for j in range(2, n_mp, 2):
            ao_copy(h, j).wait_recv()
            ao_copy(h, j + 1).start()

    for h in range(heads):
        attend(
            h, own[0, :, lanes(h)], tkv[h, 0], lambda: (own[1, :, lanes(h)], tkv[h, 1]), True
        )
    for s in range(1, half):
        for h in range(heads):
            for p in range(4):
                for d in (0, 1):
                    kv_copy(h, d, s, p).wait_recv()
                    if exists(d, s + 1, p):
                        kv_copy(h, d, s + 1, p).start()
            attend(
                h,
                kv[h, s - 1, 0],
                kv[h, s - 1, 2],
                lambda: (kv[h, s - 1, 1], kv[h, s - 1, 3]),
                False,
            )
    for h in range(heads):
        def opposite(first_p, second_p):
            kv_copy(h, 0, half, first_p).wait_recv()
            kv_copy(h, 1, half, second_p).wait_recv()
            return opp[h, first_p], opp[h, second_p]

        keys, d_keys = opposite(0, 2)
        attend(h, keys, d_keys, lambda: opposite(1, 3), False)
        finish(h)

    step = 2 * HD if cols % (2 * HD) == 0 else cols
    chunks = [slice(c, c + step) for c in range(0, cols, step)]

    def w_part(h, j, chunk):
        part = slice(h * HD, (h + 1) * HD)
        if move_w:
            return wbuf[j, part, chunk]
        return w_hbm[peers[j], part, chunk]

    def project(slots, chunk):
        attn = jnp.concatenate([ao[h, j] for h, j in slots], axis=1)
        weight = jnp.concatenate([w_part(h, j, chunk) for h, j in slots], axis=0)
        return dot_nn(attn, weight)

    if move_w:
        for h in range(heads):
            w_copy(h, 0).wait()
            for j in range(1, n_mp):
                w_copy(h, j).wait_recv()
    for load in x_loads:
        load.wait()
    last = heads - 1
    for h in range(heads):
        ao_copy(h, 1).wait_recv()
    near = [(h, j) for h in range(heads) for j in (0, 1)]
    for chunk in chunks:
        acc[:, chunk] = project(near, chunk)
    for h in range(last):
        relay(h)
    for h in range(last):
        for j in range(3, n_mp, 2):
            ao_copy(h, j).wait_recv()
    far = [(h, j) for h in range(last) for j in range(2, n_mp)]
    for chunk in chunks:
        acc[:, chunk] += project(far, chunk)
    for h in range(heads):
        for s in range(1, half + 1):
            for p in range(4):
                for d in (0, 1):
                    if exists(d, s, p):
                        kv_copy(h, d, s, p).wait_send()
        if move_w:
            for j in range(1, n_mp):
                w_copy(h, j).wait_send()
    relay(last)
    even = [(last, j) for j in range(2, n_mp, 2)]
    for chunk in chunks:
        acc[:, chunk] += project(even, chunk)
    for j in range(3, n_mp, 2):
        ao_copy(last, j).wait_recv()
    odd = [(last, j) for j in range(3, n_mp, 2)]
    for chunk in chunks:
        part = acc[:, chunk] + project(odd, chunk)
        scale = gate[chunk].reshape(1, step)
        out[:, chunk] = (xbuf[0, :, chunk].astype(F32) + scale * part[0:rows]).astype(BF16)
        for i in range(rows // FRAME):
            piece = slice(i * FRAME, (i + 1) * FRAME)
            base = xbuf[1, piece, chunk].astype(F32)
            base = base * jnp.full(base.shape, live[i], F32)
            delta = part[rows + i * FRAME : rows + (i + 1) * FRAME]
            d_out[piece, chunk] = (base + scale * delta).astype(BF16)

    for h in range(heads):
        for j in range(1, n_mp):
            ao_copy(h, j).wait_send()


def per_device(n, n_mp, q, dq, k, v, dk, dv, flags, w, gate, x, dx):
    rows, width = q.shape
    cols = x.shape[1]
    heads = width // HD
    half = n // 2
    move_w = cols % HD == 0
    if not move_w:
        w = lax.all_to_all(w, "mp", split_axis=1, concat_axis=0, tiled=True)
        w = w.reshape(n_mp, width, cols)
    anywhere = pl.BlockSpec(memory_space=pl.ANY)
    vmem = pl.BlockSpec(memory_space=pltpu.VMEM)
    dma = pltpu.SemaphoreType.DMA
    return pl.pallas_call(
        functools.partial(fused, n, n_mp, move_w),
        out_shape=(pltpu.VMEM(x.shape, BF16), pltpu.VMEM(x.shape, BF16)),
        in_specs=[anywhere] * 6
        + [anywhere, anywhere if move_w else vmem, anywhere]
        + [anywhere] * 2,
        out_specs=(vmem, vmem),
        scratch_shapes=[
            pltpu.VMEM((6, rows, width), BF16),
            pltpu.VMEM((heads, rows, 2 * HD), BF16),
            pltpu.VMEM((heads, 2, rows, HD), BF16),
            pltpu.VMEM((heads, half - 1, 4, 2 * rows, HD), BF16),
            pltpu.VMEM((heads, 4, rows, HD), BF16),
            pltpu.VMEM((heads, rows, 1), F32),
            pltpu.VMEM((heads, rows, 1), F32),
            pltpu.VMEM((heads, rows, 1), F32),
            pltpu.VMEM((heads, rows, HD), F32),
            pltpu.VMEM((heads, rows, HD), F32),
            pltpu.VMEM((heads, n_mp, 2 * rows, HD), BF16),
            pltpu.VMEM((n_mp, width, cols) if move_w else (1, 16, HD), BF16),
            pltpu.VMEM((2 * rows, cols), F32),
            pltpu.VMEM((2, rows, cols), BF16),
            pltpu.SMEM((rows,), jnp.int32),
            pltpu.VMEM((cols,), F32),
            dma((6,)),
            dma((2,)),
            dma((2,)),
            dma((heads,)),
            dma((heads, 2, half, 4)),
            dma((heads, 2, half, 4)),
            dma((heads, n_mp)),
            dma((heads, n_mp)),
            dma((heads, n_mp)),
            dma((heads, n_mp)),
        ],
        compiler_params=pltpu.CompilerParams(
            collective_id=0, has_side_effects=True, vmem_limit_bytes=65000000
        ),
    )(q, dq, k, v, dk, dv, flags, w, gate, x, dx)


def gathered(
    n,
    n_mp,
    q_hbm,
    dq_hbm,
    k_hbm,
    v_hbm,
    dk_hbm,
    dv_hbm,
    flags_hbm,
    w_hbm,
    gate_hbm,
    x_hbm,
    dx_hbm,
    out,
    d_out,
    own,
    qpack,
    pack,
    qpeer,
    peer,
    qcat,
    kv,
    m_s,
    l_s,
    c_s,
    a_s,
    g_s,
    res,
    ao,
    wbuf,
    acc,
    xbuf,
    flags,
    gate,
    own_sem,
    raw_sem,
    x_sem,
    small_sem,
    w_local,
    qr,
    ks,
    kr,
    ps,
    pr,
    ts,
    fs,
    wts,
    wtr,
    wxs,
    wxr,
    wys,
    wyr,
    rs,
    rr,
    as_,
    ar,
):
    rows, width = q_hbm.shape
    heads = width // HD
    cols = out.shape[1]
    t = lax.axis_index("tm")
    m = lax.axis_index("mp")
    z, y = t // 2, t % 2
    plane, core = m // 2, m % 2
    side = z // 2
    role = jnp.where(side == 0, 1 - z % 2, z % 2)
    home = role == 0
    straight = y == core
    itself = jnp.logical_and(home, straight)

    def chip(side_, role_):
        return 2 * side_ + jnp.where(side_ == 0, 1 - role_, role_)

    order = (side, 1 - side)
    homes = [(2 * chip(h, 0) + core, 2 * plane + y) for h in order]
    sources = [
        (2 * chip((side + g // 2) % 2, g % 2) + core, 2 * plane + y) for g in range(4)
    ]
    twin = (t, 2 * plane + 1 - core)
    across = (t, 2 * (1 - plane) + core)
    diagonal = (t, 2 * (1 - plane) + 1 - core)
    row_peer = (2 * z + 1 - y, m)
    factor = 1.0 / math.sqrt(HD)

    def lanes(h):
        return slice(h * HD, (h + 1) * HD)

    def both(flag, yes, no):
        pl.when(flag)(yes)
        pl.when(jnp.logical_not(flag))(no)

    def unless(flag, no):
        pl.when(jnp.logical_not(flag))(no)

    barrier = pltpu.get_barrier_semaphore()

    def greet(dev):
        pl.semaphore_signal(barrier, inc=1, device_id=dev, device_id_type=MESH)

    greet(homes[1])
    unless(itself, lambda: greet(homes[0]))

    @pl.when(home)
    def _():
        for i in (3, 2, 1):
            greet(sources[i])
        unless(itself, lambda: greet(sources[0]))

    @pl.when(straight)
    def _():
        for h in order:
            greet((2 * chip(h, 0) + y, 2 * plane + 1 - y))

    @pl.when(jnp.logical_and(home, jnp.logical_not(straight)))
    def _():
        for g in range(4):
            greet((2 * chip((side + g // 2) % 2, g % 2) + y, 2 * plane + y))

    for dev in (across, diagonal, row_peer, twin):
        greet(dev)

    loads = [
        pltpu.make_async_copy(src, own.at[i], own_sem.at[i])
        for i, src in enumerate((dq_hbm, dk_hbm, dv_hbm))
    ]
    loads.append(pltpu.make_async_copy(flags_hbm, flags, small_sem.at[0]))
    raw = []
    for j in range(heads):
        for i, (src, dst) in enumerate(
            (
                (q_hbm, qpack.at[j, :, HD : 2 * HD]),
                (k_hbm, pack.at[j, 0]),
                (v_hbm, pack.at[j, 2]),
            )
        ):
            raw.append(
                pltpu.make_async_copy(src.at[:, lanes(j)], dst, raw_sem.at[j, i])
            )
    for load in loads + raw:
        load.start()
    for load in loads:
        load.wait()

    live = [
        jnp.where(flags[i * FRAME] > 0, 1.0, 0.0).astype(F32)
        for i in range(rows // FRAME)
    ]

    def masked(value, i):
        scale = jnp.full(value.shape, live[i], F32)
        return (value.astype(F32) * scale).astype(BF16)

    for h in range(heads):
        for i in range(rows // FRAME):
            piece = slice(i * FRAME, (i + 1) * FRAME)
            qpack[h, piece, 0:HD] = masked(own[0, piece, lanes(h)], i)
            pack[h, 1, piece] = masked(own[1, piece, lanes(h)], i)
            pack[h, 3, piece] = masked(own[2, piece, lanes(h)], i)
    for load in raw:
        load.wait()

    pl.semaphore_wait(
        barrier,
        4 + heads + 4 * home.astype(jnp.int32) - 2 * itself.astype(jnp.int32)
        + 2 * straight.astype(jnp.int32)
        + 4 * (home.astype(jnp.int32) - itself.astype(jnp.int32)),
    )

    def remote(ends, send_sem, dev):
        src, dst, sem = ends
        return pltpu.make_async_remote_copy(
            src_ref=src,
            dst_ref=dst,
            send_sem=send_sem,
            recv_sem=sem,
            device_id=dev,
            device_id_type=MESH,
        )

    def home_ends(o, piece, relayed=False):
        h = order[o]
        g = 2 * o + role
        if piece == 0:
            return (qpeer.at[o] if relayed else qpack.at[h]), qcat.at[g], qr.at[g]
        pair = slice(2 * piece - 2, 2 * piece)
        crossing = 1 if relayed else (y + core) % 2
        slot = g + 4 * crossing
        src = peer.at[o, pair] if relayed else pack.at[h, pair]
        return src, kv.at[pair, slot], kr.at[piece - 1, slot]

    def home_copy(o, piece):
        return remote(home_ends(o, piece), ks.at[o, piece], homes[o])

    def home_all(o):
        for piece in range(3):
            home_copy(o, piece).start()

    def home_local():
        for piece in range(3):
            pltpu.make_async_copy(*home_ends(0, piece)).start()

    def peer_copy(o, piece):
        h = order[o]
        if piece == 0:
            ends = (qpack.at[h], qpeer.at[o], pr.at[o, piece])
        else:
            pair = slice(2 * piece - 2, 2 * piece)
            ends = (pack.at[h, pair], peer.at[o, pair], pr.at[o, piece])
        return remote(ends, ps.at[o, piece], row_peer)

    def peer_all(o):
        for piece in range(3):
            peer_copy(o, piece).start()

    def onward(o, piece):
        dev = (2 * chip(order[o], 0) + y, 2 * plane + 1 - y)
        return remote(home_ends(o, piece, True), ts.at[o, piece], dev)

    def relay(o):
        for piece in range(3):
            peer_copy(o, piece).wait_recv()
            onward(o, piece).start()

    def straight_sends():
        both(itself, home_local, lambda: home_all(0))
        home_all(1)

    def crossing_sends():
        def middle():
            peer_all(1)
            home_all(0)

        def end():
            peer_all(0)
            peer_all(1)

        both(home, middle, end)

    both(straight, straight_sends, crossing_sends)

    tile = 16
    y_rows = (width // tile * 5 // 16) * tile
    rest = slice(2 * y_rows, width)
    halves = 2 if cols % (2 * HD) == 0 else 1
    span = cols // halves

    def y_part(index):
        return pl.ds(pl.multiple_of(index * y_rows, tile), y_rows)

    def w_cols(owner, first, size):
        return pl.ds(pl.multiple_of(owner * cols + first, HD), size)

    def w_cross(slot, piece):
        dev = across if slot == 0 else diagonal
        if piece < halves:
            rows_ = y_part(y)
            first, size = piece * span, span
        else:
            rows_ = rest
            first, size = (piece - halves) * span, span
        return remote(
            (
                w_hbm.at[rows_, w_cols(dev[1], first, size)],
                wbuf.at[2 + slot, rows_, pl.ds(first, size)],
                wxr.at[slot, piece],
            ),
            wxs.at[slot, piece],
            dev,
        )

    def w_row(slot, piece):
        ref = wbuf.at[2 + slot, y_part(y), pl.ds(piece * span, span)]
        return remote((ref, ref, wyr.at[slot, piece]), wys.at[slot, piece], row_peer)

    def w_row_relay(piece):
        for slot in range(2):
            w_cross(slot, piece).wait_recv()
            w_row(slot, piece).start()

    w_twin = remote(
        (w_hbm.at[:, w_cols(twin[1], 0, cols)], wbuf.at[1], wtr), wts, twin
    )
    w_own = pltpu.make_async_copy(w_hbm.at[:, w_cols(m, 0, cols)], wbuf.at[0], w_local)

    for piece in range(2 * halves):
        for slot in range(2):
            w_cross(slot, piece).start()
    w_twin.start()
    w_own.start()
    x_loads = [
        pltpu.make_async_copy(src, xbuf.at[i], x_sem.at[i])
        for i, src in enumerate((x_hbm, dx_hbm))
    ]
    x_loads.append(pltpu.make_async_copy(gate_hbm, gate, small_sem.at[1]))
    for load in x_loads:
        load.start()

    mine_at = 4 * ((y + core) % 2)
    twins_at = 4 - mine_at

    def to_twin(pair, g):
        ref = kv.at[2 * pair : 2 * pair + 2, g + mine_at]
        return remote((ref, ref, kr.at[pair, g + mine_at]), fs.at[pair, g], twin)

    def kv_wait(pair, slot):
        ref = kv.at[2 * pair : 2 * pair + 2, slot]
        pltpu.make_async_copy(ref, ref, kr.at[pair, slot]).wait()

    def arrive(g):
        for pair in range(2):
            kv_wait(pair, g + mine_at)
            to_twin(pair, g).start()

    def from_twin(g):
        for pair in range(2):
            kv_wait(pair, g + twins_at)

    def q_wait(i):
        pltpu.make_async_copy(qcat.at[i], qcat.at[i], qr.at[i]).wait()

    def attend(blocks, i):
        first = blocks[0] == 0
        last = blocks[1] == 8
        keys = (blocks[1] - blocks[0]) * rows
        k, tk, v, tv = (
            kv[p, blocks[0] : blocks[1]].reshape(keys, HD) for p in range(4)
        )
        scores = dot_nt(qcat[i, :, HD : 2 * HD], k)
        d_scores = dot_nt(qcat[i], jnp.concatenate([k, tk], axis=1)) * factor
        peak = jnp.max(scores, axis=1, keepdims=True)
        if not first:
            peak_old = m_s[i]
            peak = jnp.maximum(peak_old, peak)
            rescale = jnp.exp((peak_old - peak) * factor)
        weights = jnp.exp((scores - peak) * factor)
        product = weights * d_scores
        total = jnp.sum(weights, axis=1, keepdims=True)
        slope = jnp.sum(product, axis=1, keepdims=True)
        weights_b = weights.astype(BF16)
        product_b = product.astype(BF16)
        wide = dot_nn(weights_b, jnp.concatenate([v, tv], axis=1))
        primal = wide[:, 0:HD]
        tangent = dot_nn(product_b, v) + wide[:, HD : 2 * HD]
        if not first:
            total = l_s[i] * rescale + total
            slope = c_s[i] * rescale + slope
            primal = a_s[i] * rescale + primal
            tangent = g_s[i] * rescale + tangent
        if last:
            inverse = 1.0 / total
            outputs = primal * inverse
            d_outputs = tangent * inverse - (slope * inverse) * outputs
            res[i, 0] = outputs.astype(BF16)
            res[i, 1] = d_outputs.astype(BF16)
        else:
            m_s[i] = peak
            l_s[i] = total
            c_s[i] = slope
            a_s[i] = primal
            g_s[i] = tangent

    def res_ends(i, a):
        return res.at[i, a], ao.at[side, 0, a], rr.at[side, a]

    def res_remote(i, a):
        return remote(res_ends(i, a), rs.at[i, a], sources[i])

    def res_start(i):
        def local():
            for a in range(2):
                pltpu.make_async_copy(*res_ends(i, a)).start()

        def away():
            for a in range(2):
                res_remote(i, a).start()

        if i == 0:
            both(itself, local, away)
        else:
            away()

    @pl.when(home)
    def _():
        def early_straight():
            relay(1)
            for g in range(4):
                arrive(g)
            from_twin(0)

        def early_crossing():
            arrive(0)
            for g in range(4):
                from_twin(g)

        def late_straight():
            for g in range(1, 4):
                from_twin(g)

        def late_crossing():
            for g in range(1, 4):
                arrive(g)

        both(straight, early_straight, early_crossing)
        q_wait(0)
        attend((0, 5), 0)
        w_row_relay(0)
        for g in range(1, 4):
            q_wait(g)
            attend((0, 5), g)
        for piece in range(1, halves):
            w_row_relay(piece)
        both(straight, late_straight, late_crossing)
        for i in (3, 2, 1, 0):
            attend((5, 8), i)
            res_start(i)

    @pl.when(jnp.logical_not(home))
    def _():
        @pl.when(straight)
        def _():
            relay(0)
            relay(1)

        for piece in range(halves):
            w_row_relay(piece)

    def ao_copy(h, j, a):
        src = ao.at[h, 2 if j == 3 else 0, a]
        dst = ao.at[h, j, a]
        dev = across if j == 2 else twin
        return remote((src, dst, ar.at[h, j, a]), as_.at[h, j, a], dev)

    def own_heads(h, a):
        ref = ao.at[h, 0, a]
        pltpu.make_async_copy(ref, ref, rr.at[h, a]).wait()
        ao_copy(h, 2, a).start()
        ao_copy(h, 1, a).start()

    def cross_heads(h, a):
        ao_copy(h, 2, a).wait_recv()
        ao_copy(h, 3, a).start()

    step = 2 * HD if cols % (2 * HD) == 0 else cols
    chunks = [slice(c, c + step) for c in range(0, cols, step)]

    def project(slots, a, chunk):
        attn = jnp.concatenate([ao[heads_[h], j, a] for h, j in slots], axis=1)
        weight = jnp.concatenate([wbuf[j, w_rows[h], chunk] for h, j in slots], axis=0)
        return dot_nn(attn, weight)

    heads_ = (side, 1 - side)
    w_rows = [pl.ds(pl.multiple_of(h * HD, HD), HD) for h in heads_]
    near, far = heads_

    def own_plane(a):
        for h in heads_:
            ao_copy(h, 1, a).wait_recv()
        for chunk in chunks:
            acc[a, :, chunk] = project([(0, 0), (0, 1), (1, 0), (1, 1)], a, chunk)

    def other_plane(a, result):
        for h in heads_:
            ao_copy(h, 3, a).wait_recv()
        slots = [(0, 2), (0, 3), (1, 2), (1, 3)]
        for chunk in chunks:
            total = acc[a, :, chunk] + project(slots, a, chunk)
            scale = gate[chunk].reshape(1, step)
            base = xbuf[a, :, chunk].astype(F32)
            result[:, chunk] = (base + scale * total).astype(BF16)

    w_own.wait()
    w_twin.wait_recv()
    for load in x_loads:
        load.wait()
    for i in range(rows // FRAME):
        piece = slice(i * FRAME, (i + 1) * FRAME)
        xbuf[1, piece] = masked(xbuf[1, piece], i)
    for h in heads_:
        own_heads(h, 0)
    own_plane(0)
    for h in heads_:
        own_heads(h, 1)
    for slot in range(2):
        for piece in range(halves, 2 * halves):
            w_cross(slot, piece).wait_recv()
        for piece in range(halves):
            w_row(slot, piece).wait_recv()
    for h in heads_:
        cross_heads(h, 0)
    own_plane(1)
    for h in heads_:
        cross_heads(h, 1)
    other_plane(0, out)
    other_plane(1, d_out)

    def sent(o):
        for piece in range(3):
            home_copy(o, piece).wait_send()

    def peers_sent(o):
        for piece in range(3):
            peer_copy(o, piece).wait_send()

    def relays_sent(o):
        for piece in range(3):
            onward(o, piece).wait_send()

    def straight_sent():
        sent(1)
        unless(itself, lambda: sent(0))
        relays_sent(1)
        unless(home, lambda: relays_sent(0))

    def crossing_sent():
        peers_sent(1)
        both(home, lambda: sent(0), lambda: peers_sent(0))

    both(straight, straight_sent, crossing_sent)
    for slot in range(2):
        for piece in range(2 * halves):
            w_cross(slot, piece).wait_send()
        for piece in range(halves):
            w_row(slot, piece).wait_send()
    w_twin.wait_send()

    @pl.when(home)
    def _():
        for g in range(4):
            for pair in range(2):
                to_twin(pair, g).wait_send()
        for i in range(1, 4):
            for a in range(2):
                res_remote(i, a).wait_send()

        @pl.when(jnp.logical_not(itself))
        def _():
            for a in range(2):
                res_remote(0, a).wait_send()

    for h in range(heads):
        for j in range(1, n_mp):
            for a in range(2):
                ao_copy(h, j, a).wait_send()


def gathered_call(n, n_mp, q, dq, k, v, dk, dv, flags, w, gate, x, dx):
    rows, width = q.shape
    cols = x.shape[1]
    heads = width // HD
    halves = 2 if cols % (2 * HD) == 0 else 1
    anywhere = pl.BlockSpec(memory_space=pl.ANY)
    vmem = pl.BlockSpec(memory_space=pltpu.VMEM)
    dma = pltpu.SemaphoreType.DMA
    return pl.pallas_call(
        functools.partial(gathered, n, n_mp),
        out_shape=(pltpu.VMEM(x.shape, BF16), pltpu.VMEM(x.shape, BF16)),
        in_specs=[anywhere] * 11,
        out_specs=(vmem, vmem),
        scratch_shapes=[
            pltpu.VMEM((3, rows, width), BF16),
            pltpu.VMEM((heads, rows, 2 * HD), BF16),
            pltpu.VMEM((heads, 4, rows, HD), BF16),
            pltpu.VMEM((heads, rows, 2 * HD), BF16),
            pltpu.VMEM((heads, 4, rows, HD), BF16),
            pltpu.VMEM((4, rows, 2 * HD), BF16),
            pltpu.VMEM((4, 8, rows, HD), BF16),
            pltpu.VMEM((4, rows, 1), F32),
            pltpu.VMEM((4, rows, 1), F32),
            pltpu.VMEM((4, rows, 1), F32),
            pltpu.VMEM((4, rows, HD), F32),
            pltpu.VMEM((4, rows, HD), F32),
            pltpu.VMEM((4, 2, rows, HD), BF16),
            pltpu.VMEM((heads, n_mp, 2, rows, HD), BF16),
            pltpu.VMEM((n_mp, width, cols), BF16),
            pltpu.VMEM((2, rows, cols), F32),
            pltpu.VMEM((2, rows, cols), BF16),
            pltpu.SMEM((rows,), jnp.int32),
            pltpu.VMEM((cols,), F32),
            dma((3,)),
            dma((heads, 3)),
            dma((2,)),
            dma((2,)),
            dma,
            dma((4,)),
            dma((heads, 3)),
            dma((2, 8)),
            dma((heads, 3)),
            dma((heads, 3)),
            dma((heads, 3)),
            dma((2, 4)),
            dma,
            dma,
            dma((2, 2 * halves)),
            dma((2, 2 * halves)),
            dma((2, halves)),
            dma((2, halves)),
            dma((4, 2)),
            dma((heads, 2)),
            dma((heads, n_mp, 2)),
            dma((heads, n_mp, 2)),
        ],
        compiler_params=pltpu.CompilerParams(
            collective_id=0, has_side_effects=True, vmem_limit_bytes=65000000
        ),
    )(q, dq, k, v, dk, dv, flags, w, gate, x, dx)


def gathers(n, n_mp, q, x):
    heads = q.shape[1] // HD
    return (
        n_mp == 4
        and n == 8
        and heads == 2
        and x.shape[1] % HD == 0
        and q.shape[0] % FRAME == 0
    )


def program(n, n_mp, q, dq, k, v, dk, dv, flags, w, gate, x, dx):
    call = gathered_call if gathers(n, n_mp, q, x) else per_device
    return call(n, n_mp, q, dq, k, v, dk, dv, flags, w, gate, x, dx)


def solution(mesh):
    both = P("tm", "mp")
    placed = (both,) * 6 + (P("tm"), P("mp", None), P("mp"), both, both)
    return jax.shard_map(
        functools.partial(program, mesh.shape["tm"], mesh.shape["mp"]),
        mesh=mesh,
        in_specs=placed,
        out_specs=(both, both),
        check_vma=False,
    )
```

```python
import functools
import math

import jax
import jax.numpy as jnp
from jax import lax
from jax.experimental import pallas as pl
from jax.experimental.pallas import tpu as pltpu
from jax.sharding import PartitionSpec as P

HD = 128
FRAME = 32
MESH = pl.DeviceIdType.MESH
F32 = jnp.float32
BF16 = jnp.bfloat16


def ring_place(t, n):
    return jnp.where(t % 2 == 0, t // 2, n - 1 - t // 2)


def ring_member(r, n):
    return jnp.where(r < n // 2, 2 * r, 2 * (n - 1 - r) + 1)


def flipped(me, j):
    other = me
    bit = 1
    while bit <= j:
        if j & bit:
            other = other + bit * (1 - 2 * ((me // bit) % 2))
        bit *= 2
    return other


def dot_nt(a, b):
    return lax.dot_general(a, b, (((1,), (1,)), ((), ())), preferred_element_type=F32)


def dot_nn(a, b):
    return lax.dot_general(a, b, (((1,), (0,)), ((), ())), preferred_element_type=F32)


def fused(
    n,
    n_mp,
    move_w,
    q_hbm,
    dq_hbm,
    k_hbm,
    v_hbm,
    dk_hbm,
    dv_hbm,
    flags_hbm,
    w_hbm,
    gate_hbm,
    x_hbm,
    dx_hbm,
    out,
    d_out,
    own,
    qcat,
    tkv,
    kv,
    opp,
    m_s,
    l_s,
    c_s,
    a_s,
    g_s,
    ao,
    wbuf,
    acc,
    xbuf,
    flags,
    gate,
    own_sem,
    x_sem,
    small_sem,
    w_local,
    ks,
    kr,
    ws,
    wr,
    as_,
    ar,
):
    rows, width = q_hbm.shape
    heads = width // HD
    cols = out.shape[1]
    half = n // 2
    t = lax.axis_index("tm")
    m = lax.axis_index("mp")
    place = ring_place(t, n)
    right = ring_member((place + 1) % n, n)
    left = ring_member((place + n - 1) % n, n)
    peers = [flipped(m, j) for j in range(n_mp)]
    factor = 1.0 / math.sqrt(HD)

    def lanes(h):
        return slice(h * HD, (h + 1) * HD)

    loads = [
        pltpu.make_async_copy(src, own.at[i], own_sem.at[i])
        for i, src in enumerate((k_hbm, v_hbm, dk_hbm, dv_hbm, q_hbm, dq_hbm))
    ]
    loads.append(pltpu.make_async_copy(flags_hbm, flags, small_sem.at[0]))
    for load in loads:
        load.start()

    barrier = pltpu.get_barrier_semaphore()
    for dev in [(right, m), (left, m)] + [(t, peers[j]) for j in range(1, n_mp)]:
        pl.semaphore_signal(barrier, inc=1, device_id=dev, device_id_type=MESH)
    pl.semaphore_wait(barrier, 1 + n_mp)

    def exists(d, s, p):
        return s < half or (s == half and (p < 2) == (d == 0))

    def kv_copy(h, d, s, p):
        side = slice(d * rows, (d + 1) * rows)
        if s > 1:
            src = kv.at[h, s - 2, p, side]
        elif p < 2:
            src = (k_hbm, v_hbm)[p].at[:, lanes(h)]
        else:
            src = tkv.at[h, p - 2]
        dst = kv.at[h, s - 1, p, side] if s < half else opp.at[h, p]
        return pltpu.make_async_remote_copy(
            src_ref=src,
            dst_ref=dst,
            send_sem=ks.at[h, d, s - 1, p],
            recv_sem=kr.at[h, d, s - 1, p],
            device_id=((right, left)[d], m),
            device_id_type=MESH,
        )

    def send_own(h, pieces):
        for p in pieces:
            for d in (0, 1):
                kv_copy(h, d, 1, p).start()

    def w_copy(h, j):
        span = pl.ds(pl.multiple_of(peers[j] * cols, HD), cols)
        part = slice(h * HD, (h + 1) * HD)
        if j == 0:
            return pltpu.make_async_copy(
                w_hbm.at[part, span], wbuf.at[0, part], w_local.at[h]
            )
        return pltpu.make_async_remote_copy(
            src_ref=w_hbm.at[part, span],
            dst_ref=wbuf.at[j, part],
            send_sem=ws.at[h, j],
            recv_sem=wr.at[h, j],
            device_id=(t, peers[j]),
            device_id_type=MESH,
        )

    def ao_copy(h, j):
        relay = j % 2 == 1 and j > 1
        return pltpu.make_async_remote_copy(
            src_ref=ao.at[h, j - 1 if relay else 0],
            dst_ref=ao.at[h, j],
            send_sem=as_.at[h, j],
            recv_sem=ar.at[h, j],
            device_id=(t, peers[1] if relay else peers[j]),
            device_id_type=MESH,
        )

    send_own(0, (0, 1))
    if move_w:
        for h in range(heads):
            for j in list(range(2, n_mp)) + [1, 0]:
                w_copy(h, j).start()
    x_loads = [
        pltpu.make_async_copy(src, xbuf.at[i], x_sem.at[i])
        for i, src in enumerate((x_hbm, dx_hbm))
    ]
    x_loads.append(pltpu.make_async_copy(gate_hbm, gate, small_sem.at[1]))
    for load in x_loads:
        load.start()
    for load in loads:
        load.wait()

    live = [
        jnp.where(flags[i * FRAME] > 0, 1.0, 0.0).astype(F32)
        for i in range(rows // FRAME)
    ]

    def masked(value, i):
        scale = jnp.full(value.shape, live[i], F32)
        return (value.astype(F32) * scale).astype(BF16)

    for h in range(heads):
        for i in range(rows // FRAME):
            part = slice(i * FRAME, (i + 1) * FRAME)
            tkv[h, 0, part] = masked(own[2, part, lanes(h)], i)
            tkv[h, 1, part] = masked(own[3, part, lanes(h)], i)
        if h == 0:
            send_own(0, (2, 3))
            for g in range(1, heads):
                send_own(g, (0, 1))
        else:
            send_own(h, (2, 3))
    for h in range(heads):
        for i in range(rows // FRAME):
            part = slice(i * FRAME, (i + 1) * FRAME)
            qcat[h, part, 0:HD] = masked(own[5, part, lanes(h)], i)
        qcat[h, :, HD : 2 * HD] = own[4, :, lanes(h)]

    def attend(h, k, tk, values, first):
        queries = qcat[h, :, HD : 2 * HD]
        scores = dot_nt(queries, k)
        d_scores = dot_nt(qcat[h], jnp.concatenate([k, tk], axis=1)) * factor
        peak = jnp.max(scores, axis=1, keepdims=True)
        if not first:
            peak_old = m_s[h]
            peak = jnp.maximum(peak_old, peak)
            rescale = jnp.exp((peak_old - peak) * factor)
        weights = jnp.exp((scores - peak) * factor)
        product = weights * d_scores
        total = jnp.sum(weights, axis=1, keepdims=True)
        slope = jnp.sum(product, axis=1, keepdims=True)
        weights_b = weights.astype(BF16)
        product_b = product.astype(BF16)
        v, tv = values()
        primal = dot_nn(weights_b, v)
        tangent = dot_nn(product_b, v) + dot_nn(weights_b, tv)
        m_s[h] = peak
        if first:
            l_s[h] = total
            c_s[h] = slope
            a_s[h] = primal
            g_s[h] = tangent
        else:
            l_s[h] = l_s[h] * rescale + total
            c_s[h] = c_s[h] * rescale + slope
            a_s[h] = a_s[h] * rescale + primal
            g_s[h] = g_s[h] * rescale + tangent

    def finish(h):
        inverse = 1.0 / l_s[h]
        outputs = a_s[h] * inverse
        d_outputs = g_s[h] * inverse - (c_s[h] * inverse) * outputs
        ao[h, 0, 0:rows] = outputs.astype(BF16)
        ao[h, 0, rows : 2 * rows] = d_outputs.astype(BF16)
        for j in list(range(2, n_mp, 2)) + [1]:
            ao_copy(h, j).start()

    def relay(h):
        for j in range(2, n_mp, 2):
            ao_copy(h, j).wait_recv()
            ao_copy(h, j + 1).start()

    for h in range(heads):
        attend(
            h, own[0, :, lanes(h)], tkv[h, 0], lambda: (own[1, :, lanes(h)], tkv[h, 1]), True
        )
    for s in range(1, half):
        for h in range(heads):
            for p in range(4):
                for d in (0, 1):
                    kv_copy(h, d, s, p).wait_recv()
                    if exists(d, s + 1, p):
                        kv_copy(h, d, s + 1, p).start()
            attend(
                h,
                kv[h, s - 1, 0],
                kv[h, s - 1, 2],
                lambda: (kv[h, s - 1, 1], kv[h, s - 1, 3]),
                False,
            )
    for h in range(heads):
        def opposite(first_p, second_p):
            kv_copy(h, 0, half, first_p).wait_recv()
            kv_copy(h, 1, half, second_p).wait_recv()
            return opp[h, first_p], opp[h, second_p]

        keys, d_keys = opposite(0, 2)
        attend(h, keys, d_keys, lambda: opposite(1, 3), False)
        finish(h)

    step = 2 * HD if cols % (2 * HD) == 0 else cols
    chunks = [slice(c, c + step) for c in range(0, cols, step)]

    def w_part(h, j, chunk):
        part = slice(h * HD, (h + 1) * HD)
        if move_w:
            return wbuf[j, part, chunk]
        return w_hbm[peers[j], part, chunk]

    def project(slots, chunk):
        attn = jnp.concatenate([ao[h, j] for h, j in slots], axis=1)
        weight = jnp.concatenate([w_part(h, j, chunk) for h, j in slots], axis=0)
        return dot_nn(attn, weight)

    if move_w:
        for h in range(heads):
            w_copy(h, 0).wait()
            for j in range(1, n_mp):
                w_copy(h, j).wait_recv()
    for load in x_loads:
        load.wait()
    last = heads - 1
    for h in range(heads):
        ao_copy(h, 1).wait_recv()
    near = [(h, j) for h in range(heads) for j in (0, 1)]
    for chunk in chunks:
        acc[:, chunk] = project(near, chunk)
    for h in range(last):
        relay(h)
    for h in range(last):
        for j in range(3, n_mp, 2):
            ao_copy(h, j).wait_recv()
    far = [(h, j) for h in range(last) for j in range(2, n_mp)]
    for chunk in chunks:
        acc[:, chunk] += project(far, chunk)
    for h in range(heads):
        for s in range(1, half + 1):
            for p in range(4):
                for d in (0, 1):
                    if exists(d, s, p):
                        kv_copy(h, d, s, p).wait_send()
        if move_w:
            for j in range(1, n_mp):
                w_copy(h, j).wait_send()
    relay(last)
    even = [(last, j) for j in range(2, n_mp, 2)]
    for chunk in chunks:
        acc[:, chunk] += project(even, chunk)
    for j in range(3, n_mp, 2):
        ao_copy(last, j).wait_recv()
    odd = [(last, j) for j in range(3, n_mp, 2)]
    for chunk in chunks:
        part = acc[:, chunk] + project(odd, chunk)
        scale = gate[chunk].reshape(1, step)
        out[:, chunk] = (xbuf[0, :, chunk].astype(F32) + scale * part[0:rows]).astype(BF16)
        for i in range(rows // FRAME):
            piece = slice(i * FRAME, (i + 1) * FRAME)
            base = xbuf[1, piece, chunk].astype(F32)
            base = base * jnp.full(base.shape, live[i], F32)
            delta = part[rows + i * FRAME : rows + (i + 1) * FRAME]
            d_out[piece, chunk] = (base + scale * delta).astype(BF16)

    for h in range(heads):
        for j in range(1, n_mp):
            ao_copy(h, j).wait_send()


def per_device(n, n_mp, q, dq, k, v, dk, dv, flags, w, gate, x, dx):
    rows, width = q.shape
    cols = x.shape[1]
    heads = width // HD
    half = n // 2
    move_w = cols % HD == 0
    if not move_w:
        w = lax.all_to_all(w, "mp", split_axis=1, concat_axis=0, tiled=True)
        w = w.reshape(n_mp, width, cols)
    anywhere = pl.BlockSpec(memory_space=pl.ANY)
    vmem = pl.BlockSpec(memory_space=pltpu.VMEM)
    dma = pltpu.SemaphoreType.DMA
    return pl.pallas_call(
        functools.partial(fused, n, n_mp, move_w),
        out_shape=(pltpu.VMEM(x.shape, BF16), pltpu.VMEM(x.shape, BF16)),
        in_specs=[anywhere] * 6
        + [anywhere, anywhere if move_w else vmem, anywhere]
        + [anywhere] * 2,
        out_specs=(vmem, vmem),
        scratch_shapes=[
            pltpu.VMEM((6, rows, width), BF16),
            pltpu.VMEM((heads, rows, 2 * HD), BF16),
            pltpu.VMEM((heads, 2, rows, HD), BF16),
            pltpu.VMEM((heads, half - 1, 4, 2 * rows, HD), BF16),
            pltpu.VMEM((heads, 4, rows, HD), BF16),
            pltpu.VMEM((heads, rows, 1), F32),
            pltpu.VMEM((heads, rows, 1), F32),
            pltpu.VMEM((heads, rows, 1), F32),
            pltpu.VMEM((heads, rows, HD), F32),
            pltpu.VMEM((heads, rows, HD), F32),
            pltpu.VMEM((heads, n_mp, 2 * rows, HD), BF16),
            pltpu.VMEM((n_mp, width, cols) if move_w else (1, 16, HD), BF16),
            pltpu.VMEM((2 * rows, cols), F32),
            pltpu.VMEM((2, rows, cols), BF16),
            pltpu.SMEM((rows,), jnp.int32),
            pltpu.VMEM((cols,), F32),
            dma((6,)),
            dma((2,)),
            dma((2,)),
            dma((heads,)),
            dma((heads, 2, half, 4)),
            dma((heads, 2, half, 4)),
            dma((heads, n_mp)),
            dma((heads, n_mp)),
            dma((heads, n_mp)),
            dma((heads, n_mp)),
        ],
        compiler_params=pltpu.CompilerParams(
            collective_id=0, has_side_effects=True, vmem_limit_bytes=65000000
        ),
    )(q, dq, k, v, dk, dv, flags, w, gate, x, dx)


def gathered(
    n,
    n_mp,
    q_hbm,
    dq_hbm,
    k_hbm,
    v_hbm,
    dk_hbm,
    dv_hbm,
    flags_hbm,
    w_hbm,
    gate_hbm,
    x_hbm,
    dx_hbm,
    out,
    d_out,
    own,
    qpack,
    pack,
    qpeer,
    peer,
    qcat,
    kv,
    m_s,
    l_s,
    c_s,
    a_s,
    g_s,
    res,
    ao,
    wbuf,
    acc,
    xbuf,
    flags,
    gate,
    raw_sem,
    x_sem,
    small_sem,
    w_local,
    qr,
    zs,
    kr,
    pr,
    fs,
    wts,
    wtr,
    wxs,
    wxr,
    wys,
    wyr,
    rs,
    rr,
    as_,
    ar,
):
    rows, width = q_hbm.shape
    heads = width // HD
    cols = out.shape[1]
    t = lax.axis_index("tm")
    m = lax.axis_index("mp")
    z, y = t // 2, t % 2
    plane, core = m // 2, m % 2
    side = z // 2
    role = jnp.where(side == 0, 1 - z % 2, z % 2)
    home = role == 0
    straight = y == core
    itself = jnp.logical_and(home, straight)

    def chip(side_, role_):
        return 2 * side_ + jnp.where(side_ == 0, 1 - role_, role_)

    order = (side, 1 - side)
    homes = [(2 * chip(h, 0) + core, 2 * plane + y) for h in order]
    sources = [
        (2 * chip((side + g // 2) % 2, g % 2) + core, 2 * plane + y) for g in range(4)
    ]
    twin = (t, 2 * plane + 1 - core)
    across = (t, 2 * (1 - plane) + core)
    diagonal = (t, 2 * (1 - plane) + 1 - core)
    row_peer = (2 * z + 1 - y, m)
    factor = 1.0 / math.sqrt(HD)
    power = factor * math.log2(math.e)

    def lanes(h):
        return slice(h * HD, (h + 1) * HD)

    def both(flag, yes, no):
        pl.when(flag)(yes)
        pl.when(jnp.logical_not(flag))(no)

    def unless(flag, no):
        pl.when(jnp.logical_not(flag))(no)

    barrier = pltpu.get_barrier_semaphore()

    def greet(dev):
        pl.semaphore_signal(barrier, inc=1, device_id=dev, device_id_type=MESH)

    greet(homes[1])
    unless(itself, lambda: greet(homes[0]))

    @pl.when(home)
    def _():
        for i in (3, 2, 1):
            greet(sources[i])
        unless(itself, lambda: greet(sources[0]))

    @pl.when(straight)
    def _():
        for h in order:
            greet((2 * chip(h, 0) + y, 2 * plane + 1 - y))

    @pl.when(jnp.logical_and(home, jnp.logical_not(straight)))
    def _():
        for g in range(4):
            greet((2 * chip((side + g // 2) % 2, g % 2) + y, 2 * plane + y))

    for dev in (across, diagonal, row_peer, twin):
        greet(dev)

    loads = [
        pltpu.make_async_copy(src, own.at[i], raw_sem)
        for i, src in enumerate((dq_hbm, dk_hbm, dv_hbm))
    ]
    flags_load = pltpu.make_async_copy(flags_hbm, flags, small_sem.at[0])
    raw = []

    def done(ref, sem):
        pltpu.make_async_copy(ref, ref, sem).wait()

    for j in range(heads):
        for i, (src, dst) in enumerate(
            (
                (q_hbm, qpack.at[j, :, HD : 2 * HD]),
                (k_hbm, pack.at[j, 0]),
                (v_hbm, pack.at[j, 2]),
            )
        ):
            raw.append(
                pltpu.make_async_copy(src.at[:, lanes(j)], dst, raw_sem)
            )
    flags_load.start()
    for load in loads + raw:
        load.start()
    flags_load.wait()
    done(kv.at[0:4, 0:3], raw_sem)

    live = [
        jnp.where(flags[i * FRAME] > 0, 1.0, 0.0).astype(F32)
        for i in range(rows // FRAME)
    ]

    def masked(value, i):
        scale = jnp.full(value.shape, live[i], F32)
        return (value.astype(F32) * scale).astype(BF16)

    for h in range(heads):
        for i in range(rows // FRAME):
            piece = slice(i * FRAME, (i + 1) * FRAME)
            qpack[h, piece, 0:HD] = masked(own[0, piece, lanes(h)], i)
            pack[h, 1, piece] = masked(own[1, piece, lanes(h)], i)
            pack[h, 3, piece] = masked(own[2, piece, lanes(h)], i)
    pl.semaphore_wait(
        barrier,
        4 + heads + 4 * home.astype(jnp.int32) - 2 * itself.astype(jnp.int32)
        + 2 * straight.astype(jnp.int32)
        + 4 * (home.astype(jnp.int32) - itself.astype(jnp.int32)),
    )

    def remote(ends, send_sem, dev):
        src, dst, sem = ends
        return pltpu.make_async_remote_copy(
            src_ref=src,
            dst_ref=dst,
            send_sem=send_sem,
            recv_sem=sem,
            device_id=dev,
            device_id_type=MESH,
        )

    def home_ends(o, piece, relayed=False):
        h = order[o]
        g = 2 * o + role
        if piece == 0:
            return (qpeer.at[o] if relayed else qpack.at[h]), qcat.at[g], qr.at[g]
        pair = slice(2 * piece - 2, 2 * piece)
        crossing = 1 if relayed else (y + core) % 2
        slot = g + 4 * crossing
        src = peer.at[o, pair] if relayed else pack.at[h, pair]
        return src, kv.at[pair, slot], kr.at[piece - 1, slot]

    def home_copy(o, piece):
        return remote(home_ends(o, piece), zs, homes[o])

    def home_all(o):
        for piece in range(3):
            home_copy(o, piece).start()

    def home_local():
        for piece in range(3):
            pltpu.make_async_copy(*home_ends(0, piece)).start()

    def peer_copy(o, piece):
        h = order[o]
        if piece == 0:
            ends = (qpack.at[h], qpeer.at[o], pr.at[o, piece])
        else:
            pair = slice(2 * piece - 2, 2 * piece)
            ends = (pack.at[h, pair], peer.at[o, pair], pr.at[o, piece])
        return remote(ends, zs, row_peer)

    def peer_all(o):
        for piece in range(3):
            peer_copy(o, piece).start()

    def onward(o, piece):
        dev = (2 * chip(order[o], 0) + y, 2 * plane + 1 - y)
        return remote(home_ends(o, piece, True), zs, dev)

    def relay(o):
        for piece in range(3):
            peer_copy(o, piece).wait_recv()
            onward(o, piece).start()

    def straight_sends():
        both(itself, home_local, lambda: home_all(0))
        home_all(1)

    def crossing_sends():
        def middle():
            peer_all(1)
            home_all(0)

        def end():
            peer_all(0)
            peer_all(1)

        both(home, middle, end)

    both(straight, straight_sends, crossing_sends)

    tile = 16
    y_rows = (width // tile // 4) * tile
    rest = slice(2 * y_rows, width)
    halves = 2 if cols % (2 * HD) == 0 else 1
    span = cols // halves

    def y_part(index):
        return pl.ds(pl.multiple_of(index * y_rows, tile), y_rows)

    def w_cols(owner, first, size):
        return pl.ds(pl.multiple_of(owner * cols + first, HD), size)

    def w_cross(slot, piece):
        dev = across if slot == 0 else diagonal
        if piece < halves:
            rows_ = y_part(y)
            first, size = piece * span, span
        else:
            rows_ = rest
            first, size = (piece - halves) * span, span
        return remote(
            (
                w_hbm.at[rows_, w_cols(dev[1], first, size)],
                wbuf.at[2 + slot, rows_, pl.ds(first, size)],
                wxr.at[2 * piece + slot if piece < halves else 2 * halves],
            ),
            wxs,
            dev,
        )

    def w_row(slot, piece):
        ref = wbuf.at[2 + slot, y_part(y), pl.ds(piece * span, span)]
        return remote((ref, ref, wyr), wys, row_peer)

    def w_row_relay(piece):
        for slot in range(2):
            w_cross(slot, piece).wait_recv()
            w_row(slot, piece).start()

    w_twin = remote(
        (w_hbm.at[:, w_cols(twin[1], 0, cols)], wbuf.at[1], wtr), wts, twin
    )
    w_own = pltpu.make_async_copy(w_hbm.at[:, w_cols(m, 0, cols)], wbuf.at[0], w_local)

    for piece in range(2 * halves):
        for slot in range(2):
            w_cross(slot, piece).start()
    w_twin.start()
    w_own.start()
    x_loads = [
        pltpu.make_async_copy(src, xbuf.at[i], x_sem)
        for i, src in enumerate((x_hbm, dx_hbm))
    ]
    gate_load = pltpu.make_async_copy(gate_hbm, gate, small_sem.at[1])
    for load in x_loads:
        load.start()
    gate_load.start()

    mine_at = 4 * ((y + core) % 2)
    twins_at = 4 - mine_at

    def to_twin(pair, g):
        ref = kv.at[2 * pair : 2 * pair + 2, g + mine_at]
        return remote((ref, ref, kr.at[pair, g + mine_at]), fs, twin)

    def kv_wait(pair, slot):
        ref = kv.at[2 * pair : 2 * pair + 2, slot]
        pltpu.make_async_copy(ref, ref, kr.at[pair, slot]).wait()

    def arrive(g):
        for pair in range(2):
            kv_wait(pair, g + mine_at)
            to_twin(pair, g).start()

    def from_twin(g):
        for pair in range(2):
            kv_wait(pair, g + twins_at)

    def q_wait(i):
        pltpu.make_async_copy(qcat.at[i], qcat.at[i], qr.at[i]).wait()

    def attend(blocks, queries):
        first = blocks[0] == 0
        last = blocks[1] == 8
        keys = (blocks[1] - blocks[0]) * rows
        count = (queries[1] - queries[0]) * rows
        at = slice(queries[0] * rows, queries[1] * rows)

        def spread(column):
            return jnp.broadcast_to(column, (count, HD))

        k, tk, v, tv = (
            kv[p, blocks[0] : blocks[1]].reshape(keys, HD) for p in range(4)
        )
        q = qcat[queries[0] : queries[1]].reshape(count, 2 * HD)
        scores = dot_nt(q[:, HD : 2 * HD], k)
        d_scores = dot_nt(q, jnp.concatenate([k, tk], axis=1))
        peak = spread(jnp.max(scores, axis=1, keepdims=True))
        if not first:
            peak_old = m_s[at]
            peak = jnp.maximum(peak_old, peak)
            rescale = jnp.exp2((peak_old - peak) * power)
        weights = jnp.exp2((scores - jnp.tile(peak, (1, keys // HD))) * power)
        product = weights * d_scores
        total = spread(jnp.sum(weights, axis=1, keepdims=True))
        slope = spread(jnp.sum(product, axis=1, keepdims=True))
        weights_b = weights.astype(BF16)
        product_b = product.astype(BF16)
        wide = dot_nn(weights_b, jnp.concatenate([v, tv], axis=1))
        primal = wide[:, 0:HD]
        tangent = dot_nn(product_b, v) * factor + wide[:, HD : 2 * HD]
        if not first:
            total = l_s[at] * rescale + total
            slope = c_s[at] * rescale + slope
            primal = a_s[at] * rescale + primal
            tangent = g_s[at] * rescale + tangent
        if last:
            inverse = 1.0 / total
            outputs = primal * inverse
            d_outputs = tangent * inverse - (slope * (factor * inverse)) * outputs
            for i in range(*queries):
                own_rows = slice((i - queries[0]) * rows, (i - queries[0] + 1) * rows)
                res[i, 0] = outputs[own_rows].astype(BF16)
                res[i, 1] = d_outputs[own_rows].astype(BF16)
        else:
            m_s[at] = peak
            l_s[at] = total
            c_s[at] = slope
            a_s[at] = primal
            g_s[at] = tangent

    def res_ends(i, a):
        return res.at[i, a], ao.at[side, 0, a], rr.at[side, a]

    def res_remote(i, a):
        return remote(res_ends(i, a), rs, sources[i])

    def res_start(i, a):
        def local():
            pltpu.make_async_copy(*res_ends(i, a)).start()

        def away():
            res_remote(i, a).start()

        if i == 0:
            both(itself, local, away)
        else:
            away()

    @pl.when(home)
    def _():
        def nothing(g):
            pass

        def each(groups, on_straight, on_crossing):
            for g in groups:
                both(straight, lambda: on_straight(g), lambda: on_crossing(g))

        pl.when(straight)(lambda: relay(1))
        unless(straight, lambda: arrive(0))
        each(range(4), arrive, from_twin)
        q_wait(0)
        q_wait(1)
        attend((0, 4), (0, 2))
        w_row_relay(0)
        each((1,), nothing, arrive)
        q_wait(2)
        q_wait(3)
        attend((0, 4), (2, 4))
        for piece in range(1, halves):
            w_row_relay(piece)
        each((0, 1), from_twin, nothing)
        each((2,), nothing, arrive)
        attend((4, 6), (0, 4))
        each((2,), from_twin, nothing)
        each((3,), from_twin, arrive)
        for queries in ((2, 4), (0, 2)):
            attend((6, 8), queries)
            for a in range(2):
                for i in range(queries[1] - 1, queries[0] - 1, -1):
                    res_start(i, a)

    @pl.when(jnp.logical_not(home))
    def _():
        @pl.when(straight)
        def _():
            relay(0)
            relay(1)

        for piece in range(halves):
            w_row_relay(piece)

    def ao_copy(h, j, a):
        src = ao.at[h, 2 if j == 3 else 0, a]
        dst = ao.at[h, j, a]
        dev = across if j == 2 else twin
        at = 4 * a + (2 + h if j == 2 else j // 2)
        return remote((src, dst, ar.at[at]), as_, dev)

    def own_heads(h, a):
        ref = ao.at[h, 0, a]
        pltpu.make_async_copy(ref, ref, rr.at[h, a]).wait()
        ao_copy(h, 2, a).start()
        ao_copy(h, 1, a).start()

    def cross_heads(h, a):
        ao_copy(h, 2, a).wait_recv()
        ao_copy(h, 3, a).start()

    step = 2 * HD if cols % (2 * HD) == 0 else cols
    chunks = [slice(c, c + step) for c in range(0, cols, step)]

    def project(slots, a, chunk):
        attn = jnp.concatenate([ao[heads_[h], j, a] for h, j in slots], axis=1)
        weight = jnp.concatenate([wbuf[j, w_rows[h], chunk] for h, j in slots], axis=0)
        return dot_nn(attn, weight)

    heads_ = (side, 1 - side)
    w_rows = [pl.ds(pl.multiple_of(h * HD, HD), HD) for h in heads_]
    near, far = heads_

    def own_plane(a):
        done(ao.at[:, 1, a], ar.at[4 * a])
        for chunk in chunks:
            acc[a, :, chunk] = project([(0, 0), (0, 1), (1, 0), (1, 1)], a, chunk)

    def other_plane(a, result):
        done(ao.at[:, 3, a], ar.at[4 * a + 1])
        slots = [(0, 2), (0, 3), (1, 2), (1, 3)]
        for chunk in chunks:
            total = acc[a, :, chunk] + project(slots, a, chunk)
            scale = gate[chunk].reshape(1, step)
            base = xbuf[a, :, chunk].astype(F32)
            result[:, chunk] = (base + scale * total).astype(BF16)

    w_own.wait()
    w_twin.wait_recv()
    done(xbuf, x_sem)
    gate_load.wait()
    for i in range(rows // FRAME):
        piece = slice(i * FRAME, (i + 1) * FRAME)
        xbuf[1, piece] = masked(xbuf[1, piece], i)
    for a in range(2):
        for h in heads_:
            own_heads(h, a)
    own_plane(0)
    done(wbuf.at[2:4, rest], wxr.at[2 * halves])
    done(wbuf.at[2:4, y_part(1 - y)], wyr)
    both(
        jnp.logical_and(straight, jnp.logical_not(home)),
        lambda: done(kv.at[0:4, 0:6], zs),
        lambda: done(kv.at[0:2, 0:6], zs),
    )
    done(wbuf.at[0:2, 0 : width - y_rows], wxs)
    done(wbuf.at[2:4, y_part(y)], wys)
    w_twin.wait_send()

    @pl.when(home)
    def _():
        done(kv.at[0:2, 0:8], fs)

    for h in heads_:
        cross_heads(h, 0)
    own_plane(1)
    for h in heads_:
        cross_heads(h, 1)
    @pl.when(home)
    def _():
        both(itself, lambda: done(res.at[0:3], rs), lambda: done(res, rs))

    other_plane(0, out)
    other_plane(1, d_out)

    done(ao.at[:, 1:n_mp], as_)


def gathered_call(n, n_mp, q, dq, k, v, dk, dv, flags, w, gate, x, dx):
    rows, width = q.shape
    cols = x.shape[1]
    heads = width // HD
    halves = 2 if cols % (2 * HD) == 0 else 1
    anywhere = pl.BlockSpec(memory_space=pl.ANY)
    vmem = pl.BlockSpec(memory_space=pltpu.VMEM)
    dma = pltpu.SemaphoreType.DMA
    return pl.pallas_call(
        functools.partial(gathered, n, n_mp),
        out_shape=(pltpu.VMEM(x.shape, BF16), pltpu.VMEM(x.shape, BF16)),
        in_specs=[anywhere] * 11,
        out_specs=(vmem, vmem),
        scratch_shapes=[
            pltpu.VMEM((3, rows, width), BF16),
            pltpu.VMEM((heads, rows, 2 * HD), BF16),
            pltpu.VMEM((heads, 4, rows, HD), BF16),
            pltpu.VMEM((heads, rows, 2 * HD), BF16),
            pltpu.VMEM((heads, 4, rows, HD), BF16),
            pltpu.VMEM((4, rows, 2 * HD), BF16),
            pltpu.VMEM((4, 8, rows, HD), BF16),
            pltpu.VMEM((4 * rows, HD), F32),
            pltpu.VMEM((4 * rows, HD), F32),
            pltpu.VMEM((4 * rows, HD), F32),
            pltpu.VMEM((4 * rows, HD), F32),
            pltpu.VMEM((4 * rows, HD), F32),
            pltpu.VMEM((4, 2, rows, HD), BF16),
            pltpu.VMEM((heads, n_mp, 2, rows, HD), BF16),
            pltpu.VMEM((n_mp, width, cols), BF16),
            pltpu.VMEM((2, rows, cols), F32),
            pltpu.VMEM((2, rows, cols), BF16),
            pltpu.SMEM((rows,), jnp.int32),
            pltpu.VMEM((cols,), F32),
            dma,
            dma,
            dma((2,)),
            dma,
            dma((4,)),
            dma,
            dma((2, 8)),
            dma((heads, 3)),
            dma,
            dma,
            dma,
            dma,
            dma((2 * halves + 1,)),
            dma,
            dma,
            dma,
            dma((heads, 2)),
            dma,
            dma((8,)),
        ],
        compiler_params=pltpu.CompilerParams(
            collective_id=0, has_side_effects=True, vmem_limit_bytes=65000000
        ),
    )(q, dq, k, v, dk, dv, flags, w, gate, x, dx)


def gathers(n, n_mp, q, x):
    heads = q.shape[1] // HD
    return (
        n_mp == 4
        and n == 8
        and heads == 2
        and x.shape[1] % HD == 0
        and q.shape[0] % FRAME == 0
    )


def program(n, n_mp, q, dq, k, v, dk, dv, flags, w, gate, x, dx):
    call = gathered_call if gathers(n, n_mp, q, x) else per_device
    return call(n, n_mp, q, dq, k, v, dk, dv, flags, w, gate, x, dx)


def solution(mesh):
    both = P("tm", "mp")
    placed = (both,) * 6 + (P("tm"), P("mp", None), P("mp"), both, both)
    return jax.shard_map(
        functools.partial(program, mesh.shape["tm"], mesh.shape["mp"]),
        mesh=mesh,
        in_specs=placed,
        out_specs=(both, both),
        check_vma=False,
    )
```

```python
import functools
import math

import jax
import jax.numpy as jnp
from jax import lax
from jax.experimental import pallas as pl
from jax.experimental.pallas import tpu as pltpu
from jax.sharding import PartitionSpec as P

HD = 128
FRAME = 32
MESH = pl.DeviceIdType.MESH
F32 = jnp.float32
BF16 = jnp.bfloat16


def ring_place(t, n):
    return jnp.where(t % 2 == 0, t // 2, n - 1 - t // 2)


def ring_member(r, n):
    return jnp.where(r < n // 2, 2 * r, 2 * (n - 1 - r) + 1)


def flipped(me, j):
    other = me
    bit = 1
    while bit <= j:
        if j & bit:
            other = other + bit * (1 - 2 * ((me // bit) % 2))
        bit *= 2
    return other


def dot_nt(a, b):
    return lax.dot_general(a, b, (((1,), (1,)), ((), ())), preferred_element_type=F32)


def dot_nn(a, b):
    return lax.dot_general(a, b, (((1,), (0,)), ((), ())), preferred_element_type=F32)


def fused(
    n,
    n_mp,
    move_w,
    q_hbm,
    dq_hbm,
    k_hbm,
    v_hbm,
    dk_hbm,
    dv_hbm,
    flags_hbm,
    w_hbm,
    gate_hbm,
    x_hbm,
    dx_hbm,
    out,
    d_out,
    own,
    qcat,
    tkv,
    kv,
    opp,
    m_s,
    l_s,
    c_s,
    a_s,
    g_s,
    ao,
    wbuf,
    acc,
    xbuf,
    flags,
    gate,
    own_sem,
    x_sem,
    small_sem,
    w_local,
    ks,
    kr,
    ws,
    wr,
    as_,
    ar,
):
    rows, width = q_hbm.shape
    heads = width // HD
    cols = out.shape[1]
    half = n // 2
    t = lax.axis_index("tm")
    m = lax.axis_index("mp")
    place = ring_place(t, n)
    right = ring_member((place + 1) % n, n)
    left = ring_member((place + n - 1) % n, n)
    peers = [flipped(m, j) for j in range(n_mp)]
    factor = 1.0 / math.sqrt(HD)

    def lanes(h):
        return slice(h * HD, (h + 1) * HD)

    loads = [
        pltpu.make_async_copy(src, own.at[i], own_sem.at[i])
        for i, src in enumerate((k_hbm, v_hbm, dk_hbm, dv_hbm, q_hbm, dq_hbm))
    ]
    loads.append(pltpu.make_async_copy(flags_hbm, flags, small_sem.at[0]))
    for load in loads:
        load.start()

    barrier = pltpu.get_barrier_semaphore()
    for dev in [(right, m), (left, m)] + [(t, peers[j]) for j in range(1, n_mp)]:
        pl.semaphore_signal(barrier, inc=1, device_id=dev, device_id_type=MESH)
    pl.semaphore_wait(barrier, 1 + n_mp)

    def exists(d, s, p):
        return s < half or (s == half and (p < 2) == (d == 0))

    def kv_copy(h, d, s, p):
        side = slice(d * rows, (d + 1) * rows)
        if s > 1:
            src = kv.at[h, s - 2, p, side]
        elif p < 2:
            src = (k_hbm, v_hbm)[p].at[:, lanes(h)]
        else:
            src = tkv.at[h, p - 2]
        dst = kv.at[h, s - 1, p, side] if s < half else opp.at[h, p]
        return pltpu.make_async_remote_copy(
            src_ref=src,
            dst_ref=dst,
            send_sem=ks.at[h, d, s - 1, p],
            recv_sem=kr.at[h, d, s - 1, p],
            device_id=((right, left)[d], m),
            device_id_type=MESH,
        )

    def send_own(h, pieces):
        for p in pieces:
            for d in (0, 1):
                kv_copy(h, d, 1, p).start()

    def w_copy(h, j):
        span = pl.ds(pl.multiple_of(peers[j] * cols, HD), cols)
        part = slice(h * HD, (h + 1) * HD)
        if j == 0:
            return pltpu.make_async_copy(
                w_hbm.at[part, span], wbuf.at[0, part], w_local.at[h]
            )
        return pltpu.make_async_remote_copy(
            src_ref=w_hbm.at[part, span],
            dst_ref=wbuf.at[j, part],
            send_sem=ws.at[h, j],
            recv_sem=wr.at[h, j],
            device_id=(t, peers[j]),
            device_id_type=MESH,
        )

    def ao_copy(h, j):
        relay = j % 2 == 1 and j > 1
        return pltpu.make_async_remote_copy(
            src_ref=ao.at[h, j - 1 if relay else 0],
            dst_ref=ao.at[h, j],
            send_sem=as_.at[h, j],
            recv_sem=ar.at[h, j],
            device_id=(t, peers[1] if relay else peers[j]),
            device_id_type=MESH,
        )

    send_own(0, (0, 1))
    if move_w:
        for h in range(heads):
            for j in list(range(2, n_mp)) + [1, 0]:
                w_copy(h, j).start()
    x_loads = [
        pltpu.make_async_copy(src, xbuf.at[i], x_sem.at[i])
        for i, src in enumerate((x_hbm, dx_hbm))
    ]
    x_loads.append(pltpu.make_async_copy(gate_hbm, gate, small_sem.at[1]))
    for load in x_loads:
        load.start()
    for load in loads:
        load.wait()

    live = [
        jnp.where(flags[i * FRAME] > 0, 1.0, 0.0).astype(F32)
        for i in range(rows // FRAME)
    ]

    def masked(value, i):
        scale = jnp.full(value.shape, live[i], F32)
        return (value.astype(F32) * scale).astype(BF16)

    for h in range(heads):
        for i in range(rows // FRAME):
            part = slice(i * FRAME, (i + 1) * FRAME)
            tkv[h, 0, part] = masked(own[2, part, lanes(h)], i)
            tkv[h, 1, part] = masked(own[3, part, lanes(h)], i)
        if h == 0:
            send_own(0, (2, 3))
            for g in range(1, heads):
                send_own(g, (0, 1))
        else:
            send_own(h, (2, 3))
    for h in range(heads):
        for i in range(rows // FRAME):
            part = slice(i * FRAME, (i + 1) * FRAME)
            qcat[h, part, 0:HD] = masked(own[5, part, lanes(h)], i)
        qcat[h, :, HD : 2 * HD] = own[4, :, lanes(h)]

    def attend(h, k, tk, values, first):
        queries = qcat[h, :, HD : 2 * HD]
        scores = dot_nt(queries, k)
        d_scores = dot_nt(qcat[h], jnp.concatenate([k, tk], axis=1)) * factor
        peak = jnp.max(scores, axis=1, keepdims=True)
        if not first:
            peak_old = m_s[h]
            peak = jnp.maximum(peak_old, peak)
            rescale = jnp.exp((peak_old - peak) * factor)
        weights = jnp.exp((scores - peak) * factor)
        product = weights * d_scores
        total = jnp.sum(weights, axis=1, keepdims=True)
        slope = jnp.sum(product, axis=1, keepdims=True)
        weights_b = weights.astype(BF16)
        product_b = product.astype(BF16)
        v, tv = values()
        primal = dot_nn(weights_b, v)
        tangent = dot_nn(product_b, v) + dot_nn(weights_b, tv)
        m_s[h] = peak
        if first:
            l_s[h] = total
            c_s[h] = slope
            a_s[h] = primal
            g_s[h] = tangent
        else:
            l_s[h] = l_s[h] * rescale + total
            c_s[h] = c_s[h] * rescale + slope
            a_s[h] = a_s[h] * rescale + primal
            g_s[h] = g_s[h] * rescale + tangent

    def finish(h):
        inverse = 1.0 / l_s[h]
        outputs = a_s[h] * inverse
        d_outputs = g_s[h] * inverse - (c_s[h] * inverse) * outputs
        ao[h, 0, 0:rows] = outputs.astype(BF16)
        ao[h, 0, rows : 2 * rows] = d_outputs.astype(BF16)
        for j in list(range(2, n_mp, 2)) + [1]:
            ao_copy(h, j).start()

    def relay(h):
        for j in range(2, n_mp, 2):
            ao_copy(h, j).wait_recv()
            ao_copy(h, j + 1).start()

    for h in range(heads):
        attend(
            h, own[0, :, lanes(h)], tkv[h, 0], lambda: (own[1, :, lanes(h)], tkv[h, 1]), True
        )
    for s in range(1, half):
        for h in range(heads):
            for p in range(4):
                for d in (0, 1):
                    kv_copy(h, d, s, p).wait_recv()
                    if exists(d, s + 1, p):
                        kv_copy(h, d, s + 1, p).start()
            attend(
                h,
                kv[h, s - 1, 0],
                kv[h, s - 1, 2],
                lambda: (kv[h, s - 1, 1], kv[h, s - 1, 3]),
                False,
            )
    for h in range(heads):
        def opposite(first_p, second_p):
            kv_copy(h, 0, half, first_p).wait_recv()
            kv_copy(h, 1, half, second_p).wait_recv()
            return opp[h, first_p], opp[h, second_p]

        keys, d_keys = opposite(0, 2)
        attend(h, keys, d_keys, lambda: opposite(1, 3), False)
        finish(h)

    step = 2 * HD if cols % (2 * HD) == 0 else cols
    chunks = [slice(c, c + step) for c in range(0, cols, step)]

    def w_part(h, j, chunk):
        part = slice(h * HD, (h + 1) * HD)
        if move_w:
            return wbuf[j, part, chunk]
        return w_hbm[peers[j], part, chunk]

    def project(slots, chunk):
        attn = jnp.concatenate([ao[h, j] for h, j in slots], axis=1)
        weight = jnp.concatenate([w_part(h, j, chunk) for h, j in slots], axis=0)
        return dot_nn(attn, weight)

    if move_w:
        for h in range(heads):
            w_copy(h, 0).wait()
            for j in range(1, n_mp):
                w_copy(h, j).wait_recv()
    for load in x_loads:
        load.wait()
    last = heads - 1
    for h in range(heads):
        ao_copy(h, 1).wait_recv()
    near = [(h, j) for h in range(heads) for j in (0, 1)]
    for chunk in chunks:
        acc[:, chunk] = project(near, chunk)
    for h in range(last):
        relay(h)
    for h in range(last):
        for j in range(3, n_mp, 2):
            ao_copy(h, j).wait_recv()
    far = [(h, j) for h in range(last) for j in range(2, n_mp)]
    for chunk in chunks:
        acc[:, chunk] += project(far, chunk)
    for h in range(heads):
        for s in range(1, half + 1):
            for p in range(4):
                for d in (0, 1):
                    if exists(d, s, p):
                        kv_copy(h, d, s, p).wait_send()
        if move_w:
            for j in range(1, n_mp):
                w_copy(h, j).wait_send()
    relay(last)
    even = [(last, j) for j in range(2, n_mp, 2)]
    for chunk in chunks:
        acc[:, chunk] += project(even, chunk)
    for j in range(3, n_mp, 2):
        ao_copy(last, j).wait_recv()
    odd = [(last, j) for j in range(3, n_mp, 2)]
    for chunk in chunks:
        part = acc[:, chunk] + project(odd, chunk)
        scale = gate[chunk].reshape(1, step)
        out[:, chunk] = (xbuf[0, :, chunk].astype(F32) + scale * part[0:rows]).astype(BF16)
        for i in range(rows // FRAME):
            piece = slice(i * FRAME, (i + 1) * FRAME)
            base = xbuf[1, piece, chunk].astype(F32)
            base = base * jnp.full(base.shape, live[i], F32)
            delta = part[rows + i * FRAME : rows + (i + 1) * FRAME]
            d_out[piece, chunk] = (base + scale * delta).astype(BF16)

    for h in range(heads):
        for j in range(1, n_mp):
            ao_copy(h, j).wait_send()


def per_device(n, n_mp, q, dq, k, v, dk, dv, flags, w, gate, x, dx):
    rows, width = q.shape
    cols = x.shape[1]
    heads = width // HD
    half = n // 2
    move_w = cols % HD == 0
    if not move_w:
        w = lax.all_to_all(w, "mp", split_axis=1, concat_axis=0, tiled=True)
        w = w.reshape(n_mp, width, cols)
    anywhere = pl.BlockSpec(memory_space=pl.ANY)
    vmem = pl.BlockSpec(memory_space=pltpu.VMEM)
    dma = pltpu.SemaphoreType.DMA
    return pl.pallas_call(
        functools.partial(fused, n, n_mp, move_w),
        out_shape=(pltpu.VMEM(x.shape, BF16), pltpu.VMEM(x.shape, BF16)),
        in_specs=[anywhere] * 6
        + [anywhere, anywhere if move_w else vmem, anywhere]
        + [anywhere] * 2,
        out_specs=(vmem, vmem),
        scratch_shapes=[
            pltpu.VMEM((6, rows, width), BF16),
            pltpu.VMEM((heads, rows, 2 * HD), BF16),
            pltpu.VMEM((heads, 2, rows, HD), BF16),
            pltpu.VMEM((heads, half - 1, 4, 2 * rows, HD), BF16),
            pltpu.VMEM((heads, 4, rows, HD), BF16),
            pltpu.VMEM((heads, rows, 1), F32),
            pltpu.VMEM((heads, rows, 1), F32),
            pltpu.VMEM((heads, rows, 1), F32),
            pltpu.VMEM((heads, rows, HD), F32),
            pltpu.VMEM((heads, rows, HD), F32),
            pltpu.VMEM((heads, n_mp, 2 * rows, HD), BF16),
            pltpu.VMEM((n_mp, width, cols) if move_w else (1, 16, HD), BF16),
            pltpu.VMEM((2 * rows, cols), F32),
            pltpu.VMEM((2, rows, cols), BF16),
            pltpu.SMEM((rows,), jnp.int32),
            pltpu.VMEM((cols,), F32),
            dma((6,)),
            dma((2,)),
            dma((2,)),
            dma((heads,)),
            dma((heads, 2, half, 4)),
            dma((heads, 2, half, 4)),
            dma((heads, n_mp)),
            dma((heads, n_mp)),
            dma((heads, n_mp)),
            dma((heads, n_mp)),
        ],
        compiler_params=pltpu.CompilerParams(
            collective_id=0, has_side_effects=True, vmem_limit_bytes=65000000
        ),
    )(q, dq, k, v, dk, dv, flags, w, gate, x, dx)


def gathered(
    n,
    n_mp,
    q_hbm,
    dq_hbm,
    k_hbm,
    v_hbm,
    dk_hbm,
    dv_hbm,
    flags_hbm,
    w_hbm,
    gate_hbm,
    x_hbm,
    dx_hbm,
    out,
    d_out,
    own,
    qpack,
    pack,
    qpeer,
    peer,
    qcat,
    kv,
    m_s,
    l_s,
    c_s,
    a_s,
    g_s,
    res,
    ao,
    wbuf,
    acc,
    xbuf,
    flags,
    gate,
    raw_sem,
    x_sem,
    small_sem,
    w_local,
    qr,
    zs,
    kr,
    pr,
    fs,
    wts,
    wtr,
    wxs,
    wxr,
    wys,
    wyr,
    rs,
    rr,
    as_,
    ar,
):
    rows, width = q_hbm.shape
    heads = width // HD
    cols = out.shape[1]
    t = lax.axis_index("tm")
    m = lax.axis_index("mp")
    z, y = t // 2, t % 2
    plane, core = m // 2, m % 2
    side = z // 2
    role = jnp.where(side == 0, 1 - z % 2, z % 2)
    home = role == 0
    straight = y == core
    itself = jnp.logical_and(home, straight)

    def chip(side_, role_):
        return 2 * side_ + jnp.where(side_ == 0, 1 - role_, role_)

    order = (side, 1 - side)
    homes = [(2 * chip(h, 0) + core, 2 * plane + y) for h in order]
    sources = [
        (2 * chip((side + g // 2) % 2, g % 2) + core, 2 * plane + y) for g in range(4)
    ]
    twin = (t, 2 * plane + 1 - core)
    across = (t, 2 * (1 - plane) + core)
    diagonal = (t, 2 * (1 - plane) + 1 - core)
    row_peer = (2 * z + 1 - y, m)
    factor = 1.0 / math.sqrt(HD)
    power = factor * math.log2(math.e)

    def lanes(h):
        return slice(h * HD, (h + 1) * HD)

    def both(flag, yes, no):
        pl.when(flag)(yes)
        pl.when(jnp.logical_not(flag))(no)

    def unless(flag, no):
        pl.when(jnp.logical_not(flag))(no)

    barrier = pltpu.get_barrier_semaphore()

    def greet(dev):
        pl.semaphore_signal(barrier, inc=1, device_id=dev, device_id_type=MESH)

    greet(homes[1])
    unless(itself, lambda: greet(homes[0]))

    @pl.when(home)
    def _():
        for i in (3, 2, 1):
            greet(sources[i])
        unless(itself, lambda: greet(sources[0]))

    @pl.when(straight)
    def _():
        for h in order:
            greet((2 * chip(h, 0) + y, 2 * plane + 1 - y))

    @pl.when(jnp.logical_and(home, jnp.logical_not(straight)))
    def _():
        for g in range(4):
            greet((2 * chip((side + g // 2) % 2, g % 2) + y, 2 * plane + y))

    for dev in (across, diagonal, row_peer, twin):
        greet(dev)

    loads = [
        pltpu.make_async_copy(src, own.at[i], raw_sem)
        for i, src in enumerate((dq_hbm, dk_hbm, dv_hbm))
    ]
    flags_load = pltpu.make_async_copy(flags_hbm, flags, small_sem.at[0])
    raw = []

    def done(ref, sem):
        pltpu.make_async_copy(ref, ref, sem).wait()

    for j in range(heads):
        for i, (src, dst) in enumerate(
            (
                (q_hbm, qpack.at[j, :, HD : 2 * HD]),
                (k_hbm, pack.at[j, 0]),
                (v_hbm, pack.at[j, 2]),
            )
        ):
            raw.append(
                pltpu.make_async_copy(src.at[:, lanes(j)], dst, raw_sem)
            )
    flags_load.start()
    for load in loads + raw:
        load.start()
    flags_load.wait()
    done(kv.at[0:4, 0:3], raw_sem)

    live = [
        jnp.where(flags[i * FRAME] > 0, 1.0, 0.0).astype(F32)
        for i in range(rows // FRAME)
    ]

    def masked(value, i):
        scale = jnp.full(value.shape, live[i], F32)
        return (value.astype(F32) * scale).astype(BF16)

    for h in range(heads):
        for i in range(rows // FRAME):
            piece = slice(i * FRAME, (i + 1) * FRAME)
            qpack[h, piece, 0:HD] = masked(own[0, piece, lanes(h)], i)
            pack[h, 1, piece] = masked(own[1, piece, lanes(h)], i)
            pack[h, 3, piece] = masked(own[2, piece, lanes(h)], i)
    pl.semaphore_wait(
        barrier,
        4 + heads + 4 * home.astype(jnp.int32) - 2 * itself.astype(jnp.int32)
        + 2 * straight.astype(jnp.int32)
        + 4 * (home.astype(jnp.int32) - itself.astype(jnp.int32)),
    )

    def remote(ends, send_sem, dev):
        src, dst, sem = ends
        return pltpu.make_async_remote_copy(
            src_ref=src,
            dst_ref=dst,
            send_sem=send_sem,
            recv_sem=sem,
            device_id=dev,
            device_id_type=MESH,
        )

    def home_ends(o, piece, relayed=False):
        h = order[o]
        g = 2 * o + role
        if piece == 0:
            return (qpeer.at[o] if relayed else qpack.at[h]), qcat.at[g], qr.at[g]
        pair = slice(2 * piece - 2, 2 * piece)
        crossing = 1 if relayed else (y + core) % 2
        slot = g + 4 * crossing
        src = peer.at[o, pair] if relayed else pack.at[h, pair]
        return src, kv.at[pair, slot], kr.at[piece - 1, slot]

    def home_copy(o, piece):
        return remote(home_ends(o, piece), zs, homes[o])

    def home_all(o):
        for piece in range(3):
            home_copy(o, piece).start()

    def home_local():
        for piece in range(3):
            pltpu.make_async_copy(*home_ends(0, piece)).start()

    def peer_copy(o, piece):
        h = order[o]
        if piece == 0:
            ends = (qpack.at[h], qpeer.at[o], pr.at[o, piece])
        else:
            pair = slice(2 * piece - 2, 2 * piece)
            ends = (pack.at[h, pair], peer.at[o, pair], pr.at[o, piece])
        return remote(ends, zs, row_peer)

    def peer_all(o):
        for piece in range(3):
            peer_copy(o, piece).start()

    def onward(o, piece):
        dev = (2 * chip(order[o], 0) + y, 2 * plane + 1 - y)
        return remote(home_ends(o, piece, True), zs, dev)

    def relay(o):
        for piece in range(3):
            peer_copy(o, piece).wait_recv()
            onward(o, piece).start()

    def straight_sends():
        both(itself, home_local, lambda: home_all(0))
        home_all(1)

    def crossing_sends():
        def middle():
            peer_all(1)
            home_all(0)

        def end():
            peer_all(0)
            peer_all(1)

        both(home, middle, end)

    both(straight, straight_sends, crossing_sends)

    tile = 16
    y_rows = (width // tile * 3 // 8) * tile
    rest = slice(2 * y_rows, width)
    halves = 2 if cols % (2 * HD) == 0 else 1
    span = cols // halves

    def y_part(index):
        return pl.ds(pl.multiple_of(index * y_rows, tile), y_rows)

    def w_cols(owner, first, size):
        return pl.ds(pl.multiple_of(owner * cols + first, HD), size)

    def w_cross(slot, piece):
        dev = across if slot == 0 else diagonal
        if piece < halves:
            rows_ = y_part(y)
            first, size = piece * span, span
        else:
            rows_ = rest
            first, size = (piece - halves) * span, span
        return remote(
            (
                w_hbm.at[rows_, w_cols(dev[1], first, size)],
                wbuf.at[2 + slot, rows_, pl.ds(first, size)],
                wxr.at[2 * piece + slot if piece < halves else 2 * halves],
            ),
            wxs,
            dev,
        )

    def w_row(slot, piece):
        ref = wbuf.at[2 + slot, y_part(y), pl.ds(piece * span, span)]
        return remote((ref, ref, wyr), wys, row_peer)

    def w_row_relay(piece):
        for slot in range(2):
            w_cross(slot, piece).wait_recv()
            w_row(slot, piece).start()

    w_twin = remote(
        (w_hbm.at[:, w_cols(twin[1], 0, cols)], wbuf.at[1], wtr), wts, twin
    )
    w_own = pltpu.make_async_copy(w_hbm.at[:, w_cols(m, 0, cols)], wbuf.at[0], w_local)

    for piece in range(2 * halves):
        for slot in range(2):
            w_cross(slot, piece).start()
    w_twin.start()
    w_own.start()
    x_loads = [
        pltpu.make_async_copy(src, xbuf.at[i], x_sem)
        for i, src in enumerate((x_hbm, dx_hbm))
    ]
    gate_load = pltpu.make_async_copy(gate_hbm, gate, small_sem.at[1])
    for load in x_loads:
        load.start()
    gate_load.start()

    mine_at = 4 * ((y + core) % 2)
    twins_at = 4 - mine_at

    def to_twin(pair, g):
        ref = kv.at[2 * pair : 2 * pair + 2, g + mine_at]
        return remote((ref, ref, kr.at[pair, g + mine_at]), fs, twin)

    def kv_wait(pair, slot):
        ref = kv.at[2 * pair : 2 * pair + 2, slot]
        pltpu.make_async_copy(ref, ref, kr.at[pair, slot]).wait()

    def arrive(g):
        for pair in range(2):
            kv_wait(pair, g + mine_at)
            to_twin(pair, g).start()

    def from_twin(g):
        for pair in range(2):
            kv_wait(pair, g + twins_at)

    def q_wait(i):
        pltpu.make_async_copy(qcat.at[i], qcat.at[i], qr.at[i]).wait()

    def attend(blocks, queries):
        first = blocks[0] == 0
        last = blocks[1] == 8
        keys = (blocks[1] - blocks[0]) * rows
        count = (queries[1] - queries[0]) * rows
        at = slice(queries[0] * rows, queries[1] * rows)

        def spread(column):
            return jnp.broadcast_to(column, (count, HD))

        k, tk, v, tv = (
            kv[p, blocks[0] : blocks[1]].reshape(keys, HD) for p in range(4)
        )
        q = qcat[queries[0] : queries[1]].reshape(count, 2 * HD)
        scores = dot_nt(q[:, HD : 2 * HD], k)
        d_scores = dot_nt(q, jnp.concatenate([k, tk], axis=1))
        peak = spread(jnp.max(scores, axis=1, keepdims=True))
        if not first:
            peak_old = m_s[at]
            peak = jnp.maximum(peak_old, peak)
            rescale = jnp.exp2((peak_old - peak) * power)
        weights = jnp.exp2((scores - jnp.tile(peak, (1, keys // HD))) * power)
        product = weights * d_scores
        total = spread(jnp.sum(weights, axis=1, keepdims=True))
        slope = spread(jnp.sum(product, axis=1, keepdims=True))
        weights_b = weights.astype(BF16)
        product_b = product.astype(BF16)
        wide = dot_nn(weights_b, jnp.concatenate([v, tv], axis=1))
        primal = wide[:, 0:HD]
        tangent = dot_nn(product_b, v) * factor + wide[:, HD : 2 * HD]
        if not first:
            total = l_s[at] * rescale + total
            slope = c_s[at] * rescale + slope
            primal = a_s[at] * rescale + primal
            tangent = g_s[at] * rescale + tangent
        if last:
            inverse = 1.0 / total
            outputs = primal * inverse
            d_outputs = tangent * inverse - (slope * (factor * inverse)) * outputs
            for i in range(*queries):
                own_rows = slice((i - queries[0]) * rows, (i - queries[0] + 1) * rows)
                res[i, 0] = outputs[own_rows].astype(BF16)
                res[i, 1] = d_outputs[own_rows].astype(BF16)
        else:
            m_s[at] = peak
            l_s[at] = total
            c_s[at] = slope
            a_s[at] = primal
            g_s[at] = tangent

    def res_ends(i, a):
        return res.at[i, a], ao.at[side, 0, a], rr.at[side, a]

    def res_remote(i, a):
        return remote(res_ends(i, a), rs, sources[i])

    def res_start(i, a):
        def local():
            pltpu.make_async_copy(*res_ends(i, a)).start()

        def away():
            res_remote(i, a).start()

        if i == 0:
            both(itself, local, away)
        else:
            away()

    @pl.when(home)
    def _():
        def nothing(g):
            pass

        def each(groups, on_straight, on_crossing):
            for g in groups:
                both(straight, lambda: on_straight(g), lambda: on_crossing(g))

        pl.when(straight)(lambda: relay(1))
        unless(straight, lambda: arrive(0))
        each((0, 1), arrive, from_twin)
        w_row_relay(0)
        each((2, 3), arrive, from_twin)
        q_wait(0)
        q_wait(1)
        attend((0, 4), (0, 2))
        each((0,), from_twin, nothing)
        each((1,), from_twin, arrive)
        attend((4, 6), (0, 2))
        for piece in range(1, halves):
            w_row_relay(piece)
        q_wait(2)
        q_wait(3)
        attend((0, 6), (2, 4))
        each((2, 3), from_twin, arrive)
        for queries in ((2, 4), (0, 2)):
            attend((6, 8), queries)
            for a in range(2):
                for i in range(queries[1] - 1, queries[0] - 1, -1):
                    res_start(i, a)

    @pl.when(jnp.logical_not(home))
    def _():
        @pl.when(straight)
        def _():
            relay(0)
            relay(1)

        for piece in range(halves):
            w_row_relay(piece)

    def ao_copy(h, j, a):
        src = ao.at[h, 2 if j == 3 else 0, a]
        dst = ao.at[h, j, a]
        dev = across if j == 2 else twin
        at = 4 * a + (2 + h if j == 2 else j // 2)
        return remote((src, dst, ar.at[at]), as_, dev)

    def own_heads(h, a):
        ref = ao.at[h, 0, a]
        pltpu.make_async_copy(ref, ref, rr.at[h, a]).wait()
        ao_copy(h, 2, a).start()
        ao_copy(h, 1, a).start()

    def cross_heads(h, a):
        ao_copy(h, 2, a).wait_recv()
        ao_copy(h, 3, a).start()

    step = 2 * HD if cols % (2 * HD) == 0 else cols
    chunks = [slice(c, c + step) for c in range(0, cols, step)]

    def project(slots, a, chunk):
        attn = jnp.concatenate([ao[heads_[h], j, a] for h, j in slots], axis=1)
        weight = jnp.concatenate([wbuf[j, w_rows[h], chunk] for h, j in slots], axis=0)
        return dot_nn(attn, weight)

    heads_ = (side, 1 - side)
    w_rows = [pl.ds(pl.multiple_of(h * HD, HD), HD) for h in heads_]
    first = jnp.where(home, side, 1 - side)
    second = 1 - first

    def own_plane(a):
        done(ao.at[:, 1, a], ar.at[4 * a])
        for chunk in chunks:
            acc[a, :, chunk] = project([(0, 0), (0, 1), (1, 0), (1, 1)], a, chunk)

    def other_plane(a, result):
        done(ao.at[:, 3, a], ar.at[4 * a + 1])
        slots = [(0, 2), (0, 3), (1, 2), (1, 3)]
        for chunk in chunks:
            total = acc[a, :, chunk] + project(slots, a, chunk)
            scale = gate[chunk].reshape(1, step)
            base = xbuf[a, :, chunk].astype(F32)
            result[:, chunk] = (base + scale * total).astype(BF16)

    w_own.wait()
    w_twin.wait_recv()
    done(xbuf, x_sem)
    gate_load.wait()
    for i in range(rows // FRAME):
        piece = slice(i * FRAME, (i + 1) * FRAME)
        xbuf[1, piece] = masked(xbuf[1, piece], i)
    for h in (first, second):
        for a in range(2):
            own_heads(h, a)
    own_plane(0)
    done(wbuf.at[2:4, rest], wxr.at[2 * halves])
    done(wbuf.at[2:4, y_part(1 - y)], wyr)
    both(
        jnp.logical_and(straight, jnp.logical_not(home)),
        lambda: done(kv.at[0:4, 0:6], zs),
        lambda: done(kv.at[0:2, 0:6], zs),
    )
    done(wbuf.at[0:2, 0 : width - y_rows], wxs)
    done(wbuf.at[2:4, y_part(y)], wys)
    w_twin.wait_send()

    @pl.when(home)
    def _():
        done(kv.at[0:2, 0:8], fs)

    cross_heads(first, 0)
    own_plane(1)
    cross_heads(first, 1)
    cross_heads(second, 0)
    cross_heads(second, 1)
    @pl.when(home)
    def _():
        both(itself, lambda: done(res.at[0:3], rs), lambda: done(res, rs))

    other_plane(0, out)
    other_plane(1, d_out)

    done(ao.at[:, 1:n_mp], as_)


def gathered_call(n, n_mp, q, dq, k, v, dk, dv, flags, w, gate, x, dx):
    rows, width = q.shape
    cols = x.shape[1]
    heads = width // HD
    halves = 2 if cols % (2 * HD) == 0 else 1
    anywhere = pl.BlockSpec(memory_space=pl.ANY)
    vmem = pl.BlockSpec(memory_space=pltpu.VMEM)
    dma = pltpu.SemaphoreType.DMA
    return pl.pallas_call(
        functools.partial(gathered, n, n_mp),
        out_shape=(pltpu.VMEM(x.shape, BF16), pltpu.VMEM(x.shape, BF16)),
        in_specs=[anywhere] * 11,
        out_specs=(vmem, vmem),
        scratch_shapes=[
            pltpu.VMEM((3, rows, width), BF16),
            pltpu.VMEM((heads, rows, 2 * HD), BF16),
            pltpu.VMEM((heads, 4, rows, HD), BF16),
            pltpu.VMEM((heads, rows, 2 * HD), BF16),
            pltpu.VMEM((heads, 4, rows, HD), BF16),
            pltpu.VMEM((4, rows, 2 * HD), BF16),
            pltpu.VMEM((4, 8, rows, HD), BF16),
            pltpu.VMEM((4 * rows, HD), F32),
            pltpu.VMEM((4 * rows, HD), F32),
            pltpu.VMEM((4 * rows, HD), F32),
            pltpu.VMEM((4 * rows, HD), F32),
            pltpu.VMEM((4 * rows, HD), F32),
            pltpu.VMEM((4, 2, rows, HD), BF16),
            pltpu.VMEM((heads, n_mp, 2, rows, HD), BF16),
            pltpu.VMEM((n_mp, width, cols), BF16),
            pltpu.VMEM((2, rows, cols), F32),
            pltpu.VMEM((2, rows, cols), BF16),
            pltpu.SMEM((rows,), jnp.int32),
            pltpu.VMEM((cols,), F32),
            dma,
            dma,
            dma((2,)),
            dma,
            dma((4,)),
            dma,
            dma((2, 8)),
            dma((heads, 3)),
            dma,
            dma,
            dma,
            dma,
            dma((2 * halves + 1,)),
            dma,
            dma,
            dma,
            dma((heads, 2)),
            dma,
            dma((8,)),
        ],
        compiler_params=pltpu.CompilerParams(
            collective_id=0, has_side_effects=True, vmem_limit_bytes=65000000
        ),
    )(q, dq, k, v, dk, dv, flags, w, gate, x, dx)


def gathers(n, n_mp, q, x):
    heads = q.shape[1] // HD
    return (
        n_mp == 4
        and n == 8
        and heads == 2
        and x.shape[1] % HD == 0
        and q.shape[0] % FRAME == 0
    )


def program(n, n_mp, q, dq, k, v, dk, dv, flags, w, gate, x, dx):
    call = gathered_call if gathers(n, n_mp, q, x) else per_device
    return call(n, n_mp, q, dq, k, v, dk, dv, flags, w, gate, x, dx)


def solution(mesh):
    both = P("tm", "mp")
    placed = (both,) * 6 + (P("tm"), P("mp", None), P("mp"), both, both)
    return jax.shard_map(
        functools.partial(program, mesh.shape["tm"], mesh.shape["mp"]),
        mesh=mesh,
        in_specs=placed,
        out_specs=(both, both),
        check_vma=False,
    )
```

```python
import functools
import math

import jax
import jax.numpy as jnp
from jax import lax
from jax.experimental import pallas as pl
from jax.experimental.pallas import tpu as pltpu
from jax.sharding import PartitionSpec as P

HD = 128
FRAME = 32
MESH = pl.DeviceIdType.MESH
F32 = jnp.float32
BF16 = jnp.bfloat16


def ring_place(t, n):
    return jnp.where(t % 2 == 0, t // 2, n - 1 - t // 2)


def ring_member(r, n):
    return jnp.where(r < n // 2, 2 * r, 2 * (n - 1 - r) + 1)


def flipped(me, j):
    other = me
    bit = 1
    while bit <= j:
        if j & bit:
            other = other + bit * (1 - 2 * ((me // bit) % 2))
        bit *= 2
    return other


def dot_nt(a, b):
    return lax.dot_general(a, b, (((1,), (1,)), ((), ())), preferred_element_type=F32)


def dot_nn(a, b):
    return lax.dot_general(a, b, (((1,), (0,)), ((), ())), preferred_element_type=F32)


def fused(
    n,
    n_mp,
    move_w,
    q_hbm,
    dq_hbm,
    k_hbm,
    v_hbm,
    dk_hbm,
    dv_hbm,
    flags_hbm,
    w_hbm,
    gate_hbm,
    x_hbm,
    dx_hbm,
    out,
    d_out,
    own,
    qcat,
    tkv,
    kv,
    opp,
    m_s,
    l_s,
    c_s,
    a_s,
    g_s,
    ao,
    wbuf,
    acc,
    xbuf,
    flags,
    gate,
    own_sem,
    x_sem,
    small_sem,
    w_local,
    ks,
    kr,
    ws,
    wr,
    as_,
    ar,
):
    rows, width = q_hbm.shape
    heads = width // HD
    cols = out.shape[1]
    half = n // 2
    t = lax.axis_index("tm")
    m = lax.axis_index("mp")
    place = ring_place(t, n)
    right = ring_member((place + 1) % n, n)
    left = ring_member((place + n - 1) % n, n)
    peers = [flipped(m, j) for j in range(n_mp)]
    factor = 1.0 / math.sqrt(HD)

    def lanes(h):
        return slice(h * HD, (h + 1) * HD)

    loads = [
        pltpu.make_async_copy(src, own.at[i], own_sem.at[i])
        for i, src in enumerate((k_hbm, v_hbm, dk_hbm, dv_hbm, q_hbm, dq_hbm))
    ]
    loads.append(pltpu.make_async_copy(flags_hbm, flags, small_sem.at[0]))
    for load in loads:
        load.start()

    barrier = pltpu.get_barrier_semaphore()
    for dev in [(right, m), (left, m)] + [(t, peers[j]) for j in range(1, n_mp)]:
        pl.semaphore_signal(barrier, inc=1, device_id=dev, device_id_type=MESH)
    pl.semaphore_wait(barrier, 1 + n_mp)

    def exists(d, s, p):
        return s < half or (s == half and (p < 2) == (d == 0))

    def kv_copy(h, d, s, p):
        side = slice(d * rows, (d + 1) * rows)
        if s > 1:
            src = kv.at[h, s - 2, p, side]
        elif p < 2:
            src = (k_hbm, v_hbm)[p].at[:, lanes(h)]
        else:
            src = tkv.at[h, p - 2]
        dst = kv.at[h, s - 1, p, side] if s < half else opp.at[h, p]
        return pltpu.make_async_remote_copy(
            src_ref=src,
            dst_ref=dst,
            send_sem=ks.at[h, d, s - 1, p],
            recv_sem=kr.at[h, d, s - 1, p],
            device_id=((right, left)[d], m),
            device_id_type=MESH,
        )

    def send_own(h, pieces):
        for p in pieces:
            for d in (0, 1):
                kv_copy(h, d, 1, p).start()

    def w_copy(h, j):
        span = pl.ds(pl.multiple_of(peers[j] * cols, HD), cols)
        part = slice(h * HD, (h + 1) * HD)
        if j == 0:
            return pltpu.make_async_copy(
                w_hbm.at[part, span], wbuf.at[0, part], w_local.at[h]
            )
        return pltpu.make_async_remote_copy(
            src_ref=w_hbm.at[part, span],
            dst_ref=wbuf.at[j, part],
            send_sem=ws.at[h, j],
            recv_sem=wr.at[h, j],
            device_id=(t, peers[j]),
            device_id_type=MESH,
        )

    def ao_copy(h, j):
        relay = j % 2 == 1 and j > 1
        return pltpu.make_async_remote_copy(
            src_ref=ao.at[h, j - 1 if relay else 0],
            dst_ref=ao.at[h, j],
            send_sem=as_.at[h, j],
            recv_sem=ar.at[h, j],
            device_id=(t, peers[1] if relay else peers[j]),
            device_id_type=MESH,
        )

    send_own(0, (0, 1))
    if move_w:
        for h in range(heads):
            for j in list(range(2, n_mp)) + [1, 0]:
                w_copy(h, j).start()
    x_loads = [
        pltpu.make_async_copy(src, xbuf.at[i], x_sem.at[i])
        for i, src in enumerate((x_hbm, dx_hbm))
    ]
    x_loads.append(pltpu.make_async_copy(gate_hbm, gate, small_sem.at[1]))
    for load in x_loads:
        load.start()
    for load in loads:
        load.wait()

    live = [
        jnp.where(flags[i * FRAME] > 0, 1.0, 0.0).astype(F32)
        for i in range(rows // FRAME)
    ]

    def masked(value, i):
        scale = jnp.full(value.shape, live[i], F32)
        return (value.astype(F32) * scale).astype(BF16)

    for h in range(heads):
        for i in range(rows // FRAME):
            part = slice(i * FRAME, (i + 1) * FRAME)
            tkv[h, 0, part] = masked(own[2, part, lanes(h)], i)
            tkv[h, 1, part] = masked(own[3, part, lanes(h)], i)
        if h == 0:
            send_own(0, (2, 3))
            for g in range(1, heads):
                send_own(g, (0, 1))
        else:
            send_own(h, (2, 3))
    for h in range(heads):
        for i in range(rows // FRAME):
            part = slice(i * FRAME, (i + 1) * FRAME)
            qcat[h, part, 0:HD] = masked(own[5, part, lanes(h)], i)
        qcat[h, :, HD : 2 * HD] = own[4, :, lanes(h)]

    def attend(h, k, tk, values, first):
        queries = qcat[h, :, HD : 2 * HD]
        scores = dot_nt(queries, k)
        d_scores = dot_nt(qcat[h], jnp.concatenate([k, tk], axis=1)) * factor
        peak = jnp.max(scores, axis=1, keepdims=True)
        if not first:
            peak_old = m_s[h]
            peak = jnp.maximum(peak_old, peak)
            rescale = jnp.exp((peak_old - peak) * factor)
        weights = jnp.exp((scores - peak) * factor)
        product = weights * d_scores
        total = jnp.sum(weights, axis=1, keepdims=True)
        slope = jnp.sum(product, axis=1, keepdims=True)
        weights_b = weights.astype(BF16)
        product_b = product.astype(BF16)
        v, tv = values()
        primal = dot_nn(weights_b, v)
        tangent = dot_nn(product_b, v) + dot_nn(weights_b, tv)
        m_s[h] = peak
        if first:
            l_s[h] = total
            c_s[h] = slope
            a_s[h] = primal
            g_s[h] = tangent
        else:
            l_s[h] = l_s[h] * rescale + total
            c_s[h] = c_s[h] * rescale + slope
            a_s[h] = a_s[h] * rescale + primal
            g_s[h] = g_s[h] * rescale + tangent

    def finish(h):
        inverse = 1.0 / l_s[h]
        outputs = a_s[h] * inverse
        d_outputs = g_s[h] * inverse - (c_s[h] * inverse) * outputs
        ao[h, 0, 0:rows] = outputs.astype(BF16)
        ao[h, 0, rows : 2 * rows] = d_outputs.astype(BF16)
        for j in list(range(2, n_mp, 2)) + [1]:
            ao_copy(h, j).start()

    def relay(h):
        for j in range(2, n_mp, 2):
            ao_copy(h, j).wait_recv()
            ao_copy(h, j + 1).start()

    for h in range(heads):
        attend(
            h, own[0, :, lanes(h)], tkv[h, 0], lambda: (own[1, :, lanes(h)], tkv[h, 1]), True
        )
    for s in range(1, half):
        for h in range(heads):
            for p in range(4):
                for d in (0, 1):
                    kv_copy(h, d, s, p).wait_recv()
                    if exists(d, s + 1, p):
                        kv_copy(h, d, s + 1, p).start()
            attend(
                h,
                kv[h, s - 1, 0],
                kv[h, s - 1, 2],
                lambda: (kv[h, s - 1, 1], kv[h, s - 1, 3]),
                False,
            )
    for h in range(heads):
        def opposite(first_p, second_p):
            kv_copy(h, 0, half, first_p).wait_recv()
            kv_copy(h, 1, half, second_p).wait_recv()
            return opp[h, first_p], opp[h, second_p]

        keys, d_keys = opposite(0, 2)
        attend(h, keys, d_keys, lambda: opposite(1, 3), False)
        finish(h)

    step = 2 * HD if cols % (2 * HD) == 0 else cols
    chunks = [slice(c, c + step) for c in range(0, cols, step)]

    def w_part(h, j, chunk):
        part = slice(h * HD, (h + 1) * HD)
        if move_w:
            return wbuf[j, part, chunk]
        return w_hbm[peers[j], part, chunk]

    def project(slots, chunk):
        attn = jnp.concatenate([ao[h, j] for h, j in slots], axis=1)
        weight = jnp.concatenate([w_part(h, j, chunk) for h, j in slots], axis=0)
        return dot_nn(attn, weight)

    if move_w:
        for h in range(heads):
            w_copy(h, 0).wait()
            for j in range(1, n_mp):
                w_copy(h, j).wait_recv()
    for load in x_loads:
        load.wait()
    last = heads - 1
    for h in range(heads):
        ao_copy(h, 1).wait_recv()
    near = [(h, j) for h in range(heads) for j in (0, 1)]
    for chunk in chunks:
        acc[:, chunk] = project(near, chunk)
    for h in range(last):
        relay(h)
    for h in range(last):
        for j in range(3, n_mp, 2):
            ao_copy(h, j).wait_recv()
    far = [(h, j) for h in range(last) for j in range(2, n_mp)]
    for chunk in chunks:
        acc[:, chunk] += project(far, chunk)
    for h in range(heads):
        for s in range(1, half + 1):
            for p in range(4):
                for d in (0, 1):
                    if exists(d, s, p):
                        kv_copy(h, d, s, p).wait_send()
        if move_w:
            for j in range(1, n_mp):
                w_copy(h, j).wait_send()
    relay(last)
    even = [(last, j) for j in range(2, n_mp, 2)]
    for chunk in chunks:
        acc[:, chunk] += project(even, chunk)
    for j in range(3, n_mp, 2):
        ao_copy(last, j).wait_recv()
    odd = [(last, j) for j in range(3, n_mp, 2)]
    for chunk in chunks:
        part = acc[:, chunk] + project(odd, chunk)
        scale = gate[chunk].reshape(1, step)
        out[:, chunk] = (xbuf[0, :, chunk].astype(F32) + scale * part[0:rows]).astype(BF16)
        for i in range(rows // FRAME):
            piece = slice(i * FRAME, (i + 1) * FRAME)
            base = xbuf[1, piece, chunk].astype(F32)
            base = base * jnp.full(base.shape, live[i], F32)
            delta = part[rows + i * FRAME : rows + (i + 1) * FRAME]
            d_out[piece, chunk] = (base + scale * delta).astype(BF16)

    for h in range(heads):
        for j in range(1, n_mp):
            ao_copy(h, j).wait_send()


def per_device(n, n_mp, q, dq, k, v, dk, dv, flags, w, gate, x, dx):
    rows, width = q.shape
    cols = x.shape[1]
    heads = width // HD
    half = n // 2
    move_w = cols % HD == 0
    if not move_w:
        w = lax.all_to_all(w, "mp", split_axis=1, concat_axis=0, tiled=True)
        w = w.reshape(n_mp, width, cols)
    anywhere = pl.BlockSpec(memory_space=pl.ANY)
    vmem = pl.BlockSpec(memory_space=pltpu.VMEM)
    dma = pltpu.SemaphoreType.DMA
    return pl.pallas_call(
        functools.partial(fused, n, n_mp, move_w),
        out_shape=(pltpu.VMEM(x.shape, BF16), pltpu.VMEM(x.shape, BF16)),
        in_specs=[anywhere] * 6
        + [anywhere, anywhere if move_w else vmem, anywhere]
        + [anywhere] * 2,
        out_specs=(vmem, vmem),
        scratch_shapes=[
            pltpu.VMEM((6, rows, width), BF16),
            pltpu.VMEM((heads, rows, 2 * HD), BF16),
            pltpu.VMEM((heads, 2, rows, HD), BF16),
            pltpu.VMEM((heads, half - 1, 4, 2 * rows, HD), BF16),
            pltpu.VMEM((heads, 4, rows, HD), BF16),
            pltpu.VMEM((heads, rows, 1), F32),
            pltpu.VMEM((heads, rows, 1), F32),
            pltpu.VMEM((heads, rows, 1), F32),
            pltpu.VMEM((heads, rows, HD), F32),
            pltpu.VMEM((heads, rows, HD), F32),
            pltpu.VMEM((heads, n_mp, 2 * rows, HD), BF16),
            pltpu.VMEM((n_mp, width, cols) if move_w else (1, 16, HD), BF16),
            pltpu.VMEM((2 * rows, cols), F32),
            pltpu.VMEM((2, rows, cols), BF16),
            pltpu.SMEM((rows,), jnp.int32),
            pltpu.VMEM((cols,), F32),
            dma((6,)),
            dma((2,)),
            dma((2,)),
            dma((heads,)),
            dma((heads, 2, half, 4)),
            dma((heads, 2, half, 4)),
            dma((heads, n_mp)),
            dma((heads, n_mp)),
            dma((heads, n_mp)),
            dma((heads, n_mp)),
        ],
        compiler_params=pltpu.CompilerParams(
            collective_id=0, has_side_effects=True, vmem_limit_bytes=65000000
        ),
    )(q, dq, k, v, dk, dv, flags, w, gate, x, dx)


def gathered(
    n,
    n_mp,
    q_hbm,
    dq_hbm,
    k_hbm,
    v_hbm,
    dk_hbm,
    dv_hbm,
    flags_hbm,
    w_hbm,
    gate_hbm,
    x_hbm,
    dx_hbm,
    out,
    d_out,
    own,
    qpack,
    pack,
    qpeer,
    peer,
    qcat,
    kv,
    m_s,
    l_s,
    c_s,
    a_s,
    g_s,
    res,
    ao,
    wbuf,
    acc,
    xbuf,
    flags,
    gate,
    raw_sem,
    x_sem,
    small_sem,
    w_local,
    qr,
    zs,
    kr,
    pr,
    fs,
    wts,
    wtr,
    wxs,
    wxr,
    wys,
    wyr,
    rs,
    rr,
    as_,
    ar,
):
    rows, width = q_hbm.shape
    heads = width // HD
    cols = out.shape[1]
    t = lax.axis_index("tm")
    m = lax.axis_index("mp")
    z, y = t // 2, t % 2
    plane, core = m // 2, m % 2
    side = z // 2
    role = jnp.where(side == 0, 1 - z % 2, z % 2)
    home = role == 0
    straight = y == core
    itself = jnp.logical_and(home, straight)

    def chip(side_, role_):
        return 2 * side_ + jnp.where(side_ == 0, 1 - role_, role_)

    order = (side, 1 - side)
    homes = [(2 * chip(h, 0) + core, 2 * plane + y) for h in order]
    sources = [
        (2 * chip((side + g // 2) % 2, g % 2) + core, 2 * plane + y) for g in range(4)
    ]
    twin = (t, 2 * plane + 1 - core)
    across = (t, 2 * (1 - plane) + core)
    diagonal = (t, 2 * (1 - plane) + 1 - core)
    row_peer = (2 * z + 1 - y, m)
    factor = 1.0 / math.sqrt(HD)
    power = factor * math.log2(math.e)

    def lanes(h):
        return slice(h * HD, (h + 1) * HD)

    def both(flag, yes, no):
        pl.when(flag)(yes)
        pl.when(jnp.logical_not(flag))(no)

    def unless(flag, no):
        pl.when(jnp.logical_not(flag))(no)

    barrier = pltpu.get_barrier_semaphore()

    def greet(dev):
        pl.semaphore_signal(barrier, inc=1, device_id=dev, device_id_type=MESH)

    greet(homes[1])
    unless(itself, lambda: greet(homes[0]))

    @pl.when(home)
    def _():
        for i in (3, 2, 1):
            greet(sources[i])
        unless(itself, lambda: greet(sources[0]))

    @pl.when(straight)
    def _():
        for h in order:
            greet((2 * chip(h, 0) + y, 2 * plane + 1 - y))

    @pl.when(jnp.logical_and(home, jnp.logical_not(straight)))
    def _():
        for g in range(4):
            greet((2 * chip((side + g // 2) % 2, g % 2) + y, 2 * plane + y))

    for dev in (across, diagonal, row_peer, twin):
        greet(dev)

    loads = [
        pltpu.make_async_copy(src, own.at[i], raw_sem)
        for i, src in enumerate((dq_hbm, dk_hbm, dv_hbm))
    ]
    flags_load = pltpu.make_async_copy(flags_hbm, flags, small_sem.at[0])
    raw = []

    def done(ref, sem):
        pltpu.make_async_copy(ref, ref, sem).wait()

    for j in range(heads):
        for i, (src, dst) in enumerate(
            (
                (q_hbm, qpack.at[j, :, HD : 2 * HD]),
                (k_hbm, pack.at[j, 0]),
                (v_hbm, pack.at[j, 2]),
            )
        ):
            raw.append(
                pltpu.make_async_copy(src.at[:, lanes(j)], dst, raw_sem)
            )
    flags_load.start()
    for load in loads + raw:
        load.start()
    flags_load.wait()
    done(kv.at[0:4, 0:3], raw_sem)

    live = [
        jnp.where(flags[i * FRAME] > 0, 1.0, 0.0).astype(F32)
        for i in range(rows // FRAME)
    ]

    def masked(value, i):
        scale = jnp.full(value.shape, live[i], F32)
        return (value.astype(F32) * scale).astype(BF16)

    for h in range(heads):
        for i in range(rows // FRAME):
            piece = slice(i * FRAME, (i + 1) * FRAME)
            qpack[h, piece, 0:HD] = masked(own[0, piece, lanes(h)], i)
            pack[h, 1, piece] = masked(own[1, piece, lanes(h)], i)
            pack[h, 3, piece] = masked(own[2, piece, lanes(h)], i)
    pl.semaphore_wait(
        barrier,
        4 + heads + 4 * home.astype(jnp.int32) - 2 * itself.astype(jnp.int32)
        + 2 * straight.astype(jnp.int32)
        + 4 * (home.astype(jnp.int32) - itself.astype(jnp.int32)),
    )

    def remote(ends, send_sem, dev):
        src, dst, sem = ends
        return pltpu.make_async_remote_copy(
            src_ref=src,
            dst_ref=dst,
            send_sem=send_sem,
            recv_sem=sem,
            device_id=dev,
            device_id_type=MESH,
        )

    def home_ends(o, piece, relayed=False):
        h = order[o]
        g = 2 * o + role
        if piece == 0:
            return (qpeer.at[o] if relayed else qpack.at[h]), qcat.at[g], qr.at[g]
        pair = slice(2 * piece - 2, 2 * piece)
        crossing = 1 if relayed else (y + core) % 2
        slot = g + 4 * crossing
        src = peer.at[o, pair] if relayed else pack.at[h, pair]
        return src, kv.at[pair, slot], kr.at[piece - 1, slot]

    def home_copy(o, piece):
        return remote(home_ends(o, piece), zs, homes[o])

    def home_all(o):
        for piece in range(3):
            home_copy(o, piece).start()

    def home_local():
        for piece in range(3):
            pltpu.make_async_copy(*home_ends(0, piece)).start()

    def peer_copy(o, piece):
        h = order[o]
        if piece == 0:
            ends = (qpack.at[h], qpeer.at[o], pr.at[o, piece])
        else:
            pair = slice(2 * piece - 2, 2 * piece)
            ends = (pack.at[h, pair], peer.at[o, pair], pr.at[o, piece])
        return remote(ends, zs, row_peer)

    def peer_all(o):
        for piece in range(3):
            peer_copy(o, piece).start()

    def onward(o, piece):
        dev = (2 * chip(order[o], 0) + y, 2 * plane + 1 - y)
        return remote(home_ends(o, piece, True), zs, dev)

    def relay(o):
        for piece in range(3):
            peer_copy(o, piece).wait_recv()
            onward(o, piece).start()

    def straight_sends():
        both(itself, home_local, lambda: home_all(0))
        home_all(1)

    def crossing_sends():
        def middle():
            peer_all(1)
            home_all(0)

        def end():
            peer_all(0)
            peer_all(1)

        both(home, middle, end)

    both(straight, straight_sends, crossing_sends)

    tile = 16
    y_rows = (width // tile * 5 // 16) * tile
    rest = slice(2 * y_rows, width)
    halves = 2 if cols % (2 * HD) == 0 else 1
    span = cols // halves

    def y_part(index):
        return pl.ds(pl.multiple_of(index * y_rows, tile), y_rows)

    def w_cols(owner, first, size):
        return pl.ds(pl.multiple_of(owner * cols + first, HD), size)

    def w_cross(slot, piece):
        dev = across if slot == 0 else diagonal
        if piece < halves:
            rows_ = y_part(y)
            first, size = piece * span, span
        else:
            rows_ = rest
            first, size = (piece - halves) * span, span
        return remote(
            (
                w_hbm.at[rows_, w_cols(dev[1], first, size)],
                wbuf.at[2 + slot, rows_, pl.ds(first, size)],
                wxr.at[2 * piece + slot if piece < halves else 2 * halves],
            ),
            wxs,
            dev,
        )

    def w_row(slot, piece):
        ref = wbuf.at[2 + slot, y_part(y), pl.ds(piece * span, span)]
        return remote((ref, ref, wyr), wys, row_peer)

    def w_row_relay(piece):
        for slot in range(2):
            w_cross(slot, piece).wait_recv()
            w_row(slot, piece).start()

    w_twin = remote(
        (w_hbm.at[:, w_cols(twin[1], 0, cols)], wbuf.at[1], wtr), wts, twin
    )
    w_own = pltpu.make_async_copy(w_hbm.at[:, w_cols(m, 0, cols)], wbuf.at[0], w_local)

    for piece in range(2 * halves):
        for slot in range(2):
            w_cross(slot, piece).start()
    w_twin.start()
    w_own.start()
    x_loads = [
        pltpu.make_async_copy(src, xbuf.at[i], x_sem)
        for i, src in enumerate((x_hbm, dx_hbm))
    ]
    gate_load = pltpu.make_async_copy(gate_hbm, gate, small_sem.at[1])
    for load in x_loads:
        load.start()
    gate_load.start()

    mine_at = 4 * ((y + core) % 2)
    twins_at = 4 - mine_at

    def to_twin(pair, g):
        ref = kv.at[2 * pair : 2 * pair + 2, g + mine_at]
        return remote((ref, ref, kr.at[pair, g + mine_at]), fs, twin)

    def kv_wait(pair, slot):
        ref = kv.at[2 * pair : 2 * pair + 2, slot]
        pltpu.make_async_copy(ref, ref, kr.at[pair, slot]).wait()

    def arrive(g):
        for pair in range(2):
            kv_wait(pair, g + mine_at)
            to_twin(pair, g).start()

    def from_twin(g):
        for pair in range(2):
            kv_wait(pair, g + twins_at)

    def q_wait(i):
        pltpu.make_async_copy(qcat.at[i], qcat.at[i], qr.at[i]).wait()

    def attend(blocks, queries):
        first = blocks[0] == 0
        last = blocks[1] == 8
        keys = (blocks[1] - blocks[0]) * rows
        count = (queries[1] - queries[0]) * rows
        at = slice(queries[0] * rows, queries[1] * rows)

        def spread(column):
            return jnp.broadcast_to(column, (count, HD))

        k, tk, v, tv = (
            kv[p, blocks[0] : blocks[1]].reshape(keys, HD) for p in range(4)
        )
        q = qcat[queries[0] : queries[1]].reshape(count, 2 * HD)
        scores = dot_nt(q[:, HD : 2 * HD], k)
        d_scores = dot_nt(q, jnp.concatenate([k, tk], axis=1))
        peak = spread(jnp.max(scores, axis=1, keepdims=True))
        if not first:
            peak_old = m_s[at]
            peak = jnp.maximum(peak_old, peak)
            rescale = jnp.exp2((peak_old - peak) * power)
        weights = jnp.exp2((scores - jnp.tile(peak, (1, keys // HD))) * power)
        product = weights * d_scores
        total = spread(jnp.sum(weights, axis=1, keepdims=True))
        slope = spread(jnp.sum(product, axis=1, keepdims=True))
        weights_b = weights.astype(BF16)
        product_b = product.astype(BF16)
        wide = dot_nn(weights_b, jnp.concatenate([v, tv], axis=1))
        primal = wide[:, 0:HD]
        tangent = dot_nn(product_b, v) * factor + wide[:, HD : 2 * HD]
        if not first:
            total = l_s[at] * rescale + total
            slope = c_s[at] * rescale + slope
            primal = a_s[at] * rescale + primal
            tangent = g_s[at] * rescale + tangent
        if last:
            inverse = 1.0 / total
            outputs = primal * inverse
            d_outputs = tangent * inverse - (slope * (factor * inverse)) * outputs
            for i in range(*queries):
                own_rows = slice((i - queries[0]) * rows, (i - queries[0] + 1) * rows)
                res[i, 0] = outputs[own_rows].astype(BF16)
                res[i, 1] = d_outputs[own_rows].astype(BF16)
        else:
            m_s[at] = peak
            l_s[at] = total
            c_s[at] = slope
            a_s[at] = primal
            g_s[at] = tangent

    def part_of(p):
        half = rows // 2
        return p // 2, slice(p % 2 * half, (p % 2 + 1) * half)

    def res_ends(i, p):
        return (
            res.at[i, *part_of(p)],
            ao.at[side, 0, *part_of(p)],
            rr.at[side, p],
        )

    def res_remote(i, p):
        return remote(res_ends(i, p), rs, sources[i])

    def res_start(i, p):
        def local():
            pltpu.make_async_copy(*res_ends(i, p)).start()

        def away():
            res_remote(i, p).start()

        if i == 0:
            both(itself, local, away)
        else:
            away()

    @pl.when(home)
    def _():
        def nothing(g):
            pass

        def each(groups, on_straight, on_crossing):
            for g in groups:
                both(straight, lambda: on_straight(g), lambda: on_crossing(g))

        pl.when(straight)(lambda: relay(1))
        unless(straight, lambda: arrive(0))
        each((0, 1), arrive, from_twin)
        w_row_relay(0)
        each((2, 3), arrive, from_twin)
        q_wait(0)
        q_wait(1)
        attend((0, 4), (0, 2))
        each((0,), from_twin, nothing)
        each((1,), from_twin, arrive)
        attend((4, 6), (0, 2))
        for piece in range(1, halves):
            w_row_relay(piece)
        q_wait(2)
        q_wait(3)
        attend((0, 6), (2, 4))
        each((2, 3), from_twin, arrive)
        for queries in ((2, 4), (0, 2)):
            attend((6, 8), queries)
            for p in range(4):
                for i in range(queries[1] - 1, queries[0] - 1, -1):
                    res_start(i, p)

    @pl.when(jnp.logical_not(home))
    def _():
        @pl.when(straight)
        def _():
            relay(0)
            relay(1)

        for piece in range(halves):
            w_row_relay(piece)

    def ao_copy(h, j, p):
        src = ao.at[h, 2 if j == 3 else 0, *part_of(p)]
        dst = ao.at[h, j, *part_of(p)]
        dev = across if j == 2 else twin
        at = 4 + 4 * h + p if j == 2 else j - 1 + p // 2
        return remote((src, dst, ar.at[at]), as_, dev)

    def own_heads(h, p):
        done(ao.at[h, 0, *part_of(p)], rr.at[h, p])
        ao_copy(h, 2, p).start()
        ao_copy(h, 1, p).start()

    def cross_heads(h, p):
        ao_copy(h, 2, p).wait_recv()
        ao_copy(h, 3, p).start()

    step = 2 * HD if cols % (2 * HD) == 0 else cols
    chunks = [slice(c, c + step) for c in range(0, cols, step)]

    def project(slots, a, chunk):
        attn = jnp.concatenate([ao[heads_[h], j, a] for h, j in slots], axis=1)
        weight = jnp.concatenate([wbuf[j, w_rows[h], chunk] for h, j in slots], axis=0)
        return dot_nn(attn, weight)

    heads_ = (side, 1 - side)
    w_rows = [pl.ds(pl.multiple_of(h * HD, HD), HD) for h in heads_]
    def in_turn(take, lo, hi):
        def middle():
            for at in range(lo, hi):
                take((side, 1 - side)[at // 4], at % 4)

        def end():
            for at in range(lo, hi):
                take((1 - side, side)[at % 2], at // 2)

        both(home, middle, end)


    def own_plane(a):
        done(ao.at[:, 1, a], ar.at[a])
        for chunk in chunks:
            acc[a, :, chunk] = project([(0, 0), (0, 1), (1, 0), (1, 1)], a, chunk)

    def other_plane(a, result):
        done(ao.at[:, 3, a], ar.at[2 + a])
        slots = [(0, 2), (0, 3), (1, 2), (1, 3)]
        for chunk in chunks:
            total = acc[a, :, chunk] + project(slots, a, chunk)
            scale = gate[chunk].reshape(1, step)
            base = xbuf[a, :, chunk].astype(F32)
            result[:, chunk] = (base + scale * total).astype(BF16)

    w_own.wait()
    w_twin.wait_recv()
    done(xbuf, x_sem)
    gate_load.wait()
    for i in range(rows // FRAME):
        piece = slice(i * FRAME, (i + 1) * FRAME)
        xbuf[1, piece] = masked(xbuf[1, piece], i)
    in_turn(own_heads, 0, 8)
    own_plane(0)
    done(wbuf.at[2:4, rest], wxr.at[2 * halves])
    done(wbuf.at[2:4, y_part(1 - y)], wyr)
    both(
        jnp.logical_and(straight, jnp.logical_not(home)),
        lambda: done(kv.at[0:4, 0:6], zs),
        lambda: done(kv.at[0:2, 0:6], zs),
    )
    done(wbuf.at[0:2, 0 : width - y_rows], wxs)
    done(wbuf.at[2:4, y_part(y)], wys)
    w_twin.wait_send()

    @pl.when(home)
    def _():
        done(kv.at[0:2, 0:8], fs)

    in_turn(cross_heads, 0, 4)
    own_plane(1)
    in_turn(cross_heads, 4, 8)
    @pl.when(home)
    def _():
        both(itself, lambda: done(res.at[0:3], rs), lambda: done(res, rs))

    other_plane(0, out)
    other_plane(1, d_out)

    done(ao.at[:, 1:n_mp], as_)


def store(a_ref, b_ref, a_hbm, b_hbm, sems):
    copies = [
        pltpu.make_async_copy(a_ref, a_hbm, sems.at[0]),
        pltpu.make_async_copy(b_ref, b_hbm, sems.at[1]),
    ]
    for copy in copies:
        copy.start()
    for copy in copies:
        copy.wait()


def gathered_call(n, n_mp, q, dq, k, v, dk, dv, flags, w, gate, x, dx):
    rows, width = q.shape
    cols = x.shape[1]
    heads = width // HD
    halves = 2 if cols % (2 * HD) == 0 else 1
    anywhere = pl.BlockSpec(memory_space=pl.ANY)
    vmem = pl.BlockSpec(memory_space=pltpu.VMEM)
    dma = pltpu.SemaphoreType.DMA
    results = pl.pallas_call(
        functools.partial(gathered, n, n_mp),
        out_shape=(pltpu.VMEM(x.shape, BF16), pltpu.VMEM(x.shape, BF16)),
        in_specs=[anywhere] * 11,
        out_specs=(vmem, vmem),
        scratch_shapes=[
            pltpu.VMEM((3, rows, width), BF16),
            pltpu.VMEM((heads, rows, 2 * HD), BF16),
            pltpu.VMEM((heads, 4, rows, HD), BF16),
            pltpu.VMEM((heads, rows, 2 * HD), BF16),
            pltpu.VMEM((heads, 4, rows, HD), BF16),
            pltpu.VMEM((4, rows, 2 * HD), BF16),
            pltpu.VMEM((4, 8, rows, HD), BF16),
            pltpu.VMEM((4 * rows, HD), F32),
            pltpu.VMEM((4 * rows, HD), F32),
            pltpu.VMEM((4 * rows, HD), F32),
            pltpu.VMEM((4 * rows, HD), F32),
            pltpu.VMEM((4 * rows, HD), F32),
            pltpu.VMEM((4, 2, rows, HD), BF16),
            pltpu.VMEM((heads, n_mp, 2, rows, HD), BF16),
            pltpu.VMEM((n_mp, width, cols), BF16),
            pltpu.VMEM((2, rows, cols), F32),
            pltpu.VMEM((2, rows, cols), BF16),
            pltpu.SMEM((rows,), jnp.int32),
            pltpu.VMEM((cols,), F32),
            dma,
            dma,
            dma((2,)),
            dma,
            dma((4,)),
            dma,
            dma((2, 8)),
            dma((heads, 3)),
            dma,
            dma,
            dma,
            dma,
            dma((2 * halves + 1,)),
            dma,
            dma,
            dma,
            dma((heads, 4)),
            dma,
            dma((12,)),
        ],
        compiler_params=pltpu.CompilerParams(
            collective_id=0, has_side_effects=True, vmem_limit_bytes=65000000
        ),
    )(q, dq, k, v, dk, dv, flags, w, gate, x, dx)
    whole = jax.ShapeDtypeStruct(x.shape, BF16)
    return pl.pallas_call(
        store,
        out_shape=(whole, whole),
        in_specs=[vmem, vmem],
        out_specs=(anywhere, anywhere),
        scratch_shapes=[dma((2,))],
    )(*(pltpu.with_memory_space_constraint(r, pltpu.VMEM) for r in results))


def gathers(n, n_mp, q, x):
    heads = q.shape[1] // HD
    return (
        n_mp == 4
        and n == 8
        and heads == 2
        and x.shape[1] % HD == 0
        and q.shape[0] % FRAME == 0
    )


def program(n, n_mp, q, dq, k, v, dk, dv, flags, w, gate, x, dx):
    call = gathered_call if gathers(n, n_mp, q, x) else per_device
    return call(n, n_mp, q, dq, k, v, dk, dv, flags, w, gate, x, dx)


def solution(mesh):
    both = P("tm", "mp")
    placed = (both,) * 6 + (P("tm"), P("mp", None), P("mp"), both, both)
    return jax.shard_map(
        functools.partial(program, mesh.shape["tm"], mesh.shape["mp"]),
        mesh=mesh,
        in_specs=placed,
        out_specs=(both, both),
        check_vma=False,
    )
```

```python
import functools
import math

import jax
import jax.numpy as jnp
from jax import lax
from jax.experimental import pallas as pl
from jax.experimental.pallas import tpu as pltpu
from jax.sharding import PartitionSpec as P

HD = 128
FRAME = 32
MESH = pl.DeviceIdType.MESH
F32 = jnp.float32
BF16 = jnp.bfloat16


def ring_place(t, n):
    return jnp.where(t % 2 == 0, t // 2, n - 1 - t // 2)


def ring_member(r, n):
    return jnp.where(r < n // 2, 2 * r, 2 * (n - 1 - r) + 1)


def flipped(me, j):
    other = me
    bit = 1
    while bit <= j:
        if j & bit:
            other = other + bit * (1 - 2 * ((me // bit) % 2))
        bit *= 2
    return other


def dot_nt(a, b):
    return lax.dot_general(a, b, (((1,), (1,)), ((), ())), preferred_element_type=F32)


def dot_nn(a, b):
    return lax.dot_general(a, b, (((1,), (0,)), ((), ())), preferred_element_type=F32)


def fused(
    n,
    n_mp,
    move_w,
    q_hbm,
    dq_hbm,
    k_hbm,
    v_hbm,
    dk_hbm,
    dv_hbm,
    flags_hbm,
    w_hbm,
    gate_hbm,
    x_hbm,
    dx_hbm,
    out,
    d_out,
    own,
    qcat,
    tkv,
    kv,
    opp,
    m_s,
    l_s,
    c_s,
    a_s,
    g_s,
    ao,
    wbuf,
    acc,
    xbuf,
    flags,
    gate,
    own_sem,
    x_sem,
    small_sem,
    w_local,
    ks,
    kr,
    ws,
    wr,
    as_,
    ar,
):
    rows, width = q_hbm.shape
    heads = width // HD
    cols = out.shape[1]
    half = n // 2
    t = lax.axis_index("tm")
    m = lax.axis_index("mp")
    place = ring_place(t, n)
    right = ring_member((place + 1) % n, n)
    left = ring_member((place + n - 1) % n, n)
    peers = [flipped(m, j) for j in range(n_mp)]
    factor = 1.0 / math.sqrt(HD)

    def lanes(h):
        return slice(h * HD, (h + 1) * HD)

    loads = [
        pltpu.make_async_copy(src, own.at[i], own_sem.at[i])
        for i, src in enumerate((k_hbm, v_hbm, dk_hbm, dv_hbm, q_hbm, dq_hbm))
    ]
    loads.append(pltpu.make_async_copy(flags_hbm, flags, small_sem.at[0]))
    for load in loads:
        load.start()

    barrier = pltpu.get_barrier_semaphore()
    for dev in [(right, m), (left, m)] + [(t, peers[j]) for j in range(1, n_mp)]:
        pl.semaphore_signal(barrier, inc=1, device_id=dev, device_id_type=MESH)
    pl.semaphore_wait(barrier, 1 + n_mp)

    def exists(d, s, p):
        return s < half or (s == half and (p < 2) == (d == 0))

    def kv_copy(h, d, s, p):
        side = slice(d * rows, (d + 1) * rows)
        if s > 1:
            src = kv.at[h, s - 2, p, side]
        elif p < 2:
            src = (k_hbm, v_hbm)[p].at[:, lanes(h)]
        else:
            src = tkv.at[h, p - 2]
        dst = kv.at[h, s - 1, p, side] if s < half else opp.at[h, p]
        return pltpu.make_async_remote_copy(
            src_ref=src,
            dst_ref=dst,
            send_sem=ks.at[h, d, s - 1, p],
            recv_sem=kr.at[h, d, s - 1, p],
            device_id=((right, left)[d], m),
            device_id_type=MESH,
        )

    def send_own(h, pieces):
        for p in pieces:
            for d in (0, 1):
                kv_copy(h, d, 1, p).start()

    def w_copy(h, j):
        span = pl.ds(pl.multiple_of(peers[j] * cols, HD), cols)
        part = slice(h * HD, (h + 1) * HD)
        if j == 0:
            return pltpu.make_async_copy(
                w_hbm.at[part, span], wbuf.at[0, part], w_local.at[h]
            )
        return pltpu.make_async_remote_copy(
            src_ref=w_hbm.at[part, span],
            dst_ref=wbuf.at[j, part],
            send_sem=ws.at[h, j],
            recv_sem=wr.at[h, j],
            device_id=(t, peers[j]),
            device_id_type=MESH,
        )

    def ao_copy(h, j):
        relay = j % 2 == 1 and j > 1
        return pltpu.make_async_remote_copy(
            src_ref=ao.at[h, j - 1 if relay else 0],
            dst_ref=ao.at[h, j],
            send_sem=as_.at[h, j],
            recv_sem=ar.at[h, j],
            device_id=(t, peers[1] if relay else peers[j]),
            device_id_type=MESH,
        )

    send_own(0, (0, 1))
    if move_w:
        for h in range(heads):
            for j in list(range(2, n_mp)) + [1, 0]:
                w_copy(h, j).start()
    x_loads = [
        pltpu.make_async_copy(src, xbuf.at[i], x_sem.at[i])
        for i, src in enumerate((x_hbm, dx_hbm))
    ]
    x_loads.append(pltpu.make_async_copy(gate_hbm, gate, small_sem.at[1]))
    for load in x_loads:
        load.start()
    for load in loads:
        load.wait()

    live = [
        jnp.where(flags[i * FRAME] > 0, 1.0, 0.0).astype(F32)
        for i in range(rows // FRAME)
    ]

    def masked(value, i):
        scale = jnp.full(value.shape, live[i], F32)
        return (value.astype(F32) * scale).astype(BF16)

    for h in range(heads):
        for i in range(rows // FRAME):
            part = slice(i * FRAME, (i + 1) * FRAME)
            tkv[h, 0, part] = masked(own[2, part, lanes(h)], i)
            tkv[h, 1, part] = masked(own[3, part, lanes(h)], i)
        if h == 0:
            send_own(0, (2, 3))
            for g in range(1, heads):
                send_own(g, (0, 1))
        else:
            send_own(h, (2, 3))
    for h in range(heads):
        for i in range(rows // FRAME):
            part = slice(i * FRAME, (i + 1) * FRAME)
            qcat[h, part, 0:HD] = masked(own[5, part, lanes(h)], i)
        qcat[h, :, HD : 2 * HD] = own[4, :, lanes(h)]

    def attend(h, k, tk, values, first):
        queries = qcat[h, :, HD : 2 * HD]
        scores = dot_nt(queries, k)
        d_scores = dot_nt(qcat[h], jnp.concatenate([k, tk], axis=1)) * factor
        peak = jnp.max(scores, axis=1, keepdims=True)
        if not first:
            peak_old = m_s[h]
            peak = jnp.maximum(peak_old, peak)
            rescale = jnp.exp((peak_old - peak) * factor)
        weights = jnp.exp((scores - peak) * factor)
        product = weights * d_scores
        total = jnp.sum(weights, axis=1, keepdims=True)
        slope = jnp.sum(product, axis=1, keepdims=True)
        weights_b = weights.astype(BF16)
        product_b = product.astype(BF16)
        v, tv = values()
        primal = dot_nn(weights_b, v)
        tangent = dot_nn(product_b, v) + dot_nn(weights_b, tv)
        m_s[h] = peak
        if first:
            l_s[h] = total
            c_s[h] = slope
            a_s[h] = primal
            g_s[h] = tangent
        else:
            l_s[h] = l_s[h] * rescale + total
            c_s[h] = c_s[h] * rescale + slope
            a_s[h] = a_s[h] * rescale + primal
            g_s[h] = g_s[h] * rescale + tangent

    def finish(h):
        inverse = 1.0 / l_s[h]
        outputs = a_s[h] * inverse
        d_outputs = g_s[h] * inverse - (c_s[h] * inverse) * outputs
        ao[h, 0, 0:rows] = outputs.astype(BF16)
        ao[h, 0, rows : 2 * rows] = d_outputs.astype(BF16)
        for j in list(range(2, n_mp, 2)) + [1]:
            ao_copy(h, j).start()

    def relay(h):
        for j in range(2, n_mp, 2):
            ao_copy(h, j).wait_recv()
            ao_copy(h, j + 1).start()

    for h in range(heads):
        attend(
            h, own[0, :, lanes(h)], tkv[h, 0], lambda: (own[1, :, lanes(h)], tkv[h, 1]), True
        )
    for s in range(1, half):
        for h in range(heads):
            for p in range(4):
                for d in (0, 1):
                    kv_copy(h, d, s, p).wait_recv()
                    if exists(d, s + 1, p):
                        kv_copy(h, d, s + 1, p).start()
            attend(
                h,
                kv[h, s - 1, 0],
                kv[h, s - 1, 2],
                lambda: (kv[h, s - 1, 1], kv[h, s - 1, 3]),
                False,
            )
    for h in range(heads):
        def opposite(first_p, second_p):
            kv_copy(h, 0, half, first_p).wait_recv()
            kv_copy(h, 1, half, second_p).wait_recv()
            return opp[h, first_p], opp[h, second_p]

        keys, d_keys = opposite(0, 2)
        attend(h, keys, d_keys, lambda: opposite(1, 3), False)
        finish(h)

    step = 2 * HD if cols % (2 * HD) == 0 else cols
    chunks = [slice(c, c + step) for c in range(0, cols, step)]

    def w_part(h, j, chunk):
        part = slice(h * HD, (h + 1) * HD)
        if move_w:
            return wbuf[j, part, chunk]
        return w_hbm[peers[j], part, chunk]

    def project(slots, chunk):
        attn = jnp.concatenate([ao[h, j] for h, j in slots], axis=1)
        weight = jnp.concatenate([w_part(h, j, chunk) for h, j in slots], axis=0)
        return dot_nn(attn, weight)

    if move_w:
        for h in range(heads):
            w_copy(h, 0).wait()
            for j in range(1, n_mp):
                w_copy(h, j).wait_recv()
    for load in x_loads:
        load.wait()
    last = heads - 1
    for h in range(heads):
        ao_copy(h, 1).wait_recv()
    near = [(h, j) for h in range(heads) for j in (0, 1)]
    for chunk in chunks:
        acc[:, chunk] = project(near, chunk)
    for h in range(last):
        relay(h)
    for h in range(last):
        for j in range(3, n_mp, 2):
            ao_copy(h, j).wait_recv()
    far = [(h, j) for h in range(last) for j in range(2, n_mp)]
    for chunk in chunks:
        acc[:, chunk] += project(far, chunk)
    for h in range(heads):
        for s in range(1, half + 1):
            for p in range(4):
                for d in (0, 1):
                    if exists(d, s, p):
                        kv_copy(h, d, s, p).wait_send()
        if move_w:
            for j in range(1, n_mp):
                w_copy(h, j).wait_send()
    relay(last)
    even = [(last, j) for j in range(2, n_mp, 2)]
    for chunk in chunks:
        acc[:, chunk] += project(even, chunk)
    for j in range(3, n_mp, 2):
        ao_copy(last, j).wait_recv()
    odd = [(last, j) for j in range(3, n_mp, 2)]
    for chunk in chunks:
        part = acc[:, chunk] + project(odd, chunk)
        scale = gate[chunk].reshape(1, step)
        out[:, chunk] = (xbuf[0, :, chunk].astype(F32) + scale * part[0:rows]).astype(BF16)
        for i in range(rows // FRAME):
            piece = slice(i * FRAME, (i + 1) * FRAME)
            base = xbuf[1, piece, chunk].astype(F32)
            base = base * jnp.full(base.shape, live[i], F32)
            delta = part[rows + i * FRAME : rows + (i + 1) * FRAME]
            d_out[piece, chunk] = (base + scale * delta).astype(BF16)

    for h in range(heads):
        for j in range(1, n_mp):
            ao_copy(h, j).wait_send()


def per_device(n, n_mp, q, dq, k, v, dk, dv, flags, w, gate, x, dx):
    rows, width = q.shape
    cols = x.shape[1]
    heads = width // HD
    half = n // 2
    move_w = cols % HD == 0
    if not move_w:
        w = lax.all_to_all(w, "mp", split_axis=1, concat_axis=0, tiled=True)
        w = w.reshape(n_mp, width, cols)
    anywhere = pl.BlockSpec(memory_space=pl.ANY)
    vmem = pl.BlockSpec(memory_space=pltpu.VMEM)
    dma = pltpu.SemaphoreType.DMA
    return pl.pallas_call(
        functools.partial(fused, n, n_mp, move_w),
        out_shape=(pltpu.VMEM(x.shape, BF16), pltpu.VMEM(x.shape, BF16)),
        in_specs=[anywhere] * 6
        + [anywhere, anywhere if move_w else vmem, anywhere]
        + [anywhere] * 2,
        out_specs=(vmem, vmem),
        scratch_shapes=[
            pltpu.VMEM((6, rows, width), BF16),
            pltpu.VMEM((heads, rows, 2 * HD), BF16),
            pltpu.VMEM((heads, 2, rows, HD), BF16),
            pltpu.VMEM((heads, half - 1, 4, 2 * rows, HD), BF16),
            pltpu.VMEM((heads, 4, rows, HD), BF16),
            pltpu.VMEM((heads, rows, 1), F32),
            pltpu.VMEM((heads, rows, 1), F32),
            pltpu.VMEM((heads, rows, 1), F32),
            pltpu.VMEM((heads, rows, HD), F32),
            pltpu.VMEM((heads, rows, HD), F32),
            pltpu.VMEM((heads, n_mp, 2 * rows, HD), BF16),
            pltpu.VMEM((n_mp, width, cols) if move_w else (1, 16, HD), BF16),
            pltpu.VMEM((2 * rows, cols), F32),
            pltpu.VMEM((2, rows, cols), BF16),
            pltpu.SMEM((rows,), jnp.int32),
            pltpu.VMEM((cols,), F32),
            dma((6,)),
            dma((2,)),
            dma((2,)),
            dma((heads,)),
            dma((heads, 2, half, 4)),
            dma((heads, 2, half, 4)),
            dma((heads, n_mp)),
            dma((heads, n_mp)),
            dma((heads, n_mp)),
            dma((heads, n_mp)),
        ],
        compiler_params=pltpu.CompilerParams(
            collective_id=0, has_side_effects=True, vmem_limit_bytes=65000000
        ),
    )(q, dq, k, v, dk, dv, flags, w, gate, x, dx)


def gathered(
    n,
    n_mp,
    q_hbm,
    dq_hbm,
    k_hbm,
    v_hbm,
    dk_hbm,
    dv_hbm,
    flags_hbm,
    w_hbm,
    gate_hbm,
    x_hbm,
    dx_hbm,
    out,
    d_out,
    own,
    qpack,
    pack,
    qpeer,
    peer,
    qcat,
    kv,
    m_s,
    l_s,
    c_s,
    a_s,
    g_s,
    res,
    ao,
    wbuf,
    acc,
    xbuf,
    flags,
    gate,
    raw_sem,
    x_sem,
    small_sem,
    w_local,
    qr,
    zs,
    kr,
    pr,
    fs,
    wts,
    wtr,
    wxs,
    wxr,
    wys,
    wyr,
    rs,
    rr,
    as_,
    ar,
):
    rows, width = q_hbm.shape
    heads = width // HD
    cols = out.shape[1]
    t = lax.axis_index("tm")
    m = lax.axis_index("mp")
    z, y = t // 2, t % 2
    plane, core = m // 2, m % 2
    side = z // 2
    role = jnp.where(side == 0, 1 - z % 2, z % 2)
    home = role == 0
    straight = y == core
    itself = jnp.logical_and(home, straight)

    def chip(side_, role_):
        return 2 * side_ + jnp.where(side_ == 0, 1 - role_, role_)

    order = (side, 1 - side)
    homes = [(2 * chip(h, 0) + core, 2 * plane + y) for h in order]
    sources = [
        (2 * chip((side + g // 2) % 2, g % 2) + core, 2 * plane + y) for g in range(4)
    ]
    twin = (t, 2 * plane + 1 - core)
    across = (t, 2 * (1 - plane) + core)
    diagonal = (t, 2 * (1 - plane) + 1 - core)
    row_peer = (2 * z + 1 - y, m)
    factor = 1.0 / math.sqrt(HD)
    power = factor * math.log2(math.e)

    def lanes(h):
        return slice(h * HD, (h + 1) * HD)

    def both(flag, yes, no):
        pl.when(flag)(yes)
        pl.when(jnp.logical_not(flag))(no)

    def unless(flag, no):
        pl.when(jnp.logical_not(flag))(no)

    barrier = pltpu.get_barrier_semaphore()

    def greet(dev):
        pl.semaphore_signal(barrier, inc=1, device_id=dev, device_id_type=MESH)

    greet(homes[1])
    unless(itself, lambda: greet(homes[0]))

    @pl.when(home)
    def _():
        for i in (3, 2, 1):
            greet(sources[i])
        unless(itself, lambda: greet(sources[0]))

    @pl.when(straight)
    def _():
        for h in order:
            greet((2 * chip(h, 0) + y, 2 * plane + 1 - y))

    @pl.when(jnp.logical_and(home, jnp.logical_not(straight)))
    def _():
        for g in range(4):
            greet((2 * chip((side + g // 2) % 2, g % 2) + y, 2 * plane + y))

    for dev in (across, diagonal, row_peer, twin):
        greet(dev)

    loads = [
        pltpu.make_async_copy(src, own.at[i], raw_sem)
        for i, src in enumerate((dq_hbm, dk_hbm, dv_hbm))
    ]
    flags_load = pltpu.make_async_copy(flags_hbm, flags, small_sem.at[0])
    raw = []

    def done(ref, sem):
        pltpu.make_async_copy(ref, ref, sem).wait()

    for j in range(heads):
        for i, (src, dst) in enumerate(
            (
                (q_hbm, qpack.at[j, :, HD : 2 * HD]),
                (k_hbm, pack.at[j, 0]),
                (v_hbm, pack.at[j, 2]),
            )
        ):
            raw.append(
                pltpu.make_async_copy(src.at[:, lanes(j)], dst, raw_sem)
            )
    flags_load.start()
    for load in loads + raw:
        load.start()
    flags_load.wait()
    done(kv.at[0:4, 0:3], raw_sem)

    live = [
        jnp.where(flags[i * FRAME] > 0, 1.0, 0.0).astype(F32)
        for i in range(rows // FRAME)
    ]

    def masked(value, i):
        scale = jnp.full(value.shape, live[i], F32)
        return (value.astype(F32) * scale).astype(BF16)

    for h in range(heads):
        for i in range(rows // FRAME):
            piece = slice(i * FRAME, (i + 1) * FRAME)
            qpack[h, piece, 0:HD] = masked(own[0, piece, lanes(h)], i)
            pack[h, 1, piece] = masked(own[1, piece, lanes(h)], i)
            pack[h, 3, piece] = masked(own[2, piece, lanes(h)], i)
    pl.semaphore_wait(
        barrier,
        4 + heads + 4 * home.astype(jnp.int32) - 2 * itself.astype(jnp.int32)
        + 2 * straight.astype(jnp.int32)
        + 4 * (home.astype(jnp.int32) - itself.astype(jnp.int32)),
    )

    def remote(ends, send_sem, dev):
        src, dst, sem = ends
        return pltpu.make_async_remote_copy(
            src_ref=src,
            dst_ref=dst,
            send_sem=send_sem,
            recv_sem=sem,
            device_id=dev,
            device_id_type=MESH,
        )

    def home_ends(o, piece, relayed=False):
        h = order[o]
        g = 2 * o + role
        if piece == 0:
            return (qpeer.at[o] if relayed else qpack.at[h]), qcat.at[g], qr.at[g]
        pair = slice(2 * piece - 2, 2 * piece)
        crossing = 1 if relayed else (y + core) % 2
        slot = g + 4 * crossing
        src = peer.at[o, pair] if relayed else pack.at[h, pair]
        return src, kv.at[pair, slot], kr.at[piece - 1, slot]

    def home_copy(o, piece):
        return remote(home_ends(o, piece), zs, homes[o])

    def home_all(o):
        for piece in range(3):
            home_copy(o, piece).start()

    def home_local():
        for piece in range(3):
            pltpu.make_async_copy(*home_ends(0, piece)).start()

    def peer_copy(o, piece):
        h = order[o]
        if piece == 0:
            ends = (qpack.at[h], qpeer.at[o], pr.at[o, piece])
        else:
            pair = slice(2 * piece - 2, 2 * piece)
            ends = (pack.at[h, pair], peer.at[o, pair], pr.at[o, piece])
        return remote(ends, zs, row_peer)

    def peer_all(o):
        for piece in range(3):
            peer_copy(o, piece).start()

    def onward(o, piece):
        dev = (2 * chip(order[o], 0) + y, 2 * plane + 1 - y)
        return remote(home_ends(o, piece, True), zs, dev)

    def relay(o):
        for piece in range(3):
            peer_copy(o, piece).wait_recv()
            onward(o, piece).start()

    def straight_sends():
        both(itself, home_local, lambda: home_all(0))
        home_all(1)

    def crossing_sends():
        def middle():
            peer_all(1)
            home_all(0)

        def end():
            peer_all(0)
            peer_all(1)

        both(home, middle, end)

    both(straight, straight_sends, crossing_sends)

    tile = 16
    y_rows = (width // tile * 5 // 16) * tile
    rest = slice(2 * y_rows, width)
    halves = 2 if cols % (2 * HD) == 0 else 1
    span = cols // halves

    def y_part(index):
        return pl.ds(pl.multiple_of(index * y_rows, tile), y_rows)

    def w_cols(owner, first, size):
        return pl.ds(pl.multiple_of(owner * cols + first, HD), size)

    def w_cross(slot, piece):
        dev = across if slot == 0 else diagonal
        if piece < halves:
            rows_ = y_part(y)
            first, size = piece * span, span
        else:
            rows_ = rest
            first, size = (piece - halves) * span, span
        return remote(
            (
                w_hbm.at[rows_, w_cols(dev[1], first, size)],
                wbuf.at[2 + slot, rows_, pl.ds(first, size)],
                wxr.at[2 * piece + slot if piece < halves else 2 * halves],
            ),
            wxs,
            dev,
        )

    def w_row(slot, piece):
        ref = wbuf.at[2 + slot, y_part(y), pl.ds(piece * span, span)]
        return remote((ref, ref, wyr), wys, row_peer)

    def w_row_relay(piece):
        for slot in range(2):
            w_cross(slot, piece).wait_recv()
            w_row(slot, piece).start()

    w_twin = remote(
        (w_hbm.at[:, w_cols(twin[1], 0, cols)], wbuf.at[1], wtr), wts, twin
    )
    w_own = pltpu.make_async_copy(w_hbm.at[:, w_cols(m, 0, cols)], wbuf.at[0], w_local)

    for piece in range(2 * halves):
        for slot in range(2):
            w_cross(slot, piece).start()
    w_twin.start()
    w_own.start()
    x_loads = [
        pltpu.make_async_copy(src, xbuf.at[i], x_sem)
        for i, src in enumerate((x_hbm, dx_hbm))
    ]
    gate_load = pltpu.make_async_copy(gate_hbm, gate, small_sem.at[1])
    for load in x_loads:
        load.start()
    gate_load.start()

    mine_at = 4 * ((y + core) % 2)
    twins_at = 4 - mine_at

    def to_twin(pair, g):
        ref = kv.at[2 * pair : 2 * pair + 2, g + mine_at]
        return remote((ref, ref, kr.at[pair, g + mine_at]), fs, twin)

    def kv_wait(pair, slot):
        ref = kv.at[2 * pair : 2 * pair + 2, slot]
        pltpu.make_async_copy(ref, ref, kr.at[pair, slot]).wait()

    def arrive(g):
        for pair in range(2):
            kv_wait(pair, g + mine_at)
            to_twin(pair, g).start()

    def from_twin(g):
        for pair in range(2):
            kv_wait(pair, g + twins_at)

    def q_wait(i):
        pltpu.make_async_copy(qcat.at[i], qcat.at[i], qr.at[i]).wait()

    def attend(blocks, queries):
        first = blocks[0] == 0
        last = blocks[1] == 8
        keys = (blocks[1] - blocks[0]) * rows
        count = (queries[1] - queries[0]) * rows
        at = slice(queries[0] * rows, queries[1] * rows)

        def spread(column):
            return jnp.broadcast_to(column, (count, HD))

        k, tk, v, tv = (
            kv[p, blocks[0] : blocks[1]].reshape(keys, HD) for p in range(4)
        )
        q = qcat[queries[0] : queries[1]].reshape(count, 2 * HD)
        scores = dot_nt(q[:, HD : 2 * HD], k)
        d_scores = dot_nt(q, jnp.concatenate([k, tk], axis=1))
        peak = spread(jnp.max(scores, axis=1, keepdims=True))
        if not first:
            peak_old = m_s[at]
            peak = jnp.maximum(peak_old, peak)
            rescale = jnp.exp2((peak_old - peak) * power)
        weights = jnp.exp2((scores - jnp.tile(peak, (1, keys // HD))) * power)
        product = weights * d_scores
        total = spread(jnp.sum(weights, axis=1, keepdims=True))
        slope = spread(jnp.sum(product, axis=1, keepdims=True))
        weights_b = weights.astype(BF16)
        product_b = product.astype(BF16)
        wide = dot_nn(weights_b, jnp.concatenate([v, tv], axis=1))
        primal = wide[:, 0:HD]
        tangent = dot_nn(product_b, v) * factor + wide[:, HD : 2 * HD]
        if not first:
            total = l_s[at] * rescale + total
            slope = c_s[at] * rescale + slope
            primal = a_s[at] * rescale + primal
            tangent = g_s[at] * rescale + tangent
        if last:
            inverse = 1.0 / total
            outputs = primal * inverse
            d_outputs = tangent * inverse - (slope * (factor * inverse)) * outputs
            for i in range(*queries):
                own_rows = slice((i - queries[0]) * rows, (i - queries[0] + 1) * rows)
                res[i, 0] = outputs[own_rows].astype(BF16)
                res[i, 1] = d_outputs[own_rows].astype(BF16)
        else:
            m_s[at] = peak
            l_s[at] = total
            c_s[at] = slope
            a_s[at] = primal
            g_s[at] = tangent

    cuts = 3 if rows % 48 == 0 else 2
    parts = 2 * cuts

    def part_of(p):
        size = rows // cuts
        return p // cuts, slice(p % cuts * size, (p % cuts + 1) * size)

    def res_ends(i, p):
        return (
            res.at[i, *part_of(p)],
            ao.at[side, 0, *part_of(p)],
            rr.at[side, p],
        )

    def res_remote(i, p):
        return remote(res_ends(i, p), rs, sources[i])

    def res_start(i, p):
        def local():
            pltpu.make_async_copy(*res_ends(i, p)).start()

        def away():
            res_remote(i, p).start()

        if i == 0:
            both(itself, local, away)
        else:
            away()

    @pl.when(home)
    def _():
        def nothing(g):
            pass

        def each(groups, on_straight, on_crossing):
            for g in groups:
                both(straight, lambda: on_straight(g), lambda: on_crossing(g))

        pl.when(straight)(lambda: relay(1))
        unless(straight, lambda: arrive(0))
        each((0, 1), arrive, from_twin)
        w_row_relay(0)
        each((2, 3), arrive, from_twin)
        q_wait(0)
        q_wait(1)
        attend((0, 4), (0, 2))
        each((0,), from_twin, nothing)
        each((1,), from_twin, arrive)
        attend((4, 6), (0, 2))
        for piece in range(1, halves):
            w_row_relay(piece)
        q_wait(2)
        q_wait(3)
        attend((0, 6), (2, 4))
        each((2, 3), from_twin, arrive)
        for queries in ((2, 4), (0, 2)):
            attend((6, 8), queries)
            for p in range(parts):
                for i in range(queries[1] - 1, queries[0] - 1, -1):
                    res_start(i, p)

    @pl.when(jnp.logical_not(home))
    def _():
        @pl.when(straight)
        def _():
            relay(0)
            relay(1)

        for piece in range(halves):
            w_row_relay(piece)

    def ao_copy(h, j, p):
        src = ao.at[h, 2 if j == 3 else 0, *part_of(p)]
        dst = ao.at[h, j, *part_of(p)]
        dev = across if j == 2 else twin
        at = 4 + parts * h + p if j == 2 else j - 1 + p // cuts
        return remote((src, dst, ar.at[at]), as_, dev)

    def own_heads(h, p):
        done(ao.at[h, 0, *part_of(p)], rr.at[h, p])
        ao_copy(h, 2, p).start()
        ao_copy(h, 1, p).start()

    def cross_heads(h, p):
        ao_copy(h, 2, p).wait_recv()
        ao_copy(h, 3, p).start()

    step = 2 * HD if cols % (2 * HD) == 0 else cols
    chunks = [slice(c, c + step) for c in range(0, cols, step)]

    def project(slots, a, chunk):
        attn = jnp.concatenate([ao[heads_[h], j, a] for h, j in slots], axis=1)
        weight = jnp.concatenate([wbuf[j, w_rows[h], chunk] for h, j in slots], axis=0)
        return dot_nn(attn, weight)

    heads_ = (side, 1 - side)
    w_rows = [pl.ds(pl.multiple_of(h * HD, HD), HD) for h in heads_]
    def in_turn(take, lo, hi):
        def middle():
            for at in range(lo, hi):
                take((side, 1 - side)[at // parts], at % parts)

        def end():
            for at in range(lo, hi):
                take((1 - side, side)[at % 2], at // 2)

        both(home, middle, end)


    def own_plane(a):
        done(ao.at[:, 1, a], ar.at[a])
        for chunk in chunks:
            acc[a, :, chunk] = project([(0, 0), (0, 1), (1, 0), (1, 1)], a, chunk)

    def other_plane(a, result):
        done(ao.at[:, 3, a], ar.at[2 + a])
        slots = [(0, 2), (0, 3), (1, 2), (1, 3)]
        for chunk in chunks:
            total = acc[a, :, chunk] + project(slots, a, chunk)
            scale = gate[chunk].reshape(1, step)
            base = xbuf[a, :, chunk].astype(F32)
            result[:, chunk] = (base + scale * total).astype(BF16)

    w_own.wait()
    w_twin.wait_recv()
    done(xbuf, x_sem)
    gate_load.wait()
    for i in range(rows // FRAME):
        piece = slice(i * FRAME, (i + 1) * FRAME)
        xbuf[1, piece] = masked(xbuf[1, piece], i)
    in_turn(own_heads, 0, 2 * parts)
    own_plane(0)
    done(wbuf.at[2:4, rest], wxr.at[2 * halves])
    done(wbuf.at[2:4, y_part(1 - y)], wyr)
    both(
        jnp.logical_and(straight, jnp.logical_not(home)),
        lambda: done(kv.at[0:4, 0:6], zs),
        lambda: done(kv.at[0:2, 0:6], zs),
    )
    done(wbuf.at[0:2, 0 : width - y_rows], wxs)
    done(wbuf.at[2:4, y_part(y)], wys)
    w_twin.wait_send()

    @pl.when(home)
    def _():
        done(kv.at[0:2, 0:8], fs)

    in_turn(cross_heads, 0, parts)
    own_plane(1)
    in_turn(cross_heads, parts, 2 * parts)
    @pl.when(home)
    def _():
        both(itself, lambda: done(res.at[0:3], rs), lambda: done(res, rs))

    other_plane(0, out)
    other_plane(1, d_out)

    done(ao.at[:, 1:n_mp], as_)


def store(a_ref, b_ref, a_hbm, b_hbm, sems):
    quarter = a_ref.shape[0] // 4
    copies = []
    for i in range(4):
        part = slice(i * quarter, (i + 1) * quarter)
        copies.append(pltpu.make_async_copy(a_ref.at[part], a_hbm.at[part], sems.at[0]))
        copies.append(pltpu.make_async_copy(b_ref.at[part], b_hbm.at[part], sems.at[1]))
    for copy in copies:
        copy.start()
    pltpu.make_async_copy(a_ref, a_hbm, sems.at[0]).wait()
    pltpu.make_async_copy(b_ref, b_hbm, sems.at[1]).wait()


def gathered_call(n, n_mp, q, dq, k, v, dk, dv, flags, w, gate, x, dx):
    rows, width = q.shape
    cols = x.shape[1]
    heads = width // HD
    halves = 2 if cols % (2 * HD) == 0 else 1
    cuts = 3 if rows % 48 == 0 else 2
    anywhere = pl.BlockSpec(memory_space=pl.ANY)
    vmem = pl.BlockSpec(memory_space=pltpu.VMEM)
    dma = pltpu.SemaphoreType.DMA
    results = pl.pallas_call(
        functools.partial(gathered, n, n_mp),
        out_shape=(pltpu.VMEM(x.shape, BF16), pltpu.VMEM(x.shape, BF16)),
        in_specs=[anywhere] * 11,
        out_specs=(vmem, vmem),
        scratch_shapes=[
            pltpu.VMEM((3, rows, width), BF16),
            pltpu.VMEM((heads, rows, 2 * HD), BF16),
            pltpu.VMEM((heads, 4, rows, HD), BF16),
            pltpu.VMEM((heads, rows, 2 * HD), BF16),
            pltpu.VMEM((heads, 4, rows, HD), BF16),
            pltpu.VMEM((4, rows, 2 * HD), BF16),
            pltpu.VMEM((4, 8, rows, HD), BF16),
            pltpu.VMEM((4 * rows, HD), F32),
            pltpu.VMEM((4 * rows, HD), F32),
            pltpu.VMEM((4 * rows, HD), F32),
            pltpu.VMEM((4 * rows, HD), F32),
            pltpu.VMEM((4 * rows, HD), F32),
            pltpu.VMEM((4, 2, rows, HD), BF16),
            pltpu.VMEM((heads, n_mp, 2, rows, HD), BF16),
            pltpu.VMEM((n_mp, width, cols), BF16),
            pltpu.VMEM((2, rows, cols), F32),
            pltpu.VMEM((2, rows, cols), BF16),
            pltpu.SMEM((rows,), jnp.int32),
            pltpu.VMEM((cols,), F32),
            dma,
            dma,
            dma((2,)),
            dma,
            dma((4,)),
            dma,
            dma((2, 8)),
            dma((heads, 3)),
            dma,
            dma,
            dma,
            dma,
            dma((2 * halves + 1,)),
            dma,
            dma,
            dma,
            dma((heads, 2 * cuts)),
            dma,
            dma((4 + 2 * cuts * heads,)),
        ],
        compiler_params=pltpu.CompilerParams(
            collective_id=0, has_side_effects=True, vmem_limit_bytes=65000000
        ),
    )(q, dq, k, v, dk, dv, flags, w, gate, x, dx)
    whole = jax.ShapeDtypeStruct(x.shape, BF16)
    return pl.pallas_call(
        store,
        out_shape=(whole, whole),
        in_specs=[vmem, vmem],
        out_specs=(anywhere, anywhere),
        scratch_shapes=[dma((2,))],
    )(*(pltpu.with_memory_space_constraint(r, pltpu.VMEM) for r in results))


def gathers(n, n_mp, q, x):
    heads = q.shape[1] // HD
    planes = cores = sides = roles = rows = 2
    return (
        n_mp == planes * cores
        and n == sides * roles * rows
        and heads == sides
        and x.shape[1] % HD == 0
        and q.shape[0] % FRAME == 0
    )


def program(n, n_mp, q, dq, k, v, dk, dv, flags, w, gate, x, dx):
    call = gathered_call if gathers(n, n_mp, q, x) else per_device
    return call(n, n_mp, q, dq, k, v, dk, dv, flags, w, gate, x, dx)


def solution(mesh):
    both = P("tm", "mp")
    placed = (both,) * 6 + (P("tm"), P("mp", None), P("mp"), both, both)
    return jax.shard_map(
        functools.partial(program, mesh.shape["tm"], mesh.shape["mp"]),
        mesh=mesh,
        in_specs=placed,
        out_specs=(both, both),
        check_vma=False,
    )
```

```python
import functools
import math

import jax
import jax.numpy as jnp
from jax import lax
from jax.experimental import pallas as pl
from jax.experimental.pallas import tpu as pltpu
from jax.sharding import PartitionSpec as P

HD = 128
FRAME = 32
MESH = pl.DeviceIdType.MESH
F32 = jnp.float32
BF16 = jnp.bfloat16


def ring_place(t, n):
    return jnp.where(t % 2 == 0, t // 2, n - 1 - t // 2)


def ring_member(r, n):
    return jnp.where(r < n // 2, 2 * r, 2 * (n - 1 - r) + 1)


def flipped(me, j):
    other = me
    bit = 1
    while bit <= j:
        if j & bit:
            other = other + bit * (1 - 2 * ((me // bit) % 2))
        bit *= 2
    return other


def dot_nt(a, b):
    return lax.dot_general(a, b, (((1,), (1,)), ((), ())), preferred_element_type=F32)


def dot_nn(a, b):
    return lax.dot_general(a, b, (((1,), (0,)), ((), ())), preferred_element_type=F32)


def fused(
    n,
    n_mp,
    move_w,
    q_hbm,
    dq_hbm,
    k_hbm,
    v_hbm,
    dk_hbm,
    dv_hbm,
    flags_hbm,
    w_hbm,
    gate_hbm,
    x_hbm,
    dx_hbm,
    out,
    d_out,
    own,
    qcat,
    tkv,
    kv,
    opp,
    m_s,
    l_s,
    c_s,
    a_s,
    g_s,
    ao,
    wbuf,
    acc,
    xbuf,
    flags,
    gate,
    own_sem,
    x_sem,
    small_sem,
    w_local,
    ks,
    kr,
    ws,
    wr,
    as_,
    ar,
):
    rows, width = q_hbm.shape
    heads = width // HD
    cols = out.shape[1]
    half = n // 2
    t = lax.axis_index("tm")
    m = lax.axis_index("mp")
    place = ring_place(t, n)
    right = ring_member((place + 1) % n, n)
    left = ring_member((place + n - 1) % n, n)
    peers = [flipped(m, j) for j in range(n_mp)]
    factor = 1.0 / math.sqrt(HD)

    def lanes(h):
        return slice(h * HD, (h + 1) * HD)

    loads = [
        pltpu.make_async_copy(src, own.at[i], own_sem.at[i])
        for i, src in enumerate((k_hbm, v_hbm, dk_hbm, dv_hbm, q_hbm, dq_hbm))
    ]
    loads.append(pltpu.make_async_copy(flags_hbm, flags, small_sem.at[0]))
    for load in loads:
        load.start()

    barrier = pltpu.get_barrier_semaphore()
    for dev in [(right, m), (left, m)] + [(t, peers[j]) for j in range(1, n_mp)]:
        pl.semaphore_signal(barrier, inc=1, device_id=dev, device_id_type=MESH)
    pl.semaphore_wait(barrier, 1 + n_mp)

    def exists(d, s, p):
        return s < half or (s == half and (p < 2) == (d == 0))

    def kv_copy(h, d, s, p):
        side = slice(d * rows, (d + 1) * rows)
        if s > 1:
            src = kv.at[h, s - 2, p, side]
        elif p < 2:
            src = (k_hbm, v_hbm)[p].at[:, lanes(h)]
        else:
            src = tkv.at[h, p - 2]
        dst = kv.at[h, s - 1, p, side] if s < half else opp.at[h, p]
        return pltpu.make_async_remote_copy(
            src_ref=src,
            dst_ref=dst,
            send_sem=ks.at[h, d, s - 1, p],
            recv_sem=kr.at[h, d, s - 1, p],
            device_id=((right, left)[d], m),
            device_id_type=MESH,
        )

    def send_own(h, pieces):
        for p in pieces:
            for d in (0, 1):
                kv_copy(h, d, 1, p).start()

    def w_copy(h, j):
        span = pl.ds(pl.multiple_of(peers[j] * cols, HD), cols)
        part = slice(h * HD, (h + 1) * HD)
        if j == 0:
            return pltpu.make_async_copy(
                w_hbm.at[part, span], wbuf.at[0, part], w_local.at[h]
            )
        return pltpu.make_async_remote_copy(
            src_ref=w_hbm.at[part, span],
            dst_ref=wbuf.at[j, part],
            send_sem=ws.at[h, j],
            recv_sem=wr.at[h, j],
            device_id=(t, peers[j]),
            device_id_type=MESH,
        )

    def ao_copy(h, j):
        relay = j % 2 == 1 and j > 1
        return pltpu.make_async_remote_copy(
            src_ref=ao.at[h, j - 1 if relay else 0],
            dst_ref=ao.at[h, j],
            send_sem=as_.at[h, j],
            recv_sem=ar.at[h, j],
            device_id=(t, peers[1] if relay else peers[j]),
            device_id_type=MESH,
        )

    send_own(0, (0, 1))
    if move_w:
        for h in range(heads):
            for j in list(range(2, n_mp)) + [1, 0]:
                w_copy(h, j).start()
    x_loads = [
        pltpu.make_async_copy(src, xbuf.at[i], x_sem.at[i])
        for i, src in enumerate((x_hbm, dx_hbm))
    ]
    x_loads.append(pltpu.make_async_copy(gate_hbm, gate, small_sem.at[1]))
    for load in x_loads:
        load.start()
    for load in loads:
        load.wait()

    live = [
        jnp.where(flags[i * FRAME] > 0, 1.0, 0.0).astype(F32)
        for i in range(rows // FRAME)
    ]

    def masked(value, i):
        scale = jnp.full(value.shape, live[i], F32)
        return (value.astype(F32) * scale).astype(BF16)

    for h in range(heads):
        for i in range(rows // FRAME):
            part = slice(i * FRAME, (i + 1) * FRAME)
            tkv[h, 0, part] = masked(own[2, part, lanes(h)], i)
            tkv[h, 1, part] = masked(own[3, part, lanes(h)], i)
        if h == 0:
            send_own(0, (2, 3))
            for g in range(1, heads):
                send_own(g, (0, 1))
        else:
            send_own(h, (2, 3))
    for h in range(heads):
        for i in range(rows // FRAME):
            part = slice(i * FRAME, (i + 1) * FRAME)
            qcat[h, part, 0:HD] = masked(own[5, part, lanes(h)], i)
        qcat[h, :, HD : 2 * HD] = own[4, :, lanes(h)]

    def attend(h, k, tk, values, first):
        queries = qcat[h, :, HD : 2 * HD]
        scores = dot_nt(queries, k)
        d_scores = dot_nt(qcat[h], jnp.concatenate([k, tk], axis=1)) * factor
        peak = jnp.max(scores, axis=1, keepdims=True)
        if not first:
            peak_old = m_s[h]
            peak = jnp.maximum(peak_old, peak)
            rescale = jnp.exp((peak_old - peak) * factor)
        weights = jnp.exp((scores - peak) * factor)
        product = weights * d_scores
        total = jnp.sum(weights, axis=1, keepdims=True)
        slope = jnp.sum(product, axis=1, keepdims=True)
        weights_b = weights.astype(BF16)
        product_b = product.astype(BF16)
        v, tv = values()
        primal = dot_nn(weights_b, v)
        tangent = dot_nn(product_b, v) + dot_nn(weights_b, tv)
        m_s[h] = peak
        if first:
            l_s[h] = total
            c_s[h] = slope
            a_s[h] = primal
            g_s[h] = tangent
        else:
            l_s[h] = l_s[h] * rescale + total
            c_s[h] = c_s[h] * rescale + slope
            a_s[h] = a_s[h] * rescale + primal
            g_s[h] = g_s[h] * rescale + tangent

    def finish(h):
        inverse = 1.0 / l_s[h]
        outputs = a_s[h] * inverse
        d_outputs = g_s[h] * inverse - (c_s[h] * inverse) * outputs
        ao[h, 0, 0:rows] = outputs.astype(BF16)
        ao[h, 0, rows : 2 * rows] = d_outputs.astype(BF16)
        for j in list(range(2, n_mp, 2)) + [1]:
            ao_copy(h, j).start()

    def relay(h):
        for j in range(2, n_mp, 2):
            ao_copy(h, j).wait_recv()
            ao_copy(h, j + 1).start()

    for h in range(heads):
        attend(
            h, own[0, :, lanes(h)], tkv[h, 0], lambda: (own[1, :, lanes(h)], tkv[h, 1]), True
        )
    for s in range(1, half):
        for h in range(heads):
            for p in range(4):
                for d in (0, 1):
                    kv_copy(h, d, s, p).wait_recv()
                    if exists(d, s + 1, p):
                        kv_copy(h, d, s + 1, p).start()
            attend(
                h,
                kv[h, s - 1, 0],
                kv[h, s - 1, 2],
                lambda: (kv[h, s - 1, 1], kv[h, s - 1, 3]),
                False,
            )
    for h in range(heads):
        def opposite(first_p, second_p):
            kv_copy(h, 0, half, first_p).wait_recv()
            kv_copy(h, 1, half, second_p).wait_recv()
            return opp[h, first_p], opp[h, second_p]

        keys, d_keys = opposite(0, 2)
        attend(h, keys, d_keys, lambda: opposite(1, 3), False)
        finish(h)

    step = 2 * HD if cols % (2 * HD) == 0 else cols
    chunks = [slice(c, c + step) for c in range(0, cols, step)]

    def w_part(h, j, chunk):
        part = slice(h * HD, (h + 1) * HD)
        if move_w:
            return wbuf[j, part, chunk]
        return w_hbm[peers[j], part, chunk]

    def project(slots, chunk):
        attn = jnp.concatenate([ao[h, j] for h, j in slots], axis=1)
        weight = jnp.concatenate([w_part(h, j, chunk) for h, j in slots], axis=0)
        return dot_nn(attn, weight)

    if move_w:
        for h in range(heads):
            w_copy(h, 0).wait()
            for j in range(1, n_mp):
                w_copy(h, j).wait_recv()
    for load in x_loads:
        load.wait()
    last = heads - 1
    for h in range(heads):
        ao_copy(h, 1).wait_recv()
    near = [(h, j) for h in range(heads) for j in (0, 1)]
    for chunk in chunks:
        acc[:, chunk] = project(near, chunk)
    for h in range(last):
        relay(h)
    for h in range(last):
        for j in range(3, n_mp, 2):
            ao_copy(h, j).wait_recv()
    far = [(h, j) for h in range(last) for j in range(2, n_mp)]
    for chunk in chunks:
        acc[:, chunk] += project(far, chunk)
    for h in range(heads):
        for s in range(1, half + 1):
            for p in range(4):
                for d in (0, 1):
                    if exists(d, s, p):
                        kv_copy(h, d, s, p).wait_send()
        if move_w:
            for j in range(1, n_mp):
                w_copy(h, j).wait_send()
    relay(last)
    even = [(last, j) for j in range(2, n_mp, 2)]
    for chunk in chunks:
        acc[:, chunk] += project(even, chunk)
    for j in range(3, n_mp, 2):
        ao_copy(last, j).wait_recv()
    odd = [(last, j) for j in range(3, n_mp, 2)]
    for chunk in chunks:
        part = acc[:, chunk] + project(odd, chunk)
        scale = gate[chunk].reshape(1, step)
        out[:, chunk] = (xbuf[0, :, chunk].astype(F32) + scale * part[0:rows]).astype(BF16)
        for i in range(rows // FRAME):
            piece = slice(i * FRAME, (i + 1) * FRAME)
            base = xbuf[1, piece, chunk].astype(F32)
            base = base * jnp.full(base.shape, live[i], F32)
            delta = part[rows + i * FRAME : rows + (i + 1) * FRAME]
            d_out[piece, chunk] = (base + scale * delta).astype(BF16)

    for h in range(heads):
        for j in range(1, n_mp):
            ao_copy(h, j).wait_send()


def per_device(n, n_mp, q, dq, k, v, dk, dv, flags, w, gate, x, dx):
    rows, width = q.shape
    cols = x.shape[1]
    heads = width // HD
    half = n // 2
    move_w = cols % HD == 0
    if not move_w:
        w = lax.all_to_all(w, "mp", split_axis=1, concat_axis=0, tiled=True)
        w = w.reshape(n_mp, width, cols)
    anywhere = pl.BlockSpec(memory_space=pl.ANY)
    vmem = pl.BlockSpec(memory_space=pltpu.VMEM)
    dma = pltpu.SemaphoreType.DMA
    return pl.pallas_call(
        functools.partial(fused, n, n_mp, move_w),
        out_shape=(pltpu.VMEM(x.shape, BF16), pltpu.VMEM(x.shape, BF16)),
        in_specs=[anywhere] * 6
        + [anywhere, anywhere if move_w else vmem, anywhere]
        + [anywhere] * 2,
        out_specs=(vmem, vmem),
        scratch_shapes=[
            pltpu.VMEM((6, rows, width), BF16),
            pltpu.VMEM((heads, rows, 2 * HD), BF16),
            pltpu.VMEM((heads, 2, rows, HD), BF16),
            pltpu.VMEM((heads, half - 1, 4, 2 * rows, HD), BF16),
            pltpu.VMEM((heads, 4, rows, HD), BF16),
            pltpu.VMEM((heads, rows, 1), F32),
            pltpu.VMEM((heads, rows, 1), F32),
            pltpu.VMEM((heads, rows, 1), F32),
            pltpu.VMEM((heads, rows, HD), F32),
            pltpu.VMEM((heads, rows, HD), F32),
            pltpu.VMEM((heads, n_mp, 2 * rows, HD), BF16),
            pltpu.VMEM((n_mp, width, cols) if move_w else (1, 16, HD), BF16),
            pltpu.VMEM((2 * rows, cols), F32),
            pltpu.VMEM((2, rows, cols), BF16),
            pltpu.SMEM((rows,), jnp.int32),
            pltpu.VMEM((cols,), F32),
            dma((6,)),
            dma((2,)),
            dma((2,)),
            dma((heads,)),
            dma((heads, 2, half, 4)),
            dma((heads, 2, half, 4)),
            dma((heads, n_mp)),
            dma((heads, n_mp)),
            dma((heads, n_mp)),
            dma((heads, n_mp)),
        ],
        compiler_params=pltpu.CompilerParams(
            collective_id=0, has_side_effects=True, vmem_limit_bytes=65000000
        ),
    )(q, dq, k, v, dk, dv, flags, w, gate, x, dx)


def gathered(
    n,
    n_mp,
    q_hbm,
    dq_hbm,
    k_hbm,
    v_hbm,
    dk_hbm,
    dv_hbm,
    flags_hbm,
    w_hbm,
    gate_hbm,
    x_hbm,
    dx_hbm,
    out,
    d_out,
    own,
    qpack,
    pack,
    qpeer,
    peer,
    qcat,
    kv,
    m_s,
    l_s,
    c_s,
    a_s,
    g_s,
    res,
    ao,
    wbuf,
    acc,
    xbuf,
    flags,
    gate,
    raw_sem,
    x_sem,
    small_sem,
    w_local,
    qr,
    zs,
    kr,
    kt,
    pr,
    fs,
    wts,
    wtr,
    wxs,
    wxr,
    wys,
    wyr,
    rs,
    rr,
    as_,
    ar,
):
    rows, width = q_hbm.shape
    heads = width // HD
    cols = out.shape[1]
    t = lax.axis_index("tm")
    m = lax.axis_index("mp")
    z, y = t // 2, t % 2
    plane, core = m // 2, m % 2
    side = z // 2
    role = jnp.where(side == 0, 1 - z % 2, z % 2)
    home = role == 0
    straight = y == core
    itself = jnp.logical_and(home, straight)

    def chip(side_, role_):
        return 2 * side_ + jnp.where(side_ == 0, 1 - role_, role_)

    order = (side, 1 - side)
    homes = [(2 * chip(h, 0) + core, 2 * plane + y) for h in order]
    sources = [
        (2 * chip((side + g // 2) % 2, g % 2) + core, 2 * plane + y) for g in range(4)
    ]
    twin = (t, 2 * plane + 1 - core)
    across = (t, 2 * (1 - plane) + core)
    diagonal = (t, 2 * (1 - plane) + 1 - core)
    row_peer = (2 * z + 1 - y, m)
    factor = 1.0 / math.sqrt(HD)
    power = factor * math.log2(math.e)

    def lanes(h):
        return slice(h * HD, (h + 1) * HD)

    def both(flag, yes, no):
        pl.when(flag)(yes)
        pl.when(jnp.logical_not(flag))(no)

    def unless(flag, no):
        pl.when(jnp.logical_not(flag))(no)

    barrier = pltpu.get_barrier_semaphore()

    def greet(dev):
        pl.semaphore_signal(barrier, inc=1, device_id=dev, device_id_type=MESH)

    greet(homes[1])
    unless(itself, lambda: greet(homes[0]))

    @pl.when(home)
    def _():
        for i in (3, 2, 1):
            greet(sources[i])
        unless(itself, lambda: greet(sources[0]))

    @pl.when(straight)
    def _():
        for h in order:
            greet((2 * chip(h, 0) + y, 2 * plane + 1 - y))

    @pl.when(jnp.logical_and(home, jnp.logical_not(straight)))
    def _():
        for g in range(4):
            greet((2 * chip((side + g // 2) % 2, g % 2) + y, 2 * plane + y))

    for dev in (across, diagonal, row_peer, twin):
        greet(dev)

    loads = [
        pltpu.make_async_copy(src, own.at[i], raw_sem)
        for i, src in enumerate((dq_hbm, dk_hbm, dv_hbm))
    ]
    flags_load = pltpu.make_async_copy(flags_hbm, flags, small_sem.at[0])
    raw = []

    def done(ref, sem):
        pltpu.make_async_copy(ref, ref, sem).wait()

    for j in range(heads):
        for i, (src, dst) in enumerate(
            (
                (q_hbm, qpack.at[j, :, HD : 2 * HD]),
                (k_hbm, pack.at[j, 0]),
                (v_hbm, pack.at[j, 2]),
            )
        ):
            raw.append(
                pltpu.make_async_copy(src.at[:, lanes(j)], dst, raw_sem)
            )
    flags_load.start()
    for load in loads + raw:
        load.start()
    flags_load.wait()
    done(kv.at[0:4, 0:3], raw_sem)

    live = [
        jnp.where(flags[i * FRAME] > 0, 1.0, 0.0).astype(F32)
        for i in range(rows // FRAME)
    ]

    def masked(value, i):
        scale = jnp.full(value.shape, live[i], F32)
        return (value.astype(F32) * scale).astype(BF16)

    for h in range(heads):
        for i in range(rows // FRAME):
            piece = slice(i * FRAME, (i + 1) * FRAME)
            qpack[h, piece, 0:HD] = masked(own[0, piece, lanes(h)], i)
            pack[h, 1, piece] = masked(own[1, piece, lanes(h)], i)
            pack[h, 3, piece] = masked(own[2, piece, lanes(h)], i)
    pl.semaphore_wait(
        barrier,
        4 + heads + 4 * home.astype(jnp.int32) - 2 * itself.astype(jnp.int32)
        + 2 * straight.astype(jnp.int32)
        + 4 * (home.astype(jnp.int32) - itself.astype(jnp.int32)),
    )

    def remote(ends, send_sem, dev):
        src, dst, sem = ends
        return pltpu.make_async_remote_copy(
            src_ref=src,
            dst_ref=dst,
            send_sem=send_sem,
            recv_sem=sem,
            device_id=dev,
            device_id_type=MESH,
        )

    def home_ends(o, piece, relayed=False):
        h = order[o]
        g = 2 * o + role
        if piece == 0:
            return (qpeer.at[o] if relayed else qpack.at[h]), qcat.at[g], qr.at[g]
        pair = slice(2 * piece - 2, 2 * piece)
        crossing = 1 if relayed else (y + core) % 2
        slot = g + 4 * crossing
        src = peer.at[o, pair] if relayed else pack.at[h, pair]
        return src, kv.at[pair, slot], kr.at[piece - 1, g]

    def home_copy(o, piece):
        return remote(home_ends(o, piece), zs, homes[o])

    def home_all(o):
        for piece in range(3):
            home_copy(o, piece).start()

    def home_local():
        for piece in range(3):
            pltpu.make_async_copy(*home_ends(0, piece)).start()

    def peer_copy(o, piece):
        h = order[o]
        if piece == 0:
            ends = (qpack.at[h], qpeer.at[o], pr.at[o, piece])
        else:
            pair = slice(2 * piece - 2, 2 * piece)
            ends = (pack.at[h, pair], peer.at[o, pair], pr.at[o, piece])
        return remote(ends, zs, row_peer)

    def peer_all(o):
        for piece in range(3):
            peer_copy(o, piece).start()

    def onward(o, piece):
        dev = (2 * chip(order[o], 0) + y, 2 * plane + 1 - y)
        return remote(home_ends(o, piece, True), zs, dev)

    def relay(o):
        for piece in range(3):
            peer_copy(o, piece).wait_recv()
            onward(o, piece).start()

    def straight_sends():
        both(itself, home_local, lambda: home_all(0))
        home_all(1)

    def crossing_sends():
        def middle():
            peer_all(1)
            home_all(0)

        def end():
            peer_all(0)
            peer_all(1)

        both(home, middle, end)

    both(straight, straight_sends, crossing_sends)

    tile = 16
    y_rows = (width // tile * 5 // 16) * tile
    rest = slice(2 * y_rows, width)
    halves = 2 if cols % (2 * HD) == 0 else 1
    span = cols // halves

    def y_part(index):
        return pl.ds(pl.multiple_of(index * y_rows, tile), y_rows)

    def w_cols(owner, first, size):
        return pl.ds(pl.multiple_of(owner * cols + first, HD), size)

    def w_cross(slot, piece):
        dev = across if slot == 0 else diagonal
        if piece < halves:
            rows_ = y_part(y)
            first, size = piece * span, span
        else:
            rows_ = rest
            first, size = (piece - halves) * span, span
        return remote(
            (
                w_hbm.at[rows_, w_cols(dev[1], first, size)],
                wbuf.at[2 + slot, rows_, pl.ds(first, size)],
                wxr.at[2 * piece + slot if piece < halves else 2 * halves],
            ),
            wxs,
            dev,
        )

    def w_row(slot, piece):
        ref = wbuf.at[2 + slot, y_part(y), pl.ds(piece * span, span)]
        return remote((ref, ref, wyr), wys, row_peer)

    def w_row_relay(piece):
        for slot in range(2):
            w_cross(slot, piece).wait_recv()
            w_row(slot, piece).start()

    w_twin = remote(
        (w_hbm.at[:, w_cols(twin[1], 0, cols)], wbuf.at[1], wtr), wts, twin
    )
    w_own = pltpu.make_async_copy(w_hbm.at[:, w_cols(m, 0, cols)], wbuf.at[0], w_local)

    for piece in range(2 * halves):
        for slot in range(2):
            w_cross(slot, piece).start()
    w_twin.start()
    w_own.start()
    x_loads = [
        pltpu.make_async_copy(src, xbuf.at[i], x_sem)
        for i, src in enumerate((x_hbm, dx_hbm))
    ]
    gate_load = pltpu.make_async_copy(gate_hbm, gate, small_sem.at[1])
    for load in x_loads:
        load.start()
    gate_load.start()

    mine_at = 4 * ((y + core) % 2)
    twins_at = 4 - mine_at

    def to_twin(pair, g):
        ref = kv.at[2 * pair : 2 * pair + 2, g + mine_at]
        return remote((ref, ref, kt.at[g]), fs, twin)

    def arrive(g):
        for pair in range(2):
            done(kv.at[2 * pair : 2 * pair + 2, g + mine_at], kr.at[pair, g])
            to_twin(pair, g).start()

    def from_twin(g):
        done(kv.at[:, g + twins_at], kt.at[g])

    def q_wait(i):
        pltpu.make_async_copy(qcat.at[i], qcat.at[i], qr.at[i]).wait()

    def attend(blocks, queries):
        first = blocks[0] == 0
        last = blocks[1] == 8
        keys = (blocks[1] - blocks[0]) * rows
        count = (queries[1] - queries[0]) * rows
        at = slice(queries[0] * rows, queries[1] * rows)

        def spread(column):
            return jnp.broadcast_to(column, (count, HD))

        k, tk, v, tv = (
            kv[p, blocks[0] : blocks[1]].reshape(keys, HD) for p in range(4)
        )
        q = qcat[queries[0] : queries[1]].reshape(count, 2 * HD)
        scores = dot_nt(q[:, HD : 2 * HD], k)
        d_scores = dot_nt(q, jnp.concatenate([k, tk], axis=1))
        peak = spread(jnp.max(scores, axis=1, keepdims=True))
        if not first:
            peak_old = m_s[at]
            peak = jnp.maximum(peak_old, peak)
            rescale = jnp.exp2((peak_old - peak) * power)
        weights = jnp.exp2((scores - jnp.tile(peak, (1, keys // HD))) * power)
        product = weights * d_scores
        total = spread(jnp.sum(weights, axis=1, keepdims=True))
        slope = spread(jnp.sum(product, axis=1, keepdims=True))
        weights_b = weights.astype(BF16)
        product_b = product.astype(BF16)
        wide = dot_nn(weights_b, jnp.concatenate([v, tv], axis=1))
        primal = wide[:, 0:HD]
        tangent = dot_nn(product_b, v) * factor + wide[:, HD : 2 * HD]
        if not first:
            total = l_s[at] * rescale + total
            slope = c_s[at] * rescale + slope
            primal = a_s[at] * rescale + primal
            tangent = g_s[at] * rescale + tangent
        if last:
            inverse = 1.0 / total
            outputs = primal * inverse
            d_outputs = tangent * inverse - (slope * (factor * inverse)) * outputs
            for i in range(*queries):
                own_rows = slice((i - queries[0]) * rows, (i - queries[0] + 1) * rows)
                res[i, 0] = outputs[own_rows].astype(BF16)
                res[i, 1] = d_outputs[own_rows].astype(BF16)
        else:
            m_s[at] = peak
            l_s[at] = total
            c_s[at] = slope
            a_s[at] = primal
            g_s[at] = tangent

    cuts = 3 if rows % 48 == 0 else 2
    parts = 2 * cuts

    def part_of(p):
        size = rows // cuts
        return p // cuts, slice(p % cuts * size, (p % cuts + 1) * size)

    def res_ends(i, p):
        return (
            res.at[i, *part_of(p)],
            ao.at[side, 0, *part_of(p)],
            rr.at[side, p],
        )

    def res_remote(i, p):
        return remote(res_ends(i, p), rs, sources[i])

    def res_start(i, p):
        def local():
            pltpu.make_async_copy(*res_ends(i, p)).start()

        def away():
            res_remote(i, p).start()

        if i == 0:
            both(itself, local, away)
        else:
            away()

    @pl.when(home)
    def _():
        def nothing(g):
            pass

        def each(groups, on_straight, on_crossing):
            for g in groups:
                both(straight, lambda: on_straight(g), lambda: on_crossing(g))

        pl.when(straight)(lambda: relay(1))
        unless(straight, lambda: arrive(0))
        each((0, 1), arrive, from_twin)
        w_row_relay(0)
        each((2, 3), arrive, from_twin)
        q_wait(0)
        q_wait(1)
        attend((0, 4), (0, 2))
        each((0,), from_twin, nothing)
        each((1,), from_twin, arrive)
        attend((4, 6), (0, 2))
        for piece in range(1, halves):
            w_row_relay(piece)
        q_wait(2)
        q_wait(3)
        attend((0, 6), (2, 4))
        each((2, 3), from_twin, arrive)
        for queries in ((2, 4), (0, 2)):
            attend((6, 8), queries)
            for p in range(parts):
                for i in range(queries[1] - 1, queries[0] - 1, -1):
                    res_start(i, p)

    @pl.when(jnp.logical_not(home))
    def _():
        @pl.when(straight)
        def _():
            relay(0)
            relay(1)

        for piece in range(halves):
            w_row_relay(piece)

    def ao_copy(h, j, p):
        src = ao.at[h, 2 if j == 3 else 0, *part_of(p)]
        dst = ao.at[h, j, *part_of(p)]
        dev = across if j == 2 else twin
        at = 4 + parts * h + p if j == 2 else j - 1 + p // cuts
        return remote((src, dst, ar.at[at]), as_, dev)

    def own_heads(h, p):
        done(ao.at[h, 0, *part_of(p)], rr.at[h, p])
        ao_copy(h, 2, p).start()
        ao_copy(h, 1, p).start()

    def cross_heads(h, p):
        ao_copy(h, 2, p).wait_recv()
        ao_copy(h, 3, p).start()

    step = 2 * HD if cols % (2 * HD) == 0 else cols
    chunks = [slice(c, c + step) for c in range(0, cols, step)]

    def project(slots, a, chunk):
        attn = jnp.concatenate([ao[heads_[h], j, a] for h, j in slots], axis=1)
        weight = jnp.concatenate([wbuf[j, w_rows[h], chunk] for h, j in slots], axis=0)
        return dot_nn(attn, weight)

    heads_ = (side, 1 - side)
    w_rows = [pl.ds(pl.multiple_of(h * HD, HD), HD) for h in heads_]
    def in_turn(take, lo, hi):
        def middle():
            for at in range(lo, hi):
                take((side, 1 - side)[at // parts], at % parts)

        def end():
            for at in range(lo, hi):
                take((1 - side, side)[at % 2], at // 2)

        both(home, middle, end)


    def own_plane(a):
        done(ao.at[:, 1, a], ar.at[a])
        for chunk in chunks:
            acc[a, :, chunk] = project([(0, 0), (0, 1), (1, 0), (1, 1)], a, chunk)

    def other_plane(a, result):
        done(ao.at[:, 3, a], ar.at[2 + a])
        slots = [(0, 2), (0, 3), (1, 2), (1, 3)]
        for chunk in chunks:
            total = acc[a, :, chunk] + project(slots, a, chunk)
            scale = gate[chunk].reshape(1, step)
            base = xbuf[a, :, chunk].astype(F32)
            result[:, chunk] = (base + scale * total).astype(BF16)

    w_own.wait()
    w_twin.wait_recv()
    done(xbuf, x_sem)
    gate_load.wait()
    for i in range(rows // FRAME):
        piece = slice(i * FRAME, (i + 1) * FRAME)
        xbuf[1, piece] = masked(xbuf[1, piece], i)
    in_turn(own_heads, 0, 2 * parts)
    own_plane(0)
    done(wbuf.at[2:4, rest], wxr.at[2 * halves])
    done(wbuf.at[2:4, y_part(1 - y)], wyr)
    both(
        jnp.logical_and(straight, jnp.logical_not(home)),
        lambda: done(kv.at[0:4, 0:6], zs),
        lambda: done(kv.at[0:2, 0:6], zs),
    )
    done(wbuf.at[0:2, 0 : width - y_rows], wxs)
    done(wbuf.at[2:4, y_part(y)], wys)
    w_twin.wait_send()

    @pl.when(home)
    def _():
        done(kv.at[0:2, 0:8], fs)

    in_turn(cross_heads, 0, parts)
    own_plane(1)
    in_turn(cross_heads, parts, 2 * parts)
    @pl.when(home)
    def _():
        both(itself, lambda: done(res.at[0:3], rs), lambda: done(res, rs))

    other_plane(0, out)
    other_plane(1, d_out)

    done(ao.at[:, 1:n_mp], as_)


def store(a_ref, b_ref, a_hbm, b_hbm, sems):
    quarter = a_ref.shape[0] // 4
    copies = []
    for i in range(4):
        part = slice(i * quarter, (i + 1) * quarter)
        copies.append(pltpu.make_async_copy(a_ref.at[part], a_hbm.at[part], sems.at[0]))
        copies.append(pltpu.make_async_copy(b_ref.at[part], b_hbm.at[part], sems.at[1]))
    for copy in copies:
        copy.start()
    pltpu.make_async_copy(a_ref, a_hbm, sems.at[0]).wait()
    pltpu.make_async_copy(b_ref, b_hbm, sems.at[1]).wait()


def gathered_call(n, n_mp, q, dq, k, v, dk, dv, flags, w, gate, x, dx):
    rows, width = q.shape
    cols = x.shape[1]
    heads = width // HD
    halves = 2 if cols % (2 * HD) == 0 else 1
    cuts = 3 if rows % 48 == 0 else 2
    anywhere = pl.BlockSpec(memory_space=pl.ANY)
    vmem = pl.BlockSpec(memory_space=pltpu.VMEM)
    dma = pltpu.SemaphoreType.DMA
    results = pl.pallas_call(
        functools.partial(gathered, n, n_mp),
        out_shape=(pltpu.VMEM(x.shape, BF16), pltpu.VMEM(x.shape, BF16)),
        in_specs=[anywhere] * 11,
        out_specs=(vmem, vmem),
        scratch_shapes=[
            pltpu.VMEM((3, rows, width), BF16),
            pltpu.VMEM((heads, rows, 2 * HD), BF16),
            pltpu.VMEM((heads, 4, rows, HD), BF16),
            pltpu.VMEM((heads, rows, 2 * HD), BF16),
            pltpu.VMEM((heads, 4, rows, HD), BF16),
            pltpu.VMEM((4, rows, 2 * HD), BF16),
            pltpu.VMEM((4, 8, rows, HD), BF16),
            pltpu.VMEM((4 * rows, HD), F32),
            pltpu.VMEM((4 * rows, HD), F32),
            pltpu.VMEM((4 * rows, HD), F32),
            pltpu.VMEM((4 * rows, HD), F32),
            pltpu.VMEM((4 * rows, HD), F32),
            pltpu.VMEM((4, 2, rows, HD), BF16),
            pltpu.VMEM((heads, n_mp, 2, rows, HD), BF16),
            pltpu.VMEM((n_mp, width, cols), BF16),
            pltpu.VMEM((2, rows, cols), F32),
            pltpu.VMEM((2, rows, cols), BF16),
            pltpu.SMEM((rows,), jnp.int32),
            pltpu.VMEM((cols,), F32),
            dma,
            dma,
            dma((2,)),
            dma,
            dma((4,)),
            dma,
            dma((2, 4)),
            dma((4,)),
            dma((heads, 3)),
            dma,
            dma,
            dma,
            dma,
            dma((2 * halves + 1,)),
            dma,
            dma,
            dma,
            dma((heads, 2 * cuts)),
            dma,
            dma((4 + 2 * cuts * heads,)),
        ],
        compiler_params=pltpu.CompilerParams(
            collective_id=0, has_side_effects=True, vmem_limit_bytes=65000000
        ),
    )(q, dq, k, v, dk, dv, flags, w, gate, x, dx)
    whole = jax.ShapeDtypeStruct(x.shape, BF16)
    return pl.pallas_call(
        store,
        out_shape=(whole, whole),
        in_specs=[vmem, vmem],
        out_specs=(anywhere, anywhere),
        scratch_shapes=[dma((2,))],
    )(*(pltpu.with_memory_space_constraint(r, pltpu.VMEM) for r in results))


def gathers(n, n_mp, q, x):
    heads = q.shape[1] // HD
    planes = cores = sides = roles = rows = 2
    return (
        n_mp == planes * cores
        and n == sides * roles * rows
        and heads == sides
        and x.shape[1] % HD == 0
        and q.shape[0] % FRAME == 0
    )


def program(n, n_mp, q, dq, k, v, dk, dv, flags, w, gate, x, dx):
    call = gathered_call if gathers(n, n_mp, q, x) else per_device
    return call(n, n_mp, q, dq, k, v, dk, dv, flags, w, gate, x, dx)


def solution(mesh):
    both = P("tm", "mp")
    placed = (both,) * 6 + (P("tm"), P("mp", None), P("mp"), both, both)
    return jax.shard_map(
        functools.partial(program, mesh.shape["tm"], mesh.shape["mp"]),
        mesh=mesh,
        in_specs=placed,
        out_specs=(both, both),
        check_vma=False,
    )
```
